32 devices in a mesh: row: 8 (over z, y), col: 4 (over x, core).
Axes of the slice: x: 2, y: 2, z: 4, core: 2. Of those that a mesh axis runs over, the one named last changes fastest.
Arguments:
- perturbations: bfloat16 [32, 32, 256, 128], P('row', 'col'), may hold values from -6 to 6
- weights: bfloat16 [32, 32, 64, 128], P('row', 'col'), may hold values from -6 to 6
- pattern: int32 [32, 32, 9], P('row', 'col'), may hold values from 0 to 1, as said below
- taper_index: int32 [32, 32, 9], P('row', 'col'), may hold values from 0 to 15, as said below
- tapers: bfloat16 [16, 128, 128], replicated, may hold values from 0 to 1
Outputs:
- increment: float32 [32, 32, 64, 128], P('row', 'col')
The draws below stay inside these ranges and needn't reach their ends.
Inputs may be any that keep to these rules, and one draw needn't show every extreme that they name: pattern[i, k] = pattern[i + o_k, 8 - k] and taper_index[i, k] = taper_index[i + o_k, 8 - k] wherever both blocks lie in the grid; pattern[i, 4] = 1; pattern is 0 for neighbours outside the grid. `taper_index`: the same symmetry as the pattern.
All inputs are finite; a program needn't handle non-finite values.
Results may differ from the reference program's by a relative error of at most 0.0029.
Values may be sent and summed in bfloat16 or wider, within the bound.
No kernel may reach another device: no remote copies, remote signals or barrier semaphores. Data moves between devices by JAX's collectives and lax.ppermute only.
A program may use at most 128 MiB of HBM per device.

```python
import jax
import jax.numpy as jnp
from jax import lax

MEMBERS = 256
CB = 128
KW = 64
NT = 16
BPR = 4
BPC = 8
GR = 32
GC = 32


def pattern_tables(key):
    base = jax.random.fold_in(key, 7)
    keys = jax.random.split(base, 5)
    tiles_r = GR // BPR
    tiles_c = GC // BPC
    active = jax.random.randint(keys[0], (tiles_r, tiles_c, 4), 0, 2)
    chosen = jax.random.randint(keys[1], (), 0, tiles_r * tiles_c)
    tile_id = jnp.arange(tiles_r * tiles_c).reshape(tiles_r, tiles_c)
    complete_square = tile_id == chosen
    active = jnp.where(complete_square[:, :, None], 1, active)
    active = jnp.repeat(jnp.repeat(active, BPR, 0), BPC, 1)
    complete_block = jnp.repeat(jnp.repeat(complete_square, BPR, 0), BPC, 1)
    chance = jax.random.randint(keys[2], (GR, GC, 4), 0, 4)
    live = jnp.where(complete_block[:, :, None], 1, (chance < 3).astype(jnp.int32))
    forward = active * live
    arow = jnp.arange(GR)[:, None]
    bcol = jnp.arange(GC)[None, :]
    offsets = [(0, 1), (1, -1), (1, 0), (1, 1)]
    inside = []
    for drow, dcol in offsets:
        ok = (arow + drow < GR) & (bcol + dcol >= 0) & (bcol + dcol < GC)
        inside.append(ok.astype(jnp.int32))
    forward = forward * jnp.stack(inside, -1)
    index_fwd = jax.random.randint(keys[3], (GR, GC, 4), 0, NT)
    index_self = jax.random.randint(keys[4], (GR, GC), 0, NT)
    live_cols = [None] * 9
    index_cols = [None] * 9
    for f in range(4):
        drow, dcol = offsets[f]
        k = (drow + 1) * 3 + (dcol + 1)
        live_cols[k] = forward[:, :, f]
        index_cols[k] = index_fwd[:, :, f]
        live_cols[8 - k] = jnp.roll(forward[:, :, f], (drow, dcol), axis=(0, 1))
        index_cols[8 - k] = jnp.roll(index_fwd[:, :, f], (drow, dcol), axis=(0, 1))
    live_cols[4] = jnp.ones((GR, GC), jnp.int32)
    index_cols[4] = index_self
    return (jnp.stack(live_cols, -1).astype(jnp.int32), jnp.stack(index_cols, -1).astype(jnp.int32))


def draw_pattern(key, part):
    return pattern_tables(key)[0]


def draw_taper_index(key, part):
    return pattern_tables(key)[1]


def steps_of(stream_key, shape, cuts, least, largest):
    def one(dim, shards_of):
        steps = jax.random.uniform(jax.random.fold_in(jax.random.fold_in(stream_key, 6), dim), (shards_of,), jnp.float32, least / len(cuts), largest / len(cuts))
        return jnp.repeat(jnp.exp(steps), shape[dim] // shards_of).reshape((-1,) + (1,) * (len(shape) - dim - 1))

    loudness = one(*cuts[0])
    for cut in cuts[1:]:
        loudness = loudness * one(*cut)
    return loudness


def gaussian(rng, extent, deviation, limit, cuts=(), held_as=jnp.bfloat16):
    values = deviation * jax.random.normal(rng, extent, jnp.float32)
    if cuts:
        values = values * steps_of(rng, extent, cuts, -0.22, 0.18)
    return jnp.clip(values, -limit, limit).astype(held_as)


def setup_inputs(seed: int = 0) -> dict:
    arg_keys = jax.random.split(jax.random.key(seed), 6)
    return {
        "perturbations": gaussian(arg_keys[0], (GR, GC, MEMBERS, CB), 1.0, 6.0, ((0, 8), (1, 4))),
        "weights": gaussian(arg_keys[1], (GR, GC, KW, CB), 1.0, 6.0, ((0, 8), (1, 4))),
        "pattern": draw_pattern(jax.random.fold_in(arg_keys[5], 71), 0),
        "taper_index": draw_taper_index(jax.random.fold_in(arg_keys[5], 71), 0),
        "tapers": jnp.clip(jax.random.uniform(arg_keys[4], (NT, CB, CB), jnp.float32, 0.0, 1.0), 0.0, 1.0).astype(jnp.bfloat16),
    }


def reference(perturbations, weights, pattern, taper_index, tapers):
    scale = 1.0 / (MEMBERS - 1)
    padded_u = jnp.pad(perturbations, ((1, 1), (1, 1), (0, 0), (0, 0)))
    padded_weight = jnp.pad(weights, ((1, 1), (1, 1), (0, 0), (0, 0)))
    table = tapers.astype(jnp.float32)

    def single_row(arow):
        own = lax.dynamic_index_in_dim(perturbations, arow, 0, keepdims=False).astype(jnp.float32)
        live_row = lax.dynamic_index_in_dim(pattern, arow, 0, keepdims=False)
        index_row = lax.dynamic_index_in_dim(taper_index, arow, 0, keepdims=False)
        running_sum = jnp.zeros((GC, KW, CB), jnp.float32)
        for k in range(9):
            drow = k // 3 - 1
            dcol = k % 3 - 1
            start = (arow + 1 + drow).astype(jnp.int32)
            near_u = lax.dynamic_index_in_dim(padded_u, start, 0, keepdims=False)[1 + dcol:1 + dcol + GC].astype(jnp.float32)
            nearby_weight = lax.dynamic_index_in_dim(padded_weight, start, 0, keepdims=False)[1 + dcol:1 + dcol + GC].astype(jnp.float32)
            gram = jnp.einsum('bmc,bmd->bcd', own, near_u)
            rho = table[index_row[:, k]]
            if k < 4:
                rho = jnp.swapaxes(rho, 1, 2)
            if k == 4:
                rho = 0.5 * (rho + jnp.swapaxes(rho, 1, 2))
            factor = live_row[:, k].astype(jnp.float32) * scale
            tapered_matrix = (rho * gram * factor[:, None, None]).astype(jnp.bfloat16)
            running_sum = running_sum + jnp.einsum('qvj,qxj->qxv', tapered_matrix.astype(jnp.float32), nearby_weight)
        return running_sum

    return lax.map(single_row, jnp.arange(GR, dtype=jnp.int32))
```

```python
import jax
import jax.numpy as jnp
from jax import lax
from jax.experimental import pallas as pl
from jax.experimental.pallas import tpu as pltpu
from jax.sharding import PartitionSpec as P

MEMBERS = 256
SCALE = 1.0 / (MEMBERS - 1)
TN = (((0,), (0,)), ((), ()))
NT = (((1,), (1,)), ((), ()))
NN = (((1,), (0,)), ((), ()))
VMEM = pl.BlockSpec(memory_space=pltpu.VMEM)
SMEM = pl.BlockSpec(memory_space=pltpu.SMEM)
ANY = pl.BlockSpec(memory_space=pl.ANY)


def dot(a, b, dims):
    return lax.dot_general(a, b, dims, preferred_element_type=jnp.float32)


def cat(parts, axis):
    return parts[0] if len(parts) == 1 else jnp.concatenate(parts, axis=axis)


def tapered(gram, rho, live):
    factor = live.astype(jnp.float32) * SCALE
    return (rho.astype(jnp.float32) * gram * factor).astype(jnp.bfloat16)


def inner_kernel(u, w, live, index, tapers, out, sym, held):
    rows, cols, _, cells = u.shape
    for n in range(tapers.shape[0]):
        t = tapers[n].astype(jnp.float32)
        sym[n] = 0.5 * (t + t.T)

    def ahead(a, b, last):
        near = [(4, a, b)]
        if b + 1 < cols:
            near.append((5, a, b + 1))
        if not last:
            for k in (6, 7, 8):
                if 0 <= b + k - 7 < cols:
                    near.append((k, a + 1, b + k - 7))
        return near

    def row(a, last):
        for b in range(cols):
            near = ahead(a, b, last)
            gram = dot(u[a, b], cat([u[p, q] for _, p, q in near], 1), TN)
            for n, (k, _, _) in enumerate(near):
                at = index[a, b, k]
                rho = sym[at] if k == 4 else tapers[at]
                held[b, :, (k - 4) * cells : (k - 3) * cells] = tapered(
                    gram[:, n * cells : (n + 1) * cells], rho, live[a, b, k]
                )
        for b in range(cols):
            near = ahead(a, b, last)
            total = dot(
                cat([w[p, q] for _, p, q in near], 1),
                cat([held[b, :, (k - 4) * cells : (k - 3) * cells] for k, _, _ in near], 1),
                NT,
            )
            if b > 0:
                total += dot(w[a, b - 1], held[b - 1, :, cells : 2 * cells], NN)
            out[a, b] += total
            if not last:
                back = [(k, b - (k - 7)) for k in (6, 7, 8) if 0 <= b - (k - 7) < cols]
                out[a + 1, b] = dot(
                    cat([w[a, q] for _, q in back], 1),
                    cat([held[q, :, (k - 4) * cells : (k - 3) * cells] for k, q in back], 0),
                    NN,
                )

    out[0] = jnp.zeros_like(out[0])

    @pl.loop(0, rows - 1)
    def _(a):
        row(a, False)

    row(rows - 1, True)


def inner(u, w, live, index, tapers):
    rows, cols, members, cells = u.shape
    columns = w.shape[2]
    pairs = 5 * rows * cols
    return pl.pallas_call(
        inner_kernel,
        out_shape=jax.ShapeDtypeStruct((rows, cols, columns, cells), jnp.float32),
        in_specs=[VMEM, VMEM, SMEM, SMEM, VMEM],
        out_specs=VMEM,
        scratch_shapes=[
            pltpu.VMEM(tapers.shape, jnp.float32),
            pltpu.VMEM((cols, cells, 5 * cells), jnp.bfloat16),
        ],
        compiler_params=pltpu.CompilerParams(vmem_limit_bytes=24 << 20),
        cost_estimate=pl.CostEstimate(
            flops=2 * pairs * cells * cells * (members + 2 * columns),
            bytes_accessed=4 << 20,
            transcendentals=0,
        ),
        name="inner",
    )(u, w, live, index, tapers)


def above_kernel(s, u, w, left, right, live, index, side, tapers, back, held):
    cols, _, cells = s.shape
    members = u.shape[2]
    deep = members + w.shape[2]

    for c in range(cols):
        grams, weights, lives, rhos = [], [], [], []
        for k in (6, 7, 8):
            q = c + k - 7
            if q < 0:
                near, lively, at = left, side[0], side[1]
            elif q >= cols:
                near, lively, at = right, side[2], side[3]
            else:
                near, lively, at = None, live[0, q, 8 - k], index[0, q, 8 - k]
            grams.append(u[0, q] if near is None else near[0, :members])
            weights.append(w[0, q] if near is None else near[0, members:deep])
            lives.append(lively)
            rhos.append(tapers[at])
        gram = dot(s[c, :members], cat(grams, 1), TN)
        block = cat(
            [tapered(gram[:, n * cells : (n + 1) * cells], rhos[n], lives[n]) for n in range(3)], 1
        )
        held[c] = block
        back[c] = dot(cat(weights, 1), block, NT).astype(jnp.bfloat16)


def above(s, u, w, left, right, live, index, side, tapers):
    cols, _, cells = s.shape
    columns = w.shape[2]
    members = u.shape[2]
    return pl.pallas_call(
        above_kernel,
        out_shape=(
            jax.ShapeDtypeStruct((cols, columns, cells), jnp.bfloat16),
            jax.ShapeDtypeStruct((cols, cells, 3 * cells), jnp.bfloat16),
        ),
        in_specs=[VMEM, VMEM, VMEM, VMEM, VMEM, SMEM, SMEM, SMEM, VMEM],
        out_specs=(VMEM, VMEM),
        compiler_params=pltpu.CompilerParams(vmem_limit_bytes=24 << 20),
        cost_estimate=pl.CostEstimate(
            flops=2 * 3 * cols * cells * cells * (members + columns),
            bytes_accessed=2 << 20,
            transcendentals=0,
        ),
        name="above",
    )(s, u, w, left, right, live, index, side, tapers)


def outer_kernel(inc, held, s, corner, u, w, left, right, live, index, tapers, out):
    rows, cols, members, cells = u.shape
    deep = members + w.shape[2]
    last = cols - 1
    total = {}

    def add(a, q, value):
        total[a, q] = total[a, q] + value if (a, q) in total else value

    for q in range(cols):
        back = [(k, q - (k - 7)) for k in (6, 7, 8) if 0 <= q - (k - 7) < cols]
        sources = [s[c, members:deep] for _, c in back]
        blocks = [held[c, :, (k - 6) * cells : (k - 5) * cells] for k, c in back]
        for edge, k, far in ((0, 8, 0), (last, 6, 1)):
            if q == edge:
                gram = dot(corner[far, :members], u[0, q], TN)
                sources.append(corner[far, members:deep])
                blocks.append(tapered(gram, tapers[index[0, q, 8 - k]], live[0, q, 8 - k]))
        add(0, q, dot(cat(sources, 1), cat(blocks, 0), NN))

    for a in range(rows):
        near = [(5, a)] + ([(8, a + 1)] if a + 1 < rows else [])
        gram = dot(left[a, :members], cat([u[p, 0] for _, p in near], 1), TN)
        blocks = cat(
            [
                tapered(gram[:, n * cells : (n + 1) * cells], tapers[index[p, 0, 8 - k]], live[p, 0, 8 - k])
                for n, (k, p) in enumerate(near)
            ],
            1,
        )
        both = dot(left[a, members:deep], blocks, NN)
        for n, (_, p) in enumerate(near):
            add(p, 0, both[:, n * cells : (n + 1) * cells])
        gram = dot(u[a, last], cat([right[p, :members] for _, p in near], 1), TN)
        blocks = cat(
            [
                tapered(gram[:, n * cells : (n + 1) * cells], tapers[index[a, last, k]], live[a, last, k])
                for n, (k, _) in enumerate(near)
            ],
            1,
        )
        add(a, last, dot(cat([right[p, members:deep] for _, p in near], 1), blocks, NT))
        if a + 1 < rows:
            gram = dot(u[a, 0], left[a + 1, :members], TN)
            block = tapered(gram, tapers[index[a, 0, 6]], live[a, 0, 6])
            add(a, 0, dot(left[a + 1, members:deep], block, NT))
            gram = dot(right[a, :members], u[a + 1, last], TN)
            block = tapered(gram, tapers[index[a + 1, last, 2]], live[a + 1, last, 2])
            add(a + 1, last, dot(right[a, members:deep], block, NN))

    for a in range(rows):
        for q in range(cols):
            out[a, q] = inc[a, q] + total[a, q] if (a, q) in total else inc[a, q]


def outer(inc, held, s, corner, u, w, left, right, live, index, tapers):
    rows, cols, members, cells = u.shape
    columns = w.shape[2]
    return pl.pallas_call(
        outer_kernel,
        out_shape=jax.ShapeDtypeStruct(inc.shape, inc.dtype),
        in_specs=[VMEM] * 8 + [SMEM, SMEM, VMEM],
        out_specs=VMEM,
        input_output_aliases={0: 0},
        compiler_params=pltpu.CompilerParams(vmem_limit_bytes=24 << 20),
        cost_estimate=pl.CostEstimate(
            flops=2 * (6 * rows + 3 * cols) * cells * cells * (members + columns),
            bytes_accessed=4 << 20,
            transcendentals=0,
        ),
        name="outer",
    )(inc, held, s, corner, u, w, left, right, live, index, tapers)


def forward(axis):
    return [(i, i + 1) for i in range(lax.axis_size(axis) - 1)]


def backward(axis):
    return [(i + 1, i) for i in range(lax.axis_size(axis) - 1)]


def pack_row_kernel(u, w, out, sem):
    rows, _, members, _ = u.shape
    deep = members + w.shape[2]
    copies = [
        pltpu.make_async_copy(u.at[rows - 1], out.at[:, :members], sem.at[0]),
        pltpu.make_async_copy(w.at[rows - 1], out.at[:, members:deep], sem.at[1]),
    ]
    for copy in copies:
        copy.start()
    for copy in copies:
        copy.wait()


def pack_row(u, w):
    _, cols, members, cells = u.shape
    shape = (cols, members + w.shape[2], cells)
    return pl.pallas_call(
        pack_row_kernel,
        out_shape=jax.ShapeDtypeStruct(shape, u.dtype),
        in_specs=[ANY, ANY],
        out_specs=ANY,
        scratch_shapes=[pltpu.SemaphoreType.DMA((2,))],
        cost_estimate=pl.CostEstimate(flops=0, bytes_accessed=4 * cols * shape[1] * cells, transcendentals=0),
        name="pack_row",
    )(u, w)


def pack_columns_kernel(u, w, live, index, row, first, final, notes, sem):
    del row
    rows, cols, members, cells = u.shape
    deep = members + w.shape[2]
    copies = []
    for n, (out, b) in enumerate(((first, 0), (final, cols - 1))):
        copies.append(pltpu.make_async_copy(u.at[:, b], out.at[:, :members], sem.at[n, 0]))
        copies.append(pltpu.make_async_copy(w.at[:, b], out.at[:, members:deep], sem.at[n, 1]))
    for copy in copies:
        copy.start()
    for n, (out, b) in enumerate(((first, 0), (final, cols - 1))):
        for a in range(rows):
            lines = jnp.concatenate([live[a], index[a]], 0).astype(jnp.float32)
            blank = jnp.zeros((2 * cols, cells - live.shape[2]), jnp.float32)
            notes[n, a] = jnp.concatenate([lines, blank], 1).astype(jnp.bfloat16)
        copies.append(pltpu.make_async_copy(notes.at[n], out.at[:, deep:], sem.at[n, 2]))
        copies[-1].start()
    for copy in copies:
        copy.wait()


def pack_columns(u, w, live, index, row):
    rows, cols, members, cells = u.shape
    shape = (rows, members + w.shape[2] + 2 * cols, cells)
    return pl.pallas_call(
        pack_columns_kernel,
        out_shape=(jax.ShapeDtypeStruct(shape, u.dtype),) * 2,
        in_specs=[ANY, ANY, VMEM, VMEM, ANY],
        out_specs=(ANY, ANY),
        scratch_shapes=[pltpu.VMEM((2, rows, 2 * cols, cells), jnp.bfloat16), pltpu.SemaphoreType.DMA((2, 3))],
        cost_estimate=pl.CostEstimate(flops=0, bytes_accessed=8 * rows * shape[1] * cells, transcendentals=0),
        name="pack_columns",
    )(u, w, live, index, row)


def body(perturbations, weights, live, index, tapers):
    u, w = perturbations, weights
    rows, cols, members, cells = u.shape
    deep = members + w.shape[2]
    row = pack_row(u, w)
    s = lax.ppermute(row, "row", forward("row"))
    first, final = pack_columns(u, w, live, index, row)
    left = lax.ppermute(final, "col", forward("col"))
    right = lax.ppermute(first, "col", backward("col"))
    corner = lax.ppermute(
        jnp.stack([left[rows - 1, :deep], right[rows - 1, :deep]]), "row", forward("row")
    )
    inc = inner(u, w, live, index, tapers)
    side = jnp.stack(
        [
            left[0, deep + cols - 1, 2],
            left[0, deep + 2 * cols - 1, 2],
            right[0, deep, 0],
            right[0, deep + cols, 0],
        ]
    ).astype(jnp.int32)
    inc, s = lax.optimization_barrier((inc, s))
    back, held = above(s, u, w, left, right, live, index, side, tapers)
    back = lax.ppermute(back, "row", backward("row"))
    inc = outer(inc, held, s, corner, u, w, left, right, live, index, tapers)
    return lax.dynamic_update_index_in_dim(inc, inc[rows - 1] + back.astype(jnp.float32), rows - 1, 0)


def solution(mesh):
    return jax.shard_map(
        body,
        mesh=mesh,
        in_specs=(
            P("row", "col", None, None),
            P("row", "col", None, None),
            P("row", "col", None),
            P("row", "col", None),
            P(),
        ),
        out_specs=P("row", "col", None, None),
        check_vma=False,
    )
```

```python
import jax
import jax.numpy as jnp
from jax import lax
from jax.experimental import pallas as pl
from jax.experimental.pallas import tpu as pltpu
from jax.sharding import PartitionSpec as P

MEMBERS = 256
GRANT = 16 << 20
SCALE = 1.0 / (MEMBERS - 1)
TN = (((0,), (0,)), ((), ()))
NT = (((1,), (1,)), ((), ()))
NN = (((1,), (0,)), ((), ()))
VMEM = pl.BlockSpec(memory_space=pltpu.VMEM)
SMEM = pl.BlockSpec(memory_space=pltpu.SMEM)
ANY = pl.BlockSpec(memory_space=pl.ANY)
HBM = pl.BlockSpec(memory_space=pltpu.HBM)


def dot(a, b, dims):
    return lax.dot_general(a, b, dims, preferred_element_type=jnp.float32)


def cat(parts, axis):
    return parts[0] if len(parts) == 1 else jnp.concatenate(parts, axis=axis)


def tapered(gram, rho, live):
    factor = live.astype(jnp.float32) * SCALE
    return (rho.astype(jnp.float32) * gram * factor).astype(jnp.bfloat16)


def inner_kernel(u, w, live, index, tapers, out, done, sym, held):
    rows, cols, _, cells = u.shape
    for n in range(tapers.shape[0]):
        t = tapers[n].astype(jnp.float32)
        sym[n] = 0.5 * (t + t.T)

    def ahead(a, b, last):
        near = [(4, a, b)]
        if b + 1 < cols:
            near.append((5, a, b + 1))
        if not last:
            for k in (6, 7, 8):
                if 0 <= b + k - 7 < cols:
                    near.append((k, a + 1, b + k - 7))
        return near

    def row(a, last):
        for b in range(cols):
            near = ahead(a, b, last)
            gram = dot(u[a, b], cat([u[p, q] for _, p, q in near], 1), TN)
            for n, (k, _, _) in enumerate(near):
                at = index[a, b, k]
                rho = sym[at] if k == 4 else tapers[at]
                held[b, :, (k - 4) * cells : (k - 3) * cells] = tapered(
                    gram[:, n * cells : (n + 1) * cells], rho, live[a, b, k]
                )
        for b in range(cols):
            near = ahead(a, b, last)
            total = dot(
                cat([w[p, q] for _, p, q in near], 1),
                cat([held[b, :, (k - 4) * cells : (k - 3) * cells] for k, _, _ in near], 1),
                NT,
            )
            if b > 0:
                total += dot(w[a, b - 1], held[b - 1, :, cells : 2 * cells], NN)
            out[a, b] += total
            if not last:
                back = [(k, b - (k - 7)) for k in (6, 7, 8) if 0 <= b - (k - 7) < cols]
                out[a + 1, b] = dot(
                    cat([w[a, q] for _, q in back], 1),
                    cat([held[q, :, (k - 4) * cells : (k - 3) * cells] for k, q in back], 0),
                    NN,
                )

    out[0] = jnp.zeros_like(out[0])

    @pl.loop(0, rows - 1)
    def _(a):
        row(a, False)

    row(rows - 1, True)
    done[...] = jnp.zeros_like(done)


def inner(u, w, live, index, tapers):
    rows, cols, members, cells = u.shape
    columns = w.shape[2]
    pairs = 5 * rows * cols
    return pl.pallas_call(
        inner_kernel,
        out_shape=(
            jax.ShapeDtypeStruct((rows, cols, columns, cells), jnp.float32),
            jax.ShapeDtypeStruct((8, cells), jnp.float32),
        ),
        in_specs=[VMEM, VMEM, SMEM, SMEM, VMEM],
        out_specs=(VMEM, VMEM),
        scratch_shapes=[
            pltpu.VMEM(tapers.shape, jnp.float32),
            pltpu.VMEM((cols, cells, 5 * cells), jnp.bfloat16),
        ],
        compiler_params=pltpu.CompilerParams(vmem_limit_bytes=GRANT),
        cost_estimate=pl.CostEstimate(
            flops=2 * pairs * cells * cells * (members + 2 * columns),
            bytes_accessed=4 << 20,
            transcendentals=0,
        ),
        name="inner",
    )(u, w, live, index, tapers)


def above_kernel(s, u, w, left, right, live, index, tapers, back, held):
    cols, _, cells = s.shape
    members = u.shape[2]
    deep = members + w.shape[2]
    notes = [near[0, deep:].astype(jnp.int32) for near in (left, right)]
    side = [notes[0][cols - 1, 2], notes[0][2 * cols - 1, 2], notes[1][0, 0], notes[1][cols, 0]]

    for c in range(cols):
        grams, weights, lives, rhos = [], [], [], []
        for k in (6, 7, 8):
            q = c + k - 7
            if q < 0:
                near, lively, at = left, side[0], side[1]
            elif q >= cols:
                near, lively, at = right, side[2], side[3]
            else:
                near, lively, at = None, live[0, q, 8 - k], index[0, q, 8 - k]
            grams.append(u[0, q] if near is None else near[0, :members])
            weights.append(w[0, q] if near is None else near[0, members:deep])
            lives.append(lively)
            rhos.append(tapers[at])
        gram = dot(s[c, :members], cat(grams, 1), TN)
        block = cat(
            [tapered(gram[:, n * cells : (n + 1) * cells], rhos[n], lives[n]) for n in range(3)], 1
        )
        held[c] = block
        back[c] = dot(cat(weights, 1), block, NT).astype(jnp.bfloat16)


def above(s, u, w, left, right, live, index, tapers):
    cols, _, cells = s.shape
    columns = w.shape[2]
    members = u.shape[2]
    return pl.pallas_call(
        above_kernel,
        out_shape=(
            jax.ShapeDtypeStruct((cols, columns, cells), jnp.bfloat16),
            jax.ShapeDtypeStruct((cols, cells, 3 * cells), jnp.bfloat16),
        ),
        in_specs=[VMEM, VMEM, VMEM, VMEM, VMEM, SMEM, SMEM, VMEM],
        out_specs=(VMEM, VMEM),
        compiler_params=pltpu.CompilerParams(vmem_limit_bytes=GRANT),
        cost_estimate=pl.CostEstimate(
            flops=2 * 3 * cols * cells * cells * (members + columns),
            bytes_accessed=2 << 20,
            transcendentals=0,
        ),
        name="above",
    )(s, u, w, left, right, live, index, tapers)


def outer_kernel(inc, held, s, corner, u, w, left, right, live, index, tapers, out, low):
    rows, cols, members, cells = u.shape
    deep = members + w.shape[2]
    last = cols - 1
    total = {}

    def add(a, q, value):
        total[a, q] = total[a, q] + value if (a, q) in total else value

    for q in range(cols):
        back = [(k, q - (k - 7)) for k in (6, 7, 8) if 0 <= q - (k - 7) < cols]
        sources = [s[c, members:deep] for _, c in back]
        blocks = [held[c, :, (k - 6) * cells : (k - 5) * cells] for k, c in back]
        for edge, k, far in ((0, 8, 0), (last, 6, 1)):
            if q == edge:
                gram = dot(corner[far, :members], u[0, q], TN)
                sources.append(corner[far, members:deep])
                blocks.append(tapered(gram, tapers[index[0, q, 8 - k]], live[0, q, 8 - k]))
        add(0, q, dot(cat(sources, 1), cat(blocks, 0), NN))

    for a in range(rows):
        near = [(5, a)] + ([(8, a + 1)] if a + 1 < rows else [])
        gram = dot(left[a, :members], cat([u[p, 0] for _, p in near], 1), TN)
        blocks = cat(
            [
                tapered(gram[:, n * cells : (n + 1) * cells], tapers[index[p, 0, 8 - k]], live[p, 0, 8 - k])
                for n, (k, p) in enumerate(near)
            ],
            1,
        )
        both = dot(left[a, members:deep], blocks, NN)
        for n, (_, p) in enumerate(near):
            add(p, 0, both[:, n * cells : (n + 1) * cells])
        gram = dot(u[a, last], cat([right[p, :members] for _, p in near], 1), TN)
        blocks = cat(
            [
                tapered(gram[:, n * cells : (n + 1) * cells], tapers[index[a, last, k]], live[a, last, k])
                for n, (k, _) in enumerate(near)
            ],
            1,
        )
        add(a, last, dot(cat([right[p, members:deep] for _, p in near], 1), blocks, NT))
        if a + 1 < rows:
            gram = dot(u[a, 0], left[a + 1, :members], TN)
            block = tapered(gram, tapers[index[a, 0, 6]], live[a, 0, 6])
            add(a, 0, dot(left[a + 1, members:deep], block, NT))
            gram = dot(right[a, :members], u[a + 1, last], TN)
            block = tapered(gram, tapers[index[a + 1, last, 2]], live[a + 1, last, 2])
            add(a + 1, last, dot(right[a, members:deep], block, NN))

    for a in range(rows):
        for q in range(cols):
            value = inc[a, q] + total[a, q] if (a, q) in total else inc[a, q]
            out[a, q] = value
            if a == rows - 1:
                low[q] = value


def outer(inc, held, s, corner, u, w, left, right, live, index, tapers):
    rows, cols, members, cells = u.shape
    columns = w.shape[2]
    return pl.pallas_call(
        outer_kernel,
        out_shape=(jax.ShapeDtypeStruct(inc.shape, inc.dtype), jax.ShapeDtypeStruct(inc.shape[1:], inc.dtype)),
        in_specs=[VMEM] * 8 + [SMEM, SMEM, VMEM],
        out_specs=(VMEM, VMEM),
        compiler_params=pltpu.CompilerParams(vmem_limit_bytes=GRANT),
        cost_estimate=pl.CostEstimate(
            flops=2 * (6 * rows + 3 * cols) * cells * cells * (members + columns),
            bytes_accessed=4 << 20,
            transcendentals=0,
        ),
        name="outer",
    )(inc, held, s, corner, u, w, left, right, live, index, tapers)


def finish_kernel(inc, low, back, out, total, sem):
    del inc
    total[...] = low[...] + back[...].astype(jnp.float32)
    copy = pltpu.make_async_copy(total, out.at[out.shape[0] - 1], sem)
    copy.start()
    copy.wait()


def finish(inc, low, back):
    return pl.pallas_call(
        finish_kernel,
        out_shape=jax.ShapeDtypeStruct(inc.shape, inc.dtype),
        in_specs=[ANY, VMEM, VMEM],
        out_specs=ANY,
        scratch_shapes=[pltpu.VMEM(low.shape, low.dtype), pltpu.SemaphoreType.DMA(())],
        input_output_aliases={0: 0},
        compiler_params=pltpu.CompilerParams(vmem_limit_bytes=GRANT),
        cost_estimate=pl.CostEstimate(flops=low.size, bytes_accessed=10 * low.size, transcendentals=0),
        name="finish",
    )(inc, low, back)


def forward(axis):
    return [(i, i + 1) for i in range(lax.axis_size(axis) - 1)]


def backward(axis):
    return [(i + 1, i) for i in range(lax.axis_size(axis) - 1)]


def pack_row_kernel(u, w, out, sem):
    rows, _, members, _ = u.shape
    deep = members + w.shape[2]
    copies = [
        pltpu.make_async_copy(u.at[rows - 1], out.at[:, :members], sem.at[0]),
        pltpu.make_async_copy(w.at[rows - 1], out.at[:, members:deep], sem.at[1]),
    ]
    for copy in copies:
        copy.start()
    for copy in copies:
        copy.wait()


def pack_row(u, w):
    _, cols, members, cells = u.shape
    shape = (cols, members + w.shape[2], cells)
    return pl.pallas_call(
        pack_row_kernel,
        out_shape=jax.ShapeDtypeStruct(shape, u.dtype),
        in_specs=[HBM, HBM],
        out_specs=VMEM,
        scratch_shapes=[pltpu.SemaphoreType.DMA((2,))],
        compiler_params=pltpu.CompilerParams(vmem_limit_bytes=GRANT),
        cost_estimate=pl.CostEstimate(flops=0, bytes_accessed=4 * cols * shape[1] * cells, transcendentals=0),
        name="pack_row",
    )(u, w)


def pack_columns_kernel(u, w, live, index, done, first, final, sem):
    del done
    rows, cols, members, cells = u.shape
    deep = members + w.shape[2]
    copies = []
    for n, (out, b) in enumerate(((first, 0), (final, cols - 1))):
        copies.append(pltpu.make_async_copy(u.at[:, b], out.at[:, :members], sem.at[n, 0]))
        copies.append(pltpu.make_async_copy(w.at[:, b], out.at[:, members:deep], sem.at[n, 1]))
    for copy in copies:
        copy.start()
    for a in range(rows):
        lines = jnp.concatenate([live[a], index[a]], 0).astype(jnp.float32)
        blank = jnp.zeros((2 * cols, cells - live.shape[2]), jnp.float32)
        note = jnp.concatenate([lines, blank], 1).astype(jnp.bfloat16)
        first[a, deep:] = note
        final[a, deep:] = note
    for copy in copies:
        copy.wait()


def pack_columns(u, w, live, index, done):
    rows, cols, members, cells = u.shape
    shape = (rows, members + w.shape[2] + 2 * cols, cells)
    return pl.pallas_call(
        pack_columns_kernel,
        out_shape=(jax.ShapeDtypeStruct(shape, u.dtype),) * 2,
        in_specs=[ANY, ANY, VMEM, VMEM, VMEM],
        out_specs=(VMEM, VMEM),
        scratch_shapes=[pltpu.SemaphoreType.DMA((2, 2))],
        compiler_params=pltpu.CompilerParams(vmem_limit_bytes=GRANT),
        cost_estimate=pl.CostEstimate(flops=0, bytes_accessed=8 * rows * shape[1] * cells, transcendentals=0),
        name="pack_columns",
    )(u, w, live, index, done)


def body(perturbations, weights, live, index, tapers):
    u, w = perturbations, weights
    rows, cols, members, cells = u.shape
    deep = members + w.shape[2]
    s = lax.ppermute(pack_row(u, w), "row", forward("row"))
    inc, done = inner(u, w, live, index, tapers)
    first, final = pack_columns(u, w, live, index, done)
    left = lax.ppermute(final, "col", forward("col"))
    right = lax.ppermute(first, "col", backward("col"))
    corner = lax.ppermute(
        jnp.stack([left[rows - 1, :deep], right[rows - 1, :deep]]), "row", forward("row")
    )
    back, held = above(s, u, w, left, right, live, index, tapers)
    back = lax.ppermute(back, "row", backward("row"))
    inc, low = outer(inc, held, s, corner, u, w, left, right, live, index, tapers)
    return finish(inc, low, back)


def solution(mesh):
    return jax.shard_map(
        body,
        mesh=mesh,
        in_specs=(
            P("row", "col", None, None),
            P("row", "col", None, None),
            P("row", "col", None),
            P("row", "col", None),
            P(),
        ),
        out_specs=P("row", "col", None, None),
        check_vma=False,
    )
```

```python
import jax
import jax.numpy as jnp
from jax import lax
from jax.experimental import pallas as pl
from jax.experimental.pallas import tpu as pltpu
from jax.sharding import PartitionSpec as P

MEMBERS = 256
GRANT = 16 << 20
SCALE = 1.0 / (MEMBERS - 1)
TN = (((0,), (0,)), ((), ()))
NT = (((1,), (1,)), ((), ()))
NN = (((1,), (0,)), ((), ()))
VMEM = pl.BlockSpec(memory_space=pltpu.VMEM)
ANY = pl.BlockSpec(memory_space=pl.ANY)
HBM = pl.BlockSpec(memory_space=pltpu.HBM)


def dot(a, b, dims):
    return lax.dot_general(a, b, dims, preferred_element_type=jnp.float32)


def cat(parts, axis):
    return parts[0] if len(parts) == 1 else jnp.concatenate(parts, axis=axis)


def tapered(gram, rho, live):
    factor = live.astype(jnp.float32) * SCALE
    return (rho.astype(jnp.float32) * gram * factor).astype(jnp.bfloat16)


def prepare_kernel(tapers, sym):
    for n in range(tapers.shape[0]):
        t = tapers[n].astype(jnp.float32)
        sym[n] = 0.5 * (t + t.T)


def prepare(tapers):
    return pl.pallas_call(
        prepare_kernel,
        out_shape=jax.ShapeDtypeStruct(tapers.shape, jnp.float32),
        in_specs=[VMEM],
        out_specs=VMEM,
        compiler_params=pltpu.CompilerParams(vmem_limit_bytes=GRANT),
        cost_estimate=pl.CostEstimate(flops=0, bytes_accessed=16 << 20, transcendentals=0),
        name="prepare",
    )(tapers)


def inner_kernel(u, w, live, index, tapers, sym, out, held):
    rows, cols, _, cells = u.shape
    def ahead(a, b, last):
        near = [(4, a, b)]
        if b + 1 < cols:
            near.append((5, a, b + 1))
        if not last:
            for k in (6, 7, 8):
                if 0 <= b + k - 7 < cols:
                    near.append((k, a + 1, b + k - 7))
        return near

    def row(a, last):
        on, which = live[a], index[a]
        for b in range(cols):
            near = ahead(a, b, last)
            gram = dot(u[a, b], cat([u[p, q] for _, p, q in near], 1), TN)
            for n, (k, _, _) in enumerate(near):
                at = which[b, k]
                rho = sym[at] if k == 4 else tapers[at]
                held[b, :, (k - 4) * cells : (k - 3) * cells] = tapered(
                    gram[:, n * cells : (n + 1) * cells], rho, on[b, k]
                )
        for b in range(cols):
            near = ahead(a, b, last)
            total = dot(
                cat([w[p, q] for _, p, q in near], 1),
                cat([held[b, :, (k - 4) * cells : (k - 3) * cells] for k, _, _ in near], 1),
                NT,
            )
            if b > 0:
                total += dot(w[a, b - 1], held[b - 1, :, cells : 2 * cells], NN)
            out[a, b] += total
            if not last:
                back = [(k, b - (k - 7)) for k in (6, 7, 8) if 0 <= b - (k - 7) < cols]
                out[a + 1, b] = dot(
                    cat([w[a, q] for _, q in back], 1),
                    cat([held[q, :, (k - 4) * cells : (k - 3) * cells] for k, q in back], 0),
                    NN,
                )

    out[0] = jnp.zeros_like(out[0])

    @pl.loop(0, rows - 1)
    def _(a):
        row(a, False)

    row(rows - 1, True)


def inner(u, w, live, index, tapers, sym):
    rows, cols, members, cells = u.shape
    columns = w.shape[2]
    pairs = 5 * rows * cols
    return pl.pallas_call(
        inner_kernel,
        out_shape=jax.ShapeDtypeStruct((rows, cols, columns, cells), jnp.float32),
        in_specs=[VMEM] * 6,
        out_specs=VMEM,
        scratch_shapes=[pltpu.VMEM((cols, cells, 5 * cells), jnp.bfloat16)],
        compiler_params=pltpu.CompilerParams(vmem_limit_bytes=GRANT),
        cost_estimate=pl.CostEstimate(
            flops=2 * pairs * cells * cells * (members + 2 * columns),
            bytes_accessed=4 << 20,
            transcendentals=0,
        ),
        name="inner",
    )(u, w, live, index, tapers, sym)


def above_kernel(s, u, w, left, right, live, index, tapers, back, held):
    cols, _, cells = s.shape
    members = u.shape[2]
    deep = members + w.shape[2]
    on, which = live[0], index[0]
    notes = [near[0, deep:].astype(jnp.int32) for near in (left, right)]
    side = [notes[0][cols - 1, 2], notes[0][2 * cols - 1, 2], notes[1][0, 0], notes[1][cols, 0]]

    sources = []
    for c in range(cols):
        grams, weights, lives, rhos = [], [], [], []
        for k in (6, 7, 8):
            q = c + k - 7
            if q < 0:
                near, lively, at = left, side[0], side[1]
            elif q >= cols:
                near, lively, at = right, side[2], side[3]
            else:
                near, lively, at = None, on[q, 8 - k], which[q, 8 - k]
            grams.append(u[0, q] if near is None else near[0, :members])
            weights.append(w[0, q] if near is None else near[0, members:deep])
            lives.append(lively)
            rhos.append(tapers[at])
        gram = dot(s[c, :members], cat(grams, 1), TN)
        block = cat(
            [tapered(gram[:, n * cells : (n + 1) * cells], rhos[n], lives[n]) for n in range(3)], 1
        )
        held[c] = block
        sources.append(cat(weights, 1))
    for c in range(cols):
        back[c] = dot(sources[c], held[c], NT).astype(jnp.bfloat16)


def above(s, u, w, left, right, live, index, tapers):
    cols, _, cells = s.shape
    columns = w.shape[2]
    members = u.shape[2]
    return pl.pallas_call(
        above_kernel,
        out_shape=(
            jax.ShapeDtypeStruct((cols, columns, cells), jnp.bfloat16),
            jax.ShapeDtypeStruct((cols, cells, 3 * cells), jnp.bfloat16),
        ),
        in_specs=[VMEM] * 8,
        out_specs=(VMEM, VMEM),
        compiler_params=pltpu.CompilerParams(vmem_limit_bytes=GRANT),
        cost_estimate=pl.CostEstimate(
            flops=2 * 3 * cols * cells * cells * (members + columns),
            bytes_accessed=2 << 20,
            transcendentals=0,
        ),
        name="above",
    )(s, u, w, left, right, live, index, tapers)


def outer_kernel(inc, held, s, corner, u, w, left, right, live, index, tapers, out, low):
    rows, cols, members, cells = u.shape
    deep = members + w.shape[2]
    last = cols - 1
    on = [live[a] for a in range(rows)]
    which = [index[a] for a in range(rows)]
    total = {}

    def add(a, q, value):
        total[a, q] = total[a, q] + value if (a, q) in total else value

    for q in range(cols):
        back = [(k, q - (k - 7)) for k in (6, 7, 8) if 0 <= q - (k - 7) < cols]
        sources = [s[c, members:deep] for _, c in back]
        blocks = [held[c, :, (k - 6) * cells : (k - 5) * cells] for k, c in back]
        for edge, k, far in ((0, 8, 0), (last, 6, 1)):
            if q == edge:
                gram = dot(corner[far, :members], u[0, q], TN)
                sources.append(corner[far, members:deep])
                blocks.append(tapered(gram, tapers[which[0][q, 8 - k]], on[0][q, 8 - k]))
        add(0, q, dot(cat(sources, 1), cat(blocks, 0), NN))

    for a in range(rows):
        near = [(5, a)] + ([(8, a + 1)] if a + 1 < rows else [])
        gram = dot(left[a, :members], cat([u[p, 0] for _, p in near], 1), TN)
        blocks = cat(
            [
                tapered(gram[:, n * cells : (n + 1) * cells], tapers[which[p][0, 8 - k]], on[p][0, 8 - k])
                for n, (k, p) in enumerate(near)
            ],
            1,
        )
        both = dot(left[a, members:deep], blocks, NN)
        for n, (_, p) in enumerate(near):
            add(p, 0, both[:, n * cells : (n + 1) * cells])
        gram = dot(u[a, last], cat([right[p, :members] for _, p in near], 1), TN)
        blocks = cat(
            [
                tapered(gram[:, n * cells : (n + 1) * cells], tapers[which[a][last, k]], on[a][last, k])
                for n, (k, _) in enumerate(near)
            ],
            1,
        )
        add(a, last, dot(cat([right[p, members:deep] for _, p in near], 1), blocks, NT))
        if a + 1 < rows:
            gram = dot(u[a, 0], left[a + 1, :members], TN)
            block = tapered(gram, tapers[which[a][0, 6]], on[a][0, 6])
            add(a, 0, dot(left[a + 1, members:deep], block, NT))
            gram = dot(right[a, :members], u[a + 1, last], TN)
            block = tapered(gram, tapers[which[a + 1][last, 2]], on[a + 1][last, 2])
            add(a + 1, last, dot(right[a, members:deep], block, NN))

    for a in range(rows):
        for q in range(cols):
            value = inc[a, q] + total[a, q] if (a, q) in total else inc[a, q]
            out[a, q] = value
            if a == rows - 1:
                low[q] = value


def outer(inc, held, s, corner, u, w, left, right, live, index, tapers):
    rows, cols, members, cells = u.shape
    columns = w.shape[2]
    return pl.pallas_call(
        outer_kernel,
        out_shape=(jax.ShapeDtypeStruct(inc.shape, inc.dtype), jax.ShapeDtypeStruct(inc.shape[1:], inc.dtype)),
        in_specs=[VMEM] * 11,
        out_specs=(VMEM, VMEM),
        compiler_params=pltpu.CompilerParams(vmem_limit_bytes=GRANT),
        cost_estimate=pl.CostEstimate(
            flops=2 * (6 * rows + 3 * cols) * cells * cells * (members + columns),
            bytes_accessed=4 << 20,
            transcendentals=0,
        ),
        name="outer",
    )(inc, held, s, corner, u, w, left, right, live, index, tapers)


def finish_kernel(inc, low, back, out, total, sem):
    del inc
    total[...] = low[...] + back[...].astype(jnp.float32)
    copy = pltpu.make_async_copy(total, out.at[out.shape[0] - 1], sem)
    copy.start()
    copy.wait()


def finish(inc, low, back):
    return pl.pallas_call(
        finish_kernel,
        out_shape=jax.ShapeDtypeStruct(inc.shape, inc.dtype),
        in_specs=[ANY, VMEM, VMEM],
        out_specs=ANY,
        scratch_shapes=[pltpu.VMEM(low.shape, low.dtype), pltpu.SemaphoreType.DMA(())],
        input_output_aliases={0: 0},
        compiler_params=pltpu.CompilerParams(vmem_limit_bytes=GRANT),
        cost_estimate=pl.CostEstimate(flops=low.size, bytes_accessed=10 * low.size, transcendentals=0),
        name="finish",
    )(inc, low, back)


def forward(axis):
    return [(i, i + 1) for i in range(lax.axis_size(axis) - 1)]


def backward(axis):
    return [(i + 1, i) for i in range(lax.axis_size(axis) - 1)]


def pack_row_kernel(u, w, out, sem):
    rows, _, members, _ = u.shape
    deep = members + w.shape[2]
    copies = [
        pltpu.make_async_copy(u.at[rows - 1], out.at[:, :members], sem.at[0]),
        pltpu.make_async_copy(w.at[rows - 1], out.at[:, members:deep], sem.at[1]),
    ]
    for copy in copies:
        copy.start()
    for copy in copies:
        copy.wait()


def pack_row(u, w):
    _, cols, members, cells = u.shape
    shape = (cols, members + w.shape[2], cells)
    return pl.pallas_call(
        pack_row_kernel,
        out_shape=jax.ShapeDtypeStruct(shape, u.dtype),
        in_specs=[HBM, HBM],
        out_specs=VMEM,
        scratch_shapes=[pltpu.SemaphoreType.DMA((2,))],
        cost_estimate=pl.CostEstimate(flops=0, bytes_accessed=4 * cols * shape[1] * cells, transcendentals=0),
        name="pack_row",
    )(u, w)


def pack_columns_kernel(u, w, live, index, sym, first, final, sem):
    del sym
    rows, cols, members, cells = u.shape
    deep = members + w.shape[2]
    copies = []
    for n, (out, b) in enumerate(((first, 0), (final, cols - 1))):
        copies.append(pltpu.make_async_copy(u.at[:, b], out.at[:, :members], sem.at[n, 0]))
        copies.append(pltpu.make_async_copy(w.at[:, b], out.at[:, members:deep], sem.at[n, 1]))
    for copy in copies:
        copy.start()
    for a in range(rows):
        lines = jnp.concatenate([live[a], index[a]], 0).astype(jnp.float32)
        blank = jnp.zeros((2 * cols, cells - live.shape[2]), jnp.float32)
        note = jnp.concatenate([lines, blank], 1).astype(jnp.bfloat16)
        first[a, deep:] = note
        final[a, deep:] = note
    for copy in copies:
        copy.wait()


def pack_columns(u, w, live, index, sym):
    rows, cols, members, cells = u.shape
    shape = (rows, members + w.shape[2] + 2 * cols, cells)
    return pl.pallas_call(
        pack_columns_kernel,
        out_shape=(jax.ShapeDtypeStruct(shape, u.dtype),) * 2,
        in_specs=[ANY, ANY, VMEM, VMEM, VMEM],
        out_specs=(VMEM, VMEM),
        scratch_shapes=[pltpu.SemaphoreType.DMA((2, 2))],
        compiler_params=pltpu.CompilerParams(vmem_limit_bytes=GRANT),
        cost_estimate=pl.CostEstimate(flops=0, bytes_accessed=8 * rows * shape[1] * cells, transcendentals=0),
        name="pack_columns",
    )(u, w, live, index, sym)


def body(perturbations, weights, live, index, tapers):
    u, w = perturbations, weights
    rows, cols, members, cells = u.shape
    deep = members + w.shape[2]
    s = lax.ppermute(pack_row(u, w), "row", forward("row"))
    sym = prepare(tapers)
    first, final = pack_columns(u, w, live, index, sym)
    left = lax.ppermute(final, "col", forward("col"))
    right = lax.ppermute(first, "col", backward("col"))
    inc, left, right = lax.optimization_barrier((inner(u, w, live, index, tapers, sym), left, right))
    corner = lax.ppermute(
        jnp.stack([left[rows - 1, :deep], right[rows - 1, :deep]]), "row", forward("row")
    )
    back, held = above(s, u, w, left, right, live, index, tapers)
    back = lax.ppermute(back, "row", backward("row"))
    inc, low = outer(inc, held, s, corner, u, w, left, right, live, index, tapers)
    return finish(inc, low, back)


def solution(mesh):
    return jax.shard_map(
        body,
        mesh=mesh,
        in_specs=(
            P("row", "col", None, None),
            P("row", "col", None, None),
            P("row", "col", None),
            P("row", "col", None),
            P(),
        ),
        out_specs=P("row", "col", None, None),
        check_vma=False,
    )
```

```python
import jax
import jax.numpy as jnp
from jax import lax
from jax.experimental import pallas as pl
from jax.experimental.pallas import tpu as pltpu
from jax.sharding import PartitionSpec as P

MEMBERS = 256
GRANT = 16 << 20
SCALE = 1.0 / (MEMBERS - 1)
TN = (((0,), (0,)), ((), ()))
NT = (((1,), (1,)), ((), ()))
NN = (((1,), (0,)), ((), ()))
VMEM = pl.BlockSpec(memory_space=pltpu.VMEM)
ANY = pl.BlockSpec(memory_space=pl.ANY)
HBM = pl.BlockSpec(memory_space=pltpu.HBM)


def dot(a, b, dims):
    return lax.dot_general(a, b, dims, preferred_element_type=jnp.float32)


def cat(parts, axis):
    return parts[0] if len(parts) == 1 else jnp.concatenate(parts, axis=axis)


def tapered(gram, rho, live):
    factor = live.astype(jnp.float32) * SCALE
    return (rho.astype(jnp.float32) * gram * factor).astype(jnp.bfloat16)


def even_column():
    return lax.rem(lax.axis_index("col"), 2) == 0


def sides(inside, outside):
    even = even_column()
    return (
        lambda *at: jnp.where(even, outside[at], inside[at]),
        lambda *at: jnp.where(even, inside[at], outside[at]),
    )


def prepare_kernel(tapers, sym):
    for n in range(tapers.shape[0]):
        t = tapers[n].astype(jnp.float32)
        sym[n] = 0.5 * (t + t.T)


def prepare(tapers):
    return pl.pallas_call(
        prepare_kernel,
        out_shape=jax.ShapeDtypeStruct(tapers.shape, jnp.float32),
        in_specs=[VMEM],
        out_specs=VMEM,
        compiler_params=pltpu.CompilerParams(vmem_limit_bytes=GRANT),
        cost_estimate=pl.CostEstimate(flops=0, bytes_accessed=16 << 20, transcendentals=0),
        name="prepare",
    )(tapers)


def inner_kernel(u, w, live, index, tapers, sym, out, held):
    rows, cols, _, cells = u.shape
    def ahead(a, b, last):
        near = [(4, a, b)]
        if b + 1 < cols:
            near.append((5, a, b + 1))
        if not last:
            for k in (6, 7, 8):
                if 0 <= b + k - 7 < cols:
                    near.append((k, a + 1, b + k - 7))
        return near

    def row(a, last):
        on, which = live[a], index[a]
        for b in range(cols):
            near = ahead(a, b, last)
            gram = dot(u[a, b], cat([u[p, q] for _, p, q in near], 1), TN)
            for n, (k, _, _) in enumerate(near):
                at = which[b, k]
                rho = sym[at] if k == 4 else tapers[at]
                held[b, :, (k - 4) * cells : (k - 3) * cells] = tapered(
                    gram[:, n * cells : (n + 1) * cells], rho, on[b, k]
                )
        for b in range(cols):
            near = ahead(a, b, last)
            total = dot(
                cat([w[p, q] for _, p, q in near], 1),
                cat([held[b, :, (k - 4) * cells : (k - 3) * cells] for k, _, _ in near], 1),
                NT,
            )
            if b > 0:
                total += dot(w[a, b - 1], held[b - 1, :, cells : 2 * cells], NN)
            out[a, b] += total
            if not last:
                back = [(k, b - (k - 7)) for k in (6, 7, 8) if 0 <= b - (k - 7) < cols]
                out[a + 1, b] = dot(
                    cat([w[a, q] for _, q in back], 1),
                    cat([held[q, :, (k - 4) * cells : (k - 3) * cells] for k, q in back], 0),
                    NN,
                )

    out[0] = jnp.zeros_like(out[0])

    @pl.loop(0, rows - 1)
    def _(a):
        row(a, False)

    row(rows - 1, True)


def inner(u, w, live, index, tapers, sym):
    rows, cols, members, cells = u.shape
    columns = w.shape[2]
    pairs = 5 * rows * cols
    return pl.pallas_call(
        inner_kernel,
        out_shape=jax.ShapeDtypeStruct((rows, cols, columns, cells), jnp.float32),
        in_specs=[VMEM] * 6,
        out_specs=VMEM,
        scratch_shapes=[pltpu.VMEM((cols, cells, 5 * cells), jnp.bfloat16)],
        compiler_params=pltpu.CompilerParams(vmem_limit_bytes=GRANT),
        cost_estimate=pl.CostEstimate(
            flops=2 * pairs * cells * cells * (members + 2 * columns),
            bytes_accessed=4 << 20,
            transcendentals=0,
        ),
        name="inner",
    )(u, w, live, index, tapers, sym)


def above_kernel(s, u, w, inside, outside, live, index, tapers, back, held):
    cols, _, cells = s.shape
    members = u.shape[2]
    deep = members + w.shape[2]
    left, right = sides(inside, outside)
    on, which = live[0], index[0]
    notes = [near(0, slice(deep, None)).astype(jnp.int32) for near in (left, right)]
    side = [notes[0][cols - 1, 2], notes[0][2 * cols - 1, 2], notes[1][0, 0], notes[1][cols, 0]]

    sources = []
    for c in range(cols):
        grams, weights, lives, rhos = [], [], [], []
        for k in (6, 7, 8):
            q = c + k - 7
            if q < 0:
                near, lively, at = left, side[0], side[1]
            elif q >= cols:
                near, lively, at = right, side[2], side[3]
            else:
                near, lively, at = None, on[q, 8 - k], which[q, 8 - k]
            grams.append(u[0, q] if near is None else near(0, slice(0, members)))
            weights.append(w[0, q] if near is None else near(0, slice(members, deep)))
            lives.append(lively)
            rhos.append(tapers[at])
        gram = dot(s[c, :members], cat(grams, 1), TN)
        block = cat(
            [tapered(gram[:, n * cells : (n + 1) * cells], rhos[n], lives[n]) for n in range(3)], 1
        )
        held[c] = block
        sources.append(cat(weights, 1))
    for c in range(cols):
        back[c] = dot(sources[c], held[c], NT).astype(jnp.bfloat16)


def above(s, u, w, inside, outside, live, index, tapers):
    cols, _, cells = s.shape
    columns = w.shape[2]
    members = u.shape[2]
    return pl.pallas_call(
        above_kernel,
        out_shape=(
            jax.ShapeDtypeStruct((cols, columns, cells), jnp.bfloat16),
            jax.ShapeDtypeStruct((cols, cells, 3 * cells), jnp.bfloat16),
        ),
        in_specs=[VMEM] * 8,
        out_specs=(VMEM, VMEM),
        compiler_params=pltpu.CompilerParams(vmem_limit_bytes=GRANT),
        cost_estimate=pl.CostEstimate(
            flops=2 * 3 * cols * cells * cells * (members + columns),
            bytes_accessed=2 << 20,
            transcendentals=0,
        ),
        name="above",
    )(s, u, w, inside, outside, live, index, tapers)


def outer_kernel(inc, held, s, corner, u, w, inside, outside, live, index, tapers, out, low):
    rows, cols, members, cells = u.shape
    deep = members + w.shape[2]
    last = cols - 1
    left, right = sides(inside, outside)
    first = even_column().astype(jnp.int32)
    on = [live[a] for a in range(rows)]
    which = [index[a] for a in range(rows)]
    total = {}

    def add(a, q, value):
        total[a, q] = total[a, q] + value if (a, q) in total else value

    for q in range(cols):
        back = [(k, q - (k - 7)) for k in (6, 7, 8) if 0 <= q - (k - 7) < cols]
        sources = [s[c, members:deep] for _, c in back]
        blocks = [held[c, :, (k - 6) * cells : (k - 5) * cells] for k, c in back]
        for edge, k, far in ((0, 8, first), (last, 6, 1 - first)):
            if q == edge:
                gram = dot(corner[far, :members], u[0, q], TN)
                sources.append(corner[far, members:deep])
                blocks.append(tapered(gram, tapers[which[0][q, 8 - k]], on[0][q, 8 - k]))
        add(0, q, dot(cat(sources, 1), cat(blocks, 0), NN))

    for a in range(rows):
        near = [(5, a)] + ([(8, a + 1)] if a + 1 < rows else [])
        gram = dot(left(a, slice(0, members)), cat([u[p, 0] for _, p in near], 1), TN)
        blocks = cat(
            [
                tapered(gram[:, n * cells : (n + 1) * cells], tapers[which[p][0, 8 - k]], on[p][0, 8 - k])
                for n, (k, p) in enumerate(near)
            ],
            1,
        )
        both = dot(left(a, slice(members, deep)), blocks, NN)
        for n, (_, p) in enumerate(near):
            add(p, 0, both[:, n * cells : (n + 1) * cells])
        gram = dot(u[a, last], cat([right(p, slice(0, members)) for _, p in near], 1), TN)
        blocks = cat(
            [
                tapered(gram[:, n * cells : (n + 1) * cells], tapers[which[a][last, k]], on[a][last, k])
                for n, (k, _) in enumerate(near)
            ],
            1,
        )
        add(a, last, dot(cat([right(p, slice(members, deep)) for _, p in near], 1), blocks, NT))
        if a + 1 < rows:
            gram = dot(u[a, 0], left(a + 1, slice(0, members)), TN)
            block = tapered(gram, tapers[which[a][0, 6]], on[a][0, 6])
            add(a, 0, dot(left(a + 1, slice(members, deep)), block, NT))
            gram = dot(right(a, slice(0, members)), u[a + 1, last], TN)
            block = tapered(gram, tapers[which[a + 1][last, 2]], on[a + 1][last, 2])
            add(a + 1, last, dot(right(a, slice(members, deep)), block, NN))

    for a in range(rows):
        for q in range(cols):
            value = inc[a, q] + total[a, q] if (a, q) in total else inc[a, q]
            out[a, q] = value
            if a == rows - 1:
                low[q] = value


def outer(inc, held, s, corner, u, w, inside, outside, live, index, tapers):
    rows, cols, members, cells = u.shape
    columns = w.shape[2]
    return pl.pallas_call(
        outer_kernel,
        out_shape=(jax.ShapeDtypeStruct(inc.shape, inc.dtype), jax.ShapeDtypeStruct(inc.shape[1:], inc.dtype)),
        in_specs=[VMEM] * 11,
        out_specs=(VMEM, VMEM),
        compiler_params=pltpu.CompilerParams(vmem_limit_bytes=GRANT),
        cost_estimate=pl.CostEstimate(
            flops=2 * (6 * rows + 3 * cols) * cells * cells * (members + columns),
            bytes_accessed=4 << 20,
            transcendentals=0,
        ),
        name="outer",
    )(inc, held, s, corner, u, w, inside, outside, live, index, tapers)


def finish_kernel(inc, low, back, out, total, sem):
    del inc
    total[...] = low[...] + back[...].astype(jnp.float32)
    copy = pltpu.make_async_copy(total, out.at[out.shape[0] - 1], sem)
    copy.start()
    copy.wait()


def finish(inc, low, back):
    return pl.pallas_call(
        finish_kernel,
        out_shape=jax.ShapeDtypeStruct(inc.shape, inc.dtype),
        in_specs=[ANY, VMEM, VMEM],
        out_specs=ANY,
        scratch_shapes=[pltpu.VMEM(low.shape, low.dtype), pltpu.SemaphoreType.DMA(())],
        input_output_aliases={0: 0},
        compiler_params=pltpu.CompilerParams(vmem_limit_bytes=GRANT),
        cost_estimate=pl.CostEstimate(flops=low.size, bytes_accessed=10 * low.size, transcendentals=0),
        name="finish",
    )(inc, low, back)


def forward(axis):
    return [(i, i + 1) for i in range(lax.axis_size(axis) - 1)]


def swaps(axis, start):
    pairs = [(i, i + 1) for i in range(start, lax.axis_size(axis) - 1, 2)]
    return pairs + [(b, a) for a, b in pairs]


def backward(axis):
    return [(i + 1, i) for i in range(lax.axis_size(axis) - 1)]


def pack_row_kernel(u, w, out, sem):
    rows, _, members, _ = u.shape
    deep = members + w.shape[2]
    copies = [
        pltpu.make_async_copy(u.at[rows - 1], out.at[:, :members], sem.at[0]),
        pltpu.make_async_copy(w.at[rows - 1], out.at[:, members:deep], sem.at[1]),
    ]
    for copy in copies:
        copy.start()
    for copy in copies:
        copy.wait()


def pack_row(u, w):
    _, cols, members, cells = u.shape
    shape = (cols, members + w.shape[2], cells)
    return pl.pallas_call(
        pack_row_kernel,
        out_shape=pltpu.VMEM(shape, u.dtype),
        in_specs=[HBM, HBM],
        out_specs=VMEM,
        scratch_shapes=[pltpu.SemaphoreType.DMA((2,))],
        cost_estimate=pl.CostEstimate(flops=0, bytes_accessed=4 * cols * shape[1] * cells, transcendentals=0),
        name="pack_row",
    )(u, w)


def pack_columns_kernel(u, w, live, index, sym, inner_side, outer_side, sem):
    del sym
    rows, cols, members, cells = u.shape
    deep = members + w.shape[2]
    turn = (cols - 1) * even_column().astype(jnp.int32)
    copies = []
    for n, (out, b) in enumerate(((inner_side, turn), (outer_side, cols - 1 - turn))):
        copies.append(pltpu.make_async_copy(u.at[:, b], out.at[:, :members], sem.at[n, 0]))
        copies.append(pltpu.make_async_copy(w.at[:, b], out.at[:, members:deep], sem.at[n, 1]))
    for copy in copies:
        copy.start()
    for a in range(rows):
        lines = jnp.concatenate([live[a], index[a]], 0).astype(jnp.float32)
        blank = jnp.zeros((2 * cols, cells - live.shape[2]), jnp.float32)
        note = jnp.concatenate([lines, blank], 1).astype(jnp.bfloat16)
        inner_side[a, deep:] = note
        outer_side[a, deep:] = note
    for copy in copies:
        copy.wait()


def pack_columns(u, w, live, index, sym):
    rows, cols, members, cells = u.shape
    shape = (rows, members + w.shape[2] + 2 * cols, cells)
    return pl.pallas_call(
        pack_columns_kernel,
        out_shape=(jax.ShapeDtypeStruct(shape, u.dtype),) * 2,
        in_specs=[ANY, ANY, VMEM, VMEM, VMEM],
        out_specs=(VMEM, VMEM),
        scratch_shapes=[pltpu.SemaphoreType.DMA((2, 2))],
        compiler_params=pltpu.CompilerParams(vmem_limit_bytes=GRANT),
        cost_estimate=pl.CostEstimate(flops=0, bytes_accessed=8 * rows * shape[1] * cells, transcendentals=0),
        name="pack_columns",
    )(u, w, live, index, sym)


def body(perturbations, weights, live, index, tapers):
    rows, cols, members, cells = perturbations.shape
    deep = members + weights.shape[2]
    row = pack_row(perturbations, weights)
    row, u, w, tapers = lax.optimization_barrier((row, perturbations, weights, tapers))
    s = lax.ppermute(row, "row", forward("row"))
    sym = prepare(tapers)
    inner_side, outer_side = pack_columns(u, w, live, index, sym)
    inside = lax.ppermute(inner_side, "col", swaps("col", 0))
    outside = lax.ppermute(outer_side, "col", swaps("col", 1))
    inc, inside, outside = lax.optimization_barrier((inner(u, w, live, index, tapers, sym), inside, outside))
    corner = lax.ppermute(
        jnp.stack([inside[rows - 1, :deep], outside[rows - 1, :deep]]), "row", forward("row")
    )
    back, held = above(s, u, w, inside, outside, live, index, tapers)
    back = lax.ppermute(back, "row", backward("row"))
    inc, low = outer(inc, held, s, corner, u, w, inside, outside, live, index, tapers)
    return finish(inc, low, back)


def solution(mesh):
    return jax.shard_map(
        body,
        mesh=mesh,
        in_specs=(
            P("row", "col", None, None),
            P("row", "col", None, None),
            P("row", "col", None),
            P("row", "col", None),
            P(),
        ),
        out_specs=P("row", "col", None, None),
        check_vma=False,
    )
```

```python
import functools

import jax
import jax.numpy as jnp
from jax import lax
from jax.experimental import pallas as pl
from jax.experimental.pallas import tpu as pltpu
from jax.sharding import PartitionSpec as P

MEMBERS = 256
GRANT = 16 << 20
ENDS = 3
SCALE = 1.0 / (MEMBERS - 1)
TN = (((0,), (0,)), ((), ()))
NT = (((1,), (1,)), ((), ()))
NN = (((1,), (0,)), ((), ()))
VMEM = pl.BlockSpec(memory_space=pltpu.VMEM)
ANY = pl.BlockSpec(memory_space=pl.ANY)
HBM = pl.BlockSpec(memory_space=pltpu.HBM)


def dot(a, b, dims):
    return lax.dot_general(a, b, dims, preferred_element_type=jnp.float32)


def cat(parts, axis):
    return parts[0] if len(parts) == 1 else jnp.concatenate(parts, axis=axis)


def tapered(gram, rho, live):
    factor = live.astype(jnp.float32) * SCALE
    return (rho.astype(jnp.float32) * gram * factor).astype(jnp.bfloat16)


def even_column():
    return lax.rem(lax.axis_index("col"), 2) == 0


def sides(inside, outside):
    even = even_column()
    return (
        lambda *at: jnp.where(even, outside[at], inside[at]),
        lambda *at: jnp.where(even, inside[at], outside[at]),
    )


def prepare_kernel(start, tapers, after, sym):
    del after
    for n in range(sym.shape[0]):
        t = tapers[start + n].astype(jnp.float32)
        sym[n] = 0.5 * (t + t.T)


def prepare(tapers, start, count, after):
    cells = tapers.shape[1]
    return pl.pallas_call(
        functools.partial(prepare_kernel, start),
        out_shape=jax.ShapeDtypeStruct((count, cells, cells), jnp.float32),
        in_specs=[VMEM, VMEM],
        out_specs=VMEM,
        compiler_params=pltpu.CompilerParams(vmem_limit_bytes=GRANT),
        cost_estimate=pl.CostEstimate(flops=0, bytes_accessed=6 * count * cells * cells, transcendentals=0),
        name="prepare",
    )(tapers, after)


def inner_kernel(u, w, live, index, tapers, low, high, out, held):
    rows, cols, _, cells = u.shape
    half = low.shape[0]

    def own_taper(at):
        return jnp.where(at < half, low[jnp.minimum(at, half - 1)], high[jnp.maximum(at - half, 0)])

    def ahead(a, b, last):
        near = [(4, a, b)]
        if b + 1 < cols:
            near.append((5, a, b + 1))
        if not last:
            for k in (6, 7, 8):
                if 0 <= b + k - 7 < cols:
                    near.append((k, a + 1, b + k - 7))
        return near

    def row(a, last):
        on, which = live[a], index[a]
        for b in range(cols):
            near = ahead(a, b, last)
            gram = dot(u[a, b], cat([u[p, q] for _, p, q in near], 1), TN)
            for n, (k, _, _) in enumerate(near):
                at = which[b, k]
                rho = own_taper(at) if k == 4 else tapers[at]
                held[b, :, (k - 4) * cells : (k - 3) * cells] = tapered(
                    gram[:, n * cells : (n + 1) * cells], rho, on[b, k]
                )
        for b in range(cols):
            near = ahead(a, b, last)
            total = dot(
                cat([w[p, q] for _, p, q in near], 1),
                cat([held[b, :, (k - 4) * cells : (k - 3) * cells] for k, _, _ in near], 1),
                NT,
            )
            if b > 0:
                total += dot(w[a, b - 1], held[b - 1, :, cells : 2 * cells], NN)
            out[a, b] += total
            if not last:
                back = [(k, b - (k - 7)) for k in (6, 7, 8) if 0 <= b - (k - 7) < cols]
                out[a + 1, b] = dot(
                    cat([w[a, q] for _, q in back], 1),
                    cat([held[q, :, (k - 4) * cells : (k - 3) * cells] for k, q in back], 0),
                    NN,
                )

    out[0] = jnp.zeros_like(out[0])

    @pl.loop(0, rows - 1)
    def _(a):
        row(a, False)

    row(rows - 1, True)


def inner(u, w, live, index, tapers, low, high):
    rows, cols, members, cells = u.shape
    columns = w.shape[2]
    pairs = 5 * rows * cols
    return pl.pallas_call(
        inner_kernel,
        out_shape=jax.ShapeDtypeStruct((rows, cols, columns, cells), jnp.float32),
        in_specs=[VMEM] * 7,
        out_specs=VMEM,
        scratch_shapes=[pltpu.VMEM((cols, cells, 5 * cells), jnp.bfloat16)],
        compiler_params=pltpu.CompilerParams(vmem_limit_bytes=GRANT),
        cost_estimate=pl.CostEstimate(
            flops=2 * pairs * cells * cells * (members + 2 * columns),
            bytes_accessed=4 << 20,
            transcendentals=0,
        ),
        name="inner",
    )(u, w, live, index, tapers, low, high)


def edges_kernel(s, u, w, inside, outside, live, index, tapers, back, held, to_inside, to_outside):
    cols, members, cells = u.shape[1:]
    deep = members + w.shape[2]
    left, right = sides(inside, outside)
    on, which = live[0], index[0]
    places = end_places(cols)
    beyond = {}
    for q, near, k, line in ((-1, left, 2, cols - 1), (cols, right, 0, 0)):
        note = near(0, slice(deep, None)).astype(jnp.int32)
        beyond[q] = near, note[line, k], note[cols + line, k]
    sources = []
    for n, c in enumerate(places):
        grams, weights, lives, rhos = [], [], [], []
        for k in (6, 7, 8):
            q = c + k - 7
            if q in beyond:
                near, lively, at = beyond[q]
                grams.append(near(0, slice(0, members)))
                weights.append(near(0, slice(members, deep)))
            else:
                lively, at = on[q, 8 - k], which[q, 8 - k]
                grams.append(u[0, q])
                weights.append(w[0, q])
            lives.append(lively)
            rhos.append(tapers[at])
        gram = dot(s[n, :members], cat(grams, 1), TN)
        held[n] = cat([tapered(gram[:, m * cells : (m + 1) * cells], rhos[m], lives[m]) for m in range(3)], 1)
        sources.append(cat(weights, 1))
    for n in range(len(places)):
        back[n] = dot(sources[n], held[n], NT).astype(jnp.bfloat16)
    final = len(places) - 1
    to_left = dot(s[0, members:deep], held[0, :, :cells], NN)
    to_right = dot(s[final, members:deep], held[final, :, 2 * cells :], NN)
    even = even_column()
    to_inside[...] = jnp.where(even, to_right, to_left)
    to_outside[...] = jnp.where(even, to_left, to_right)


def end_places(cols):
    return list(range(ENDS)) + list(range(cols - ENDS, cols))


def edges(s, u, w, inside, outside, live, index, tapers):
    cells = u.shape[3]
    members = u.shape[2]
    columns = w.shape[2]
    part = jax.ShapeDtypeStruct((columns, cells), jnp.float32)
    return pl.pallas_call(
        edges_kernel,
        out_shape=(
            jax.ShapeDtypeStruct((2 * ENDS, columns, cells), jnp.bfloat16),
            jax.ShapeDtypeStruct((2 * ENDS, cells, 3 * cells), jnp.bfloat16),
            part,
            part,
        ),
        in_specs=[VMEM] * 8,
        out_specs=(VMEM,) * 4,
        compiler_params=pltpu.CompilerParams(vmem_limit_bytes=GRANT),
        cost_estimate=pl.CostEstimate(
            flops=2 * 6 * ENDS * cells * cells * (members + columns), bytes_accessed=1 << 20, transcendentals=0
        ),
        name="edges",
    )(s, u, w, inside, outside, live, index, tapers)


def above_kernel(s, edge_back, u, w, live, index, tapers, back, held):
    cols, members, cells = u.shape[1:]
    on, which = live[0], index[0]
    for c in range(ENDS, cols - ENDS):
        near = [(k, c + k - 7) for k in (6, 7, 8)]
        gram = dot(s[c - ENDS, :members], cat([u[0, q] for _, q in near], 1), TN)
        held[c - ENDS] = cat(
            [
                tapered(gram[:, n * cells : (n + 1) * cells], tapers[which[q, 8 - k]], on[q, 8 - k])
                for n, (k, q) in enumerate(near)
            ],
            1,
        )
    for c in range(ENDS, cols - ENDS):
        back[c] = dot(cat([w[0, c + n] for n in (-1, 0, 1)], 1), held[c - ENDS], NT).astype(jnp.bfloat16)
    for n, c in enumerate(end_places(cols)):
        back[c] = edge_back[n]


def above(s, edge_back, u, w, live, index, tapers):
    cols, members, cells = u.shape[1:]
    columns = w.shape[2]
    return pl.pallas_call(
        above_kernel,
        out_shape=(
            jax.ShapeDtypeStruct((cols, columns, cells), jnp.bfloat16),
            jax.ShapeDtypeStruct((cols - 2 * ENDS, cells, 3 * cells), jnp.bfloat16),
        ),
        in_specs=[VMEM] * 7,
        out_specs=(VMEM, VMEM),
        compiler_params=pltpu.CompilerParams(vmem_limit_bytes=GRANT),
        cost_estimate=pl.CostEstimate(
            flops=2 * 3 * cols * cells * cells * (members + columns),
            bytes_accessed=2 << 20,
            transcendentals=0,
        ),
        name="above",
    )(s, edge_back, u, w, live, index, tapers)


def outer_kernel(
    inc, ends, end_held, s, held, from_inside, from_outside, u, w, inside, outside, live, index, tapers, out, low
):
    rows, cols, members, cells = u.shape
    deep = members + w.shape[2]
    last = cols - 1
    left, right = sides(inside, outside)
    on = [live[a] for a in range(rows)]
    which = [index[a] for a in range(rows)]
    total = {}

    def add(a, q, value):
        total[a, q] = total[a, q] + value if (a, q) in total else value

    places = end_places(cols)

    def source(c):
        if c in places:
            n = places.index(c)
            return ends[n, members:deep], end_held[n]
        return s[c - ENDS, members:deep], held[c - ENDS]

    for q in range(cols):
        back = [(k, source(q - (k - 7))) for k in (6, 7, 8) if 0 <= q - (k - 7) < cols]
        blocks = [block[:, (k - 6) * cells : (k - 5) * cells] for k, (_, block) in back]
        add(0, q, dot(cat([weight for _, (weight, _) in back], 1), cat(blocks, 0), NN))
    even = even_column()
    add(0, 0, jnp.where(even, from_outside[...], from_inside[...]))
    add(0, last, jnp.where(even, from_inside[...], from_outside[...]))

    for a in range(rows):
        near = [(5, a)] + ([(8, a + 1)] if a + 1 < rows else [])
        gram = dot(left(a, slice(0, members)), cat([u[p, 0] for _, p in near], 1), TN)
        blocks = cat(
            [
                tapered(gram[:, n * cells : (n + 1) * cells], tapers[which[p][0, 8 - k]], on[p][0, 8 - k])
                for n, (k, p) in enumerate(near)
            ],
            1,
        )
        both = dot(left(a, slice(members, deep)), blocks, NN)
        for n, (_, p) in enumerate(near):
            add(p, 0, both[:, n * cells : (n + 1) * cells])
        gram = dot(u[a, last], cat([right(p, slice(0, members)) for _, p in near], 1), TN)
        blocks = cat(
            [
                tapered(gram[:, n * cells : (n + 1) * cells], tapers[which[a][last, k]], on[a][last, k])
                for n, (k, _) in enumerate(near)
            ],
            1,
        )
        add(a, last, dot(cat([right(p, slice(members, deep)) for _, p in near], 1), blocks, NT))
        if a + 1 < rows:
            gram = dot(u[a, 0], left(a + 1, slice(0, members)), TN)
            block = tapered(gram, tapers[which[a][0, 6]], on[a][0, 6])
            add(a, 0, dot(left(a + 1, slice(members, deep)), block, NT))
            gram = dot(right(a, slice(0, members)), u[a + 1, last], TN)
            block = tapered(gram, tapers[which[a + 1][last, 2]], on[a + 1][last, 2])
            add(a + 1, last, dot(right(a, slice(members, deep)), block, NN))

    for a in range(rows):
        for q in range(cols):
            value = inc[a, q] + total[a, q] if (a, q) in total else inc[a, q]
            out[a, q] = value
            if a == rows - 1:
                low[q] = value


def outer(inc, *around):
    ends, end_held, s, held, from_inside, from_outside, u, w, inside, outside, live, index, tapers = around
    rows, cols, members, cells = u.shape
    columns = w.shape[2]
    return pl.pallas_call(
        outer_kernel,
        out_shape=(jax.ShapeDtypeStruct(inc.shape, inc.dtype), jax.ShapeDtypeStruct(inc.shape[1:], inc.dtype)),
        in_specs=[VMEM] * 14,
        out_specs=(VMEM, VMEM),
        compiler_params=pltpu.CompilerParams(vmem_limit_bytes=GRANT),
        cost_estimate=pl.CostEstimate(
            flops=2 * (6 * rows + 3 * cols) * cells * cells * (members + columns),
            bytes_accessed=4 << 20,
            transcendentals=0,
        ),
        name="outer",
    )(inc, *around)


def finish_kernel(inc, low, back, out, total, sem):
    del inc
    total[...] = low[...] + back[...].astype(jnp.float32)
    copy = pltpu.make_async_copy(total, out.at[out.shape[0] - 1], sem)
    copy.start()
    copy.wait()


def finish(inc, low, back):
    return pl.pallas_call(
        finish_kernel,
        out_shape=jax.ShapeDtypeStruct(inc.shape, inc.dtype),
        in_specs=[ANY, VMEM, VMEM],
        out_specs=ANY,
        scratch_shapes=[pltpu.VMEM(low.shape, low.dtype), pltpu.SemaphoreType.DMA(())],
        input_output_aliases={0: 0},
        compiler_params=pltpu.CompilerParams(vmem_limit_bytes=GRANT),
        cost_estimate=pl.CostEstimate(flops=low.size, bytes_accessed=10 * low.size, transcendentals=0),
        name="finish",
    )(inc, low, back)


def forward(axis):
    return [(i, i + 1) for i in range(lax.axis_size(axis) - 1)]


def swaps(axis, start):
    pairs = [(i, i + 1) for i in range(start, lax.axis_size(axis) - 1, 2)]
    return pairs + [(b, a) for a, b in pairs]


def backward(axis):
    return [(i + 1, i) for i in range(lax.axis_size(axis) - 1)]


def pack_ends_kernel(u, w, out, sem):
    rows, cols, members, _ = u.shape
    deep = members + w.shape[2]
    copies = []
    for n, q in enumerate((0, cols - ENDS)):
        to = out.at[ENDS * n : ENDS * n + ENDS]
        copies.append(pltpu.make_async_copy(u.at[rows - 1, q : q + ENDS], to.at[:, :members], sem.at[n, 0]))
        copies.append(pltpu.make_async_copy(w.at[rows - 1, q : q + ENDS], to.at[:, members:deep], sem.at[n, 1]))
    for copy in copies:
        copy.start()
    for copy in copies:
        copy.wait()


def pack_ends(u, w):
    members, cells = u.shape[2:]
    shape = (2 * ENDS, members + w.shape[2], cells)
    return pl.pallas_call(
        pack_ends_kernel,
        out_shape=pltpu.VMEM(shape, u.dtype),
        in_specs=[HBM, HBM],
        out_specs=VMEM,
        scratch_shapes=[pltpu.SemaphoreType.DMA((2, 2))],
        cost_estimate=pl.CostEstimate(flops=0, bytes_accessed=8 * ENDS * shape[1] * cells, transcendentals=0),
        name="pack_ends",
    )(u, w)


def pack_row_kernel(u, w, sym, out, sem):
    del sym
    rows, cols, members, _ = u.shape
    deep = members + w.shape[2]
    between = slice(ENDS, cols - ENDS)
    copies = [
        pltpu.make_async_copy(u.at[rows - 1, between], out.at[:, :members], sem.at[0]),
        pltpu.make_async_copy(w.at[rows - 1, between], out.at[:, members:deep], sem.at[1]),
    ]
    for copy in copies:
        copy.start()
    for copy in copies:
        copy.wait()


def pack_row(u, w, sym):
    cols, members, cells = u.shape[1:]
    shape = (cols - 2 * ENDS, members + w.shape[2], cells)
    return pl.pallas_call(
        pack_row_kernel,
        out_shape=jax.ShapeDtypeStruct(shape, u.dtype),
        in_specs=[ANY, ANY, VMEM],
        out_specs=VMEM,
        scratch_shapes=[pltpu.SemaphoreType.DMA((2,))],
        compiler_params=pltpu.CompilerParams(vmem_limit_bytes=GRANT),
        cost_estimate=pl.CostEstimate(flops=0, bytes_accessed=4 * shape[0] * shape[1] * cells, transcendentals=0),
        name="pack_row",
    )(u, w, sym)


def pack_columns_kernel(u, w, live, index, sym, inner_side, outer_side, sem):
    del sym
    rows, cols, members, cells = u.shape
    deep = members + w.shape[2]
    turn = (cols - 1) * even_column().astype(jnp.int32)
    copies = []
    for n, (out, b) in enumerate(((inner_side, turn), (outer_side, cols - 1 - turn))):
        copies.append(pltpu.make_async_copy(u.at[:, b], out.at[:, :members], sem.at[n, 0]))
        copies.append(pltpu.make_async_copy(w.at[:, b], out.at[:, members:deep], sem.at[n, 1]))
    for copy in copies:
        copy.start()
    for a in range(rows):
        lines = jnp.concatenate([live[a], index[a]], 0).astype(jnp.float32)
        blank = jnp.zeros((2 * cols, cells - live.shape[2]), jnp.float32)
        note = jnp.concatenate([lines, blank], 1).astype(jnp.bfloat16)
        inner_side[a, deep:] = note
        outer_side[a, deep:] = note
    for copy in copies:
        copy.wait()


def pack_columns(u, w, live, index, sym):
    rows, cols, members, cells = u.shape
    shape = (rows, members + w.shape[2] + 2 * cols, cells)
    return pl.pallas_call(
        pack_columns_kernel,
        out_shape=(jax.ShapeDtypeStruct(shape, u.dtype),) * 2,
        in_specs=[ANY, ANY, VMEM, VMEM, VMEM],
        out_specs=(VMEM, VMEM),
        scratch_shapes=[pltpu.SemaphoreType.DMA((2, 2))],
        compiler_params=pltpu.CompilerParams(vmem_limit_bytes=GRANT),
        cost_estimate=pl.CostEstimate(flops=0, bytes_accessed=8 * rows * shape[1] * cells, transcendentals=0),
        name="pack_columns",
    )(u, w, live, index, sym)


def body(u, w, live, index, tapers):
    half = tapers.shape[0] // 2
    packed = pack_ends(u, w)
    ends = lax.ppermute(packed, "row", forward("row"))
    low = prepare(tapers, 0, half, packed)
    inner_side, outer_side = pack_columns(u, w, live, index, low)
    inside = lax.ppermute(inner_side, "col", swaps("col", 0))
    outside = lax.ppermute(outer_side, "col", swaps("col", 1))
    high = prepare(tapers, half, tapers.shape[0] - half, outer_side)
    row = lax.ppermute(pack_row(u, w, high), "row", forward("row"))
    inc, inside, outside, ends = lax.optimization_barrier(
        (inner(u, w, live, index, tapers, low, high), inside, outside, ends)
    )
    end_back, end_held, to_inside, to_outside = edges(ends, u, w, inside, outside, live, index, tapers)
    from_inside = lax.ppermute(to_inside, "col", swaps("col", 0))
    from_outside = lax.ppermute(to_outside, "col", swaps("col", 1))
    row, from_inside, from_outside = lax.optimization_barrier((row, from_inside, from_outside))
    back, held = above(row, end_back, u, w, live, index, tapers)
    back = lax.ppermute(back, "row", backward("row"))
    inc, low_row = outer(
        inc, ends, end_held, row, held, from_inside, from_outside, u, w, inside, outside, live, index, tapers
    )
    return finish(inc, low_row, back)


def solution(mesh):
    return jax.shard_map(
        body,
        mesh=mesh,
        in_specs=(
            P("row", "col", None, None),
            P("row", "col", None, None),
            P("row", "col", None),
            P("row", "col", None),
            P(),
        ),
        out_specs=P("row", "col", None, None),
        check_vma=False,
    )
```

```python
import jax
import jax.numpy as jnp
from jax import lax
from jax.experimental import pallas as pl
from jax.experimental.pallas import tpu as pltpu
from jax.sharding import PartitionSpec as P

MEMBERS = 256
GRANT = 16 << 20
ENDS = 2
SCALE = 1.0 / (MEMBERS - 1)
TN = (((0,), (0,)), ((), ()))
NT = (((1,), (1,)), ((), ()))
NN = (((1,), (0,)), ((), ()))
VMEM = pl.BlockSpec(memory_space=pltpu.VMEM)
ANY = pl.BlockSpec(memory_space=pl.ANY)
HBM = pl.BlockSpec(memory_space=pltpu.HBM)


def dot(a, b, dims):
    return lax.dot_general(a, b, dims, preferred_element_type=jnp.float32)


def cat(parts, axis):
    return parts[0] if len(parts) == 1 else jnp.concatenate(parts, axis=axis)


def tapered(gram, rho, live):
    factor = live.astype(jnp.float32) * SCALE
    return (rho.astype(jnp.float32) * gram * factor).astype(jnp.bfloat16)


def even_column():
    return lax.rem(lax.axis_index("col"), 2) == 0


def sides(inside, outside):
    even = even_column()
    return (
        lambda *at: jnp.where(even, outside[at], inside[at]),
        lambda *at: jnp.where(even, inside[at], outside[at]),
    )


def inner_kernel(u, w, live, index, tapers, ends, out, sym, held):
    rows, cols, _, cells = u.shape
    del ends
    for n in range(tapers.shape[0]):
        t = tapers[n].astype(jnp.float32)
        sym[n] = 0.5 * (t + t.T)

    def ahead(a, b, last):
        near = [(4, a, b)]
        if b + 1 < cols:
            near.append((5, a, b + 1))
        if not last:
            for k in (6, 7, 8):
                if 0 <= b + k - 7 < cols:
                    near.append((k, a + 1, b + k - 7))
        return near

    def row(a, last):
        on, which = live[a], index[a]
        for b in range(cols):
            near = ahead(a, b, last)
            gram = dot(u[a, b], cat([u[p, q] for _, p, q in near], 1), TN)
            for n, (k, _, _) in enumerate(near):
                at = which[b, k]
                rho = sym[at] if k == 4 else tapers[at]
                held[b, :, (k - 4) * cells : (k - 3) * cells] = tapered(
                    gram[:, n * cells : (n + 1) * cells], rho, on[b, k]
                )
        for b in range(cols):
            near = ahead(a, b, last)
            total = dot(
                cat([w[p, q] for _, p, q in near], 1),
                cat([held[b, :, (k - 4) * cells : (k - 3) * cells] for k, _, _ in near], 1),
                NT,
            )
            if b > 0:
                total += dot(w[a, b - 1], held[b - 1, :, cells : 2 * cells], NN)
            out[a, b] += total
            if not last:
                back = [(k, b - (k - 7)) for k in (6, 7, 8) if 0 <= b - (k - 7) < cols]
                out[a + 1, b] = dot(
                    cat([w[a, q] for _, q in back], 1),
                    cat([held[q, :, (k - 4) * cells : (k - 3) * cells] for k, q in back], 0),
                    NN,
                )

    out[0] = jnp.zeros_like(out[0])

    @pl.loop(0, rows - 1)
    def _(a):
        row(a, False)

    row(rows - 1, True)


def inner(u, w, live, index, tapers, ends):
    rows, cols, members, cells = u.shape
    columns = w.shape[2]
    pairs = 5 * rows * cols
    return pl.pallas_call(
        inner_kernel,
        out_shape=jax.ShapeDtypeStruct((rows, cols, columns, cells), jnp.float32),
        in_specs=[VMEM] * 6,
        out_specs=VMEM,
        scratch_shapes=[
            pltpu.VMEM(tapers.shape, jnp.float32),
            pltpu.VMEM((cols, cells, 5 * cells), jnp.bfloat16),
        ],
        compiler_params=pltpu.CompilerParams(vmem_limit_bytes=GRANT),
        cost_estimate=pl.CostEstimate(
            flops=2 * pairs * cells * cells * (members + 2 * columns),
            bytes_accessed=4 << 20,
            transcendentals=0,
        ),
        name="inner",
    )(u, w, live, index, tapers, ends)


def edges_kernel(s, u, w, inside, outside, live, index, tapers, back, held, to_inside, to_outside, side):
    rows, cols, members, cells = u.shape
    last = cols - 1
    deep = members + w.shape[2]
    left, right = sides(inside, outside)
    on = [live[a] for a in range(rows)]
    which = [index[a] for a in range(rows)]
    places = end_places(cols)
    beyond = {}
    for q, near, k, line in ((-1, left, 2, cols - 1), (cols, right, 0, 0)):
        note = near(0, slice(deep, None)).astype(jnp.int32)
        beyond[q] = near, note[line, k], note[cols + line, k]
    sources = []
    for n, c in enumerate(places):
        grams, weights, lives, rhos = [], [], [], []
        for k in (6, 7, 8):
            q = c + k - 7
            if q in beyond:
                near, lively, at = beyond[q]
                grams.append(near(0, slice(0, members)))
                weights.append(near(0, slice(members, deep)))
            else:
                lively, at = on[0][q, 8 - k], which[0][q, 8 - k]
                grams.append(u[0, q])
                weights.append(w[0, q])
            lives.append(lively)
            rhos.append(tapers[at])
        gram = dot(s[n, :members], cat(grams, 1), TN)
        held[n] = cat([tapered(gram[:, m * cells : (m + 1) * cells], rhos[m], lives[m]) for m in range(3)], 1)
        sources.append(cat(weights, 1))
    for n in range(len(places)):
        back[n] = dot(sources[n], held[n], NT).astype(jnp.bfloat16)
    final = len(places) - 1
    to_left = dot(s[0, members:deep], held[0, :, :cells], NN)
    to_right = dot(s[final, members:deep], held[final, :, 2 * cells :], NN)
    even = even_column()
    to_inside[...] = jnp.where(even, to_right, to_left)
    to_outside[...] = jnp.where(even, to_left, to_right)

    total = {}

    def add(a, q, value):
        total[a, q] = total[a, q] + value if (a, q) in total else value

    for a in range(rows):
        near = [(5, a)] + ([(8, a + 1)] if a + 1 < rows else [])
        gram = dot(left(a, slice(0, members)), cat([u[p, 0] for _, p in near], 1), TN)
        blocks = cat(
            [
                tapered(gram[:, n * cells : (n + 1) * cells], tapers[which[p][0, 8 - k]], on[p][0, 8 - k])
                for n, (k, p) in enumerate(near)
            ],
            1,
        )
        both = dot(left(a, slice(members, deep)), blocks, NN)
        for n, (_, p) in enumerate(near):
            add(p, 0, both[:, n * cells : (n + 1) * cells])
        gram = dot(u[a, last], cat([right(p, slice(0, members)) for _, p in near], 1), TN)
        blocks = cat(
            [
                tapered(gram[:, n * cells : (n + 1) * cells], tapers[which[a][last, k]], on[a][last, k])
                for n, (k, _) in enumerate(near)
            ],
            1,
        )
        add(a, last, dot(cat([right(p, slice(members, deep)) for _, p in near], 1), blocks, NT))
        if a + 1 < rows:
            gram = dot(u[a, 0], left(a + 1, slice(0, members)), TN)
            block = tapered(gram, tapers[which[a][0, 6]], on[a][0, 6])
            add(a, 0, dot(left(a + 1, slice(members, deep)), block, NT))
            gram = dot(right(a, slice(0, members)), u[a + 1, last], TN)
            block = tapered(gram, tapers[which[a + 1][last, 2]], on[a + 1][last, 2])
            add(a + 1, last, dot(right(a, slice(members, deep)), block, NN))
    for a in range(rows):
        side[0, a] = total[a, 0]
        side[1, a] = total[a, last]


def end_places(cols):
    return list(range(ENDS)) + list(range(cols - ENDS, cols))


def edges(s, u, w, inside, outside, live, index, tapers):
    cells = u.shape[3]
    members = u.shape[2]
    columns = w.shape[2]
    part = jax.ShapeDtypeStruct((columns, cells), jnp.float32)
    return pl.pallas_call(
        edges_kernel,
        out_shape=(
            jax.ShapeDtypeStruct((2 * ENDS, columns, cells), jnp.bfloat16),
            jax.ShapeDtypeStruct((2 * ENDS, cells, 3 * cells), jnp.bfloat16),
            part,
            part,
            jax.ShapeDtypeStruct((2, u.shape[0], columns, cells), jnp.float32),
        ),
        in_specs=[VMEM] * 8,
        out_specs=(VMEM,) * 5,
        compiler_params=pltpu.CompilerParams(vmem_limit_bytes=GRANT),
        cost_estimate=pl.CostEstimate(
            flops=2 * 6 * ENDS * cells * cells * (members + columns), bytes_accessed=1 << 20, transcendentals=0
        ),
        name="edges",
    )(s, u, w, inside, outside, live, index, tapers)


def above_kernel(s, edge_back, u, w, live, index, tapers, back, held):
    cols, members, cells = u.shape[1:]
    on, which = live[0], index[0]
    for c in range(ENDS, cols - ENDS):
        near = [(k, c + k - 7) for k in (6, 7, 8)]
        gram = dot(s[c - ENDS, :members], cat([u[0, q] for _, q in near], 1), TN)
        held[c - ENDS] = cat(
            [
                tapered(gram[:, n * cells : (n + 1) * cells], tapers[which[q, 8 - k]], on[q, 8 - k])
                for n, (k, q) in enumerate(near)
            ],
            1,
        )
    for c in range(ENDS, cols - ENDS):
        back[c] = dot(cat([w[0, c + n] for n in (-1, 0, 1)], 1), held[c - ENDS], NT).astype(jnp.bfloat16)
    for n, c in enumerate(end_places(cols)):
        back[c] = edge_back[n]


def above(s, edge_back, u, w, live, index, tapers):
    cols, members, cells = u.shape[1:]
    columns = w.shape[2]
    return pl.pallas_call(
        above_kernel,
        out_shape=(
            jax.ShapeDtypeStruct((cols, columns, cells), jnp.bfloat16),
            jax.ShapeDtypeStruct((cols - 2 * ENDS, cells, 3 * cells), jnp.bfloat16),
        ),
        in_specs=[VMEM] * 7,
        out_specs=(VMEM, VMEM),
        compiler_params=pltpu.CompilerParams(vmem_limit_bytes=GRANT),
        cost_estimate=pl.CostEstimate(
            flops=2 * 3 * cols * cells * cells * (members + columns),
            bytes_accessed=2 << 20,
            transcendentals=0,
        ),
        name="above",
    )(s, edge_back, u, w, live, index, tapers)


def outer_kernel(inc, side, ends, end_held, s, held, out, top, low):
    rows, cols, _, cells = inc.shape
    deep = s.shape[1]
    members = deep - inc.shape[2]
    last = cols - 1
    places = end_places(cols)

    def source(c):
        if c in places:
            n = places.index(c)
            return ends[n, members:deep], end_held[n]
        return s[c - ENDS, members:deep], held[c - ENDS]

    for q in range(cols):
        back = [(k, source(q - (k - 7))) for k in (6, 7, 8) if 0 <= q - (k - 7) < cols]
        blocks = [block[:, (k - 6) * cells : (k - 5) * cells] for k, (_, block) in back]
        above = dot(cat([weight for _, (weight, _) in back], 1), cat(blocks, 0), NN)
        if q in (0, last):
            above += side[q // last, 0]
            top[q // last] = inc[0, q] + above
        out[0, q] = inc[0, q] + above
    for a in range(1, rows):
        for q in range(cols):
            value = inc[a, q] + side[q // last, a] if q in (0, last) else inc[a, q]
            out[a, q] = value
            if a == rows - 1:
                low[q] = value


def outer(inc, side, ends, end_held, s, held):
    rows, cols, columns, cells = inc.shape
    return pl.pallas_call(
        outer_kernel,
        out_shape=(
            jax.ShapeDtypeStruct(inc.shape, inc.dtype),
            jax.ShapeDtypeStruct((2, columns, cells), inc.dtype),
            jax.ShapeDtypeStruct(inc.shape[1:], inc.dtype),
        ),
        in_specs=[VMEM] * 6,
        out_specs=(VMEM,) * 3,
        compiler_params=pltpu.CompilerParams(vmem_limit_bytes=GRANT),
        cost_estimate=pl.CostEstimate(
            flops=6 * cols * cells * cells * columns, bytes_accessed=4 << 20, transcendentals=0
        ),
        name="outer",
    )(inc, side, ends, end_held, s, held)


def finish_kernel(inc, top, low, back, from_inside, from_outside, out, ends, total, sem):
    del inc
    rows, cols = out.shape[:2]
    even = even_column()
    total[...] = low[...] + back[...].astype(jnp.float32)
    copies = [pltpu.make_async_copy(total, out.at[rows - 1], sem.at[0])]
    copies[0].start()
    ends[0] = top[0] + jnp.where(even, from_outside[...], from_inside[...])
    ends[1] = top[1] + jnp.where(even, from_inside[...], from_outside[...])
    for n, q in enumerate((0, cols - 1)):
        copies.append(pltpu.make_async_copy(ends.at[n], out.at[0, q], sem.at[1 + n]))
        copies[-1].start()
    for copy in copies:
        copy.wait()


def finish(inc, top, low, back, from_inside, from_outside):
    return pl.pallas_call(
        finish_kernel,
        out_shape=jax.ShapeDtypeStruct(inc.shape, inc.dtype),
        in_specs=[ANY] + [VMEM] * 5,
        out_specs=ANY,
        scratch_shapes=[
            pltpu.VMEM(top.shape, top.dtype),
            pltpu.VMEM(low.shape, low.dtype),
            pltpu.SemaphoreType.DMA((3,)),
        ],
        input_output_aliases={0: 0},
        compiler_params=pltpu.CompilerParams(vmem_limit_bytes=GRANT),
        cost_estimate=pl.CostEstimate(flops=low.size, bytes_accessed=10 * low.size, transcendentals=0),
        name="finish",
    )(inc, top, low, back, from_inside, from_outside)


def forward(axis):
    return [(i, i + 1) for i in range(lax.axis_size(axis) - 1)]


def swaps(axis, start):
    pairs = [(i, i + 1) for i in range(start, lax.axis_size(axis) - 1, 2)]
    return pairs + [(b, a) for a, b in pairs]


def backward(axis):
    return [(i + 1, i) for i in range(lax.axis_size(axis) - 1)]


def pack_ends_kernel(u, w, out, sem):
    rows, cols, members, _ = u.shape
    deep = members + w.shape[2]
    copies = []
    for n, q in enumerate((0, cols - ENDS)):
        to = out.at[ENDS * n : ENDS * n + ENDS]
        copies.append(pltpu.make_async_copy(u.at[rows - 1, q : q + ENDS], to.at[:, :members], sem.at[n, 0]))
        copies.append(pltpu.make_async_copy(w.at[rows - 1, q : q + ENDS], to.at[:, members:deep], sem.at[n, 1]))
    for copy in copies:
        copy.start()
    for copy in copies:
        copy.wait()


def pack_ends(u, w):
    members, cells = u.shape[2:]
    shape = (2 * ENDS, members + w.shape[2], cells)
    return pl.pallas_call(
        pack_ends_kernel,
        out_shape=pltpu.VMEM(shape, u.dtype),
        in_specs=[HBM, HBM],
        out_specs=VMEM,
        scratch_shapes=[pltpu.SemaphoreType.DMA((2, 2))],
        cost_estimate=pl.CostEstimate(flops=0, bytes_accessed=8 * ENDS * shape[1] * cells, transcendentals=0),
        name="pack_ends",
    )(u, w)


def pack_row_kernel(u, w, out, sem):
    rows, cols, members, _ = u.shape
    deep = members + w.shape[2]
    between = slice(ENDS, cols - ENDS)
    copies = [
        pltpu.make_async_copy(u.at[rows - 1, between], out.at[:, :members], sem.at[0]),
        pltpu.make_async_copy(w.at[rows - 1, between], out.at[:, members:deep], sem.at[1]),
    ]
    for copy in copies:
        copy.start()
    for copy in copies:
        copy.wait()


def pack_row(u, w):
    cols, members, cells = u.shape[1:]
    shape = (cols - 2 * ENDS, members + w.shape[2], cells)
    return pl.pallas_call(
        pack_row_kernel,
        out_shape=jax.ShapeDtypeStruct(shape, u.dtype),
        in_specs=[ANY, ANY],
        out_specs=VMEM,
        scratch_shapes=[pltpu.SemaphoreType.DMA((2,))],
        compiler_params=pltpu.CompilerParams(vmem_limit_bytes=GRANT),
        cost_estimate=pl.CostEstimate(flops=0, bytes_accessed=4 * shape[0] * shape[1] * cells, transcendentals=0),
        name="pack_row",
    )(u, w)


def pack_columns_kernel(u, w, live, index, packed, inner_side, outer_side, sem):
    del packed
    rows, cols, members, cells = u.shape
    deep = members + w.shape[2]
    turn = (cols - 1) * even_column().astype(jnp.int32)
    copies = []
    for n, (out, b) in enumerate(((inner_side, turn), (outer_side, cols - 1 - turn))):
        copies.append(pltpu.make_async_copy(u.at[:, b], out.at[:, :members], sem.at[n, 0]))
        copies.append(pltpu.make_async_copy(w.at[:, b], out.at[:, members:deep], sem.at[n, 1]))
    for copy in copies:
        copy.start()
    for a in range(rows):
        lines = jnp.concatenate([live[a], index[a]], 0).astype(jnp.float32)
        blank = jnp.zeros((2 * cols, cells - live.shape[2]), jnp.float32)
        note = jnp.concatenate([lines, blank], 1).astype(jnp.bfloat16)
        inner_side[a, deep:] = note
        outer_side[a, deep:] = note
    for copy in copies:
        copy.wait()


def pack_columns(u, w, live, index, packed):
    rows, cols, members, cells = u.shape
    shape = (rows, members + w.shape[2] + 2 * cols, cells)
    return pl.pallas_call(
        pack_columns_kernel,
        out_shape=(jax.ShapeDtypeStruct(shape, u.dtype),) * 2,
        in_specs=[ANY, ANY, VMEM, VMEM, VMEM],
        out_specs=(VMEM, VMEM),
        scratch_shapes=[pltpu.SemaphoreType.DMA((2, 2))],
        compiler_params=pltpu.CompilerParams(vmem_limit_bytes=GRANT),
        cost_estimate=pl.CostEstimate(flops=0, bytes_accessed=8 * rows * shape[1] * cells, transcendentals=0),
        name="pack_columns",
    )(u, w, live, index, packed)


def body(u, w, live, index, tapers):
    packed = pack_ends(u, w)
    ends = lax.ppermute(packed, "row", forward("row"))
    inner_side, outer_side = pack_columns(u, w, live, index, packed)
    inside = lax.ppermute(inner_side, "col", swaps("col", 0))
    outside = lax.ppermute(outer_side, "col", swaps("col", 1))
    row = lax.ppermute(pack_row(u, w), "row", forward("row"))
    inc = inner(u, w, live, index, tapers, ends)
    inc, inside, outside = lax.optimization_barrier((inc, inside, outside))
    end_back, end_held, to_inside, to_outside, side = edges(ends, u, w, inside, outside, live, index, tapers)
    from_inside = lax.ppermute(to_inside, "col", swaps("col", 0))
    from_outside = lax.ppermute(to_outside, "col", swaps("col", 1))
    back, held = above(row, end_back, u, w, live, index, tapers)
    back = lax.ppermute(back, "row", backward("row"))
    inc, top, low = outer(inc, side, ends, end_held, row, held)
    return finish(inc, top, low, back, from_inside, from_outside)


def solution(mesh):
    return jax.shard_map(
        body,
        mesh=mesh,
        in_specs=(
            P("row", "col", None, None),
            P("row", "col", None, None),
            P("row", "col", None),
            P("row", "col", None),
            P(),
        ),
        out_specs=P("row", "col", None, None),
        check_vma=False,
    )
```

```python
import jax
import jax.numpy as jnp
from jax import lax
from jax.experimental import pallas as pl
from jax.experimental.pallas import tpu as pltpu
from jax.sharding import PartitionSpec as P

MEMBERS = 256
GRANT = 16 << 20
SCALE = 1.0 / (MEMBERS - 1)
TN = (((0,), (0,)), ((), ()))
NT = (((1,), (1,)), ((), ()))
NN = (((1,), (0,)), ((), ()))
VMEM = pl.BlockSpec(memory_space=pltpu.VMEM)
ANY = pl.BlockSpec(memory_space=pl.ANY)
HBM = pl.BlockSpec(memory_space=pltpu.HBM)


def dot(a, b, dims):
    return lax.dot_general(a, b, dims, preferred_element_type=jnp.float32)


def cat(parts, axis):
    return parts[0] if len(parts) == 1 else jnp.concatenate(parts, axis=axis)


def tapered(gram, rho, live):
    factor = live.astype(jnp.float32) * SCALE
    return (rho.astype(jnp.float32) * gram * factor).astype(jnp.bfloat16)


def even_column():
    return lax.rem(lax.axis_index("col"), 2) == 0


def sides(inside, outside):
    even = even_column()
    return (
        lambda *at: jnp.where(even, outside[at], inside[at]),
        lambda *at: jnp.where(even, inside[at], outside[at]),
    )


def inner_kernel(u, w, live, index, tapers, out, sym, held):
    rows, cols, _, cells = u.shape
    for n in range(tapers.shape[0]):
        t = tapers[n].astype(jnp.float32)
        sym[n] = 0.5 * (t + t.T)

    def ahead(a, b, last):
        near = [(4, a, b)]
        if b + 1 < cols:
            near.append((5, a, b + 1))
        if not last:
            for k in (6, 7, 8):
                if 0 <= b + k - 7 < cols:
                    near.append((k, a + 1, b + k - 7))
        return near

    def row(a, last):
        on, which = live[a], index[a]
        for b in range(cols):
            near = ahead(a, b, last)
            gram = dot(u[a, b], cat([u[p, q] for _, p, q in near], 1), TN)
            for n, (k, _, _) in enumerate(near):
                at = which[b, k]
                rho = sym[at] if k == 4 else tapers[at]
                held[b, :, (k - 4) * cells : (k - 3) * cells] = tapered(
                    gram[:, n * cells : (n + 1) * cells], rho, on[b, k]
                )
        for b in range(cols):
            near = ahead(a, b, last)
            total = dot(
                cat([w[p, q] for _, p, q in near], 1),
                cat([held[b, :, (k - 4) * cells : (k - 3) * cells] for k, _, _ in near], 1),
                NT,
            )
            if b > 0:
                total += dot(w[a, b - 1], held[b - 1, :, cells : 2 * cells], NN)
            out[a, b] += total
            if not last:
                back = [(k, b - (k - 7)) for k in (6, 7, 8) if 0 <= b - (k - 7) < cols]
                out[a + 1, b] = dot(
                    cat([w[a, q] for _, q in back], 1),
                    cat([held[q, :, (k - 4) * cells : (k - 3) * cells] for k, q in back], 0),
                    NN,
                )

    out[0] = jnp.zeros_like(out[0])

    @pl.loop(0, rows - 1)
    def _(a):
        row(a, False)

    row(rows - 1, True)


def inner(u, w, live, index, tapers):
    rows, cols, members, cells = u.shape
    columns = w.shape[2]
    pairs = 5 * rows * cols
    return pl.pallas_call(
        inner_kernel,
        out_shape=jax.ShapeDtypeStruct((rows, cols, columns, cells), jnp.float32),
        in_specs=[VMEM] * 5,
        out_specs=VMEM,
        scratch_shapes=[
            pltpu.VMEM(tapers.shape, jnp.float32),
            pltpu.VMEM((cols, cells, 5 * cells), jnp.bfloat16),
        ],
        compiler_params=pltpu.CompilerParams(vmem_limit_bytes=GRANT),
        cost_estimate=pl.CostEstimate(
            flops=2 * pairs * cells * cells * (members + 2 * columns),
            bytes_accessed=4 << 20,
            transcendentals=0,
        ),
        name="inner",
    )(u, w, live, index, tapers)


def above_kernel(s, u, w, inside, outside, live, index, tapers, back, held, to_inside):
    cols, members, cells = u.shape[1:]
    deep = members + w.shape[2]
    last = cols - 1
    left, right = sides(inside, outside)
    on, which = live[0], index[0]
    beyond = {}
    for q, near, k, line in ((-1, left, 2, last), (cols, right, 0, 0)):
        note = near(0, slice(deep, None)).astype(jnp.int32)
        beyond[q] = near, note[line, k], note[cols + line, k]
    sources = []
    for c in range(cols):
        grams, weights, lives, rhos = [], [], [], []
        for k in (6, 7, 8):
            q = c + k - 7
            if q in beyond:
                near, lively, at = beyond[q]
                grams.append(near(0, slice(0, members)))
                weights.append(near(0, slice(members, deep)))
            else:
                lively, at = on[q, 8 - k], which[q, 8 - k]
                grams.append(u[0, q])
                weights.append(w[0, q])
            lives.append(lively)
            rhos.append(tapers[at])
        gram = dot(s[c, :members], cat(grams, 1), TN)
        held[c] = cat([tapered(gram[:, m * cells : (m + 1) * cells], rhos[m], lives[m]) for m in range(3)], 1)
        sources.append(cat(weights, 1))
    for c in range(cols):
        back[c] = dot(sources[c], held[c], NT).astype(jnp.bfloat16)
    even = even_column()
    weight = jnp.where(even, s[last, members:deep], s[0, members:deep])
    to_inside[...] = dot(weight, jnp.where(even, held[last, :, 2 * cells :], held[0, :, :cells]), NN)


def above(s, u, w, inside, outside, live, index, tapers):
    cols, members, cells = u.shape[1:]
    columns = w.shape[2]
    return pl.pallas_call(
        above_kernel,
        out_shape=(
            jax.ShapeDtypeStruct((cols, columns, cells), jnp.bfloat16),
            jax.ShapeDtypeStruct((cols, cells, 3 * cells), jnp.bfloat16),
            jax.ShapeDtypeStruct((columns, cells), jnp.float32),
        ),
        in_specs=[VMEM] * 8,
        out_specs=(VMEM,) * 3,
        compiler_params=pltpu.CompilerParams(vmem_limit_bytes=GRANT),
        cost_estimate=pl.CostEstimate(
            flops=2 * 3 * cols * cells * cells * (members + columns),
            bytes_accessed=2 << 20,
            transcendentals=0,
        ),
        name="above",
    )(s, u, w, inside, outside, live, index, tapers)


def outer_kernel(inc, held, s, corner, u, w, inside, outside, live, index, tapers, out, top, low):
    rows, cols, members, cells = u.shape
    deep = members + w.shape[2]
    last = cols - 1
    left, right = sides(inside, outside)
    even = even_column()
    on = [live[a] for a in range(rows)]
    which = [index[a] for a in range(rows)]
    total = {}

    def add(a, q, value):
        total[a, q] = total[a, q] + value if (a, q) in total else value

    for q in range(cols):
        back = [(k, q - (k - 7)) for k in (6, 7, 8) if 0 <= q - (k - 7) < cols]
        blocks = [held[c, :, (k - 6) * cells : (k - 5) * cells] for k, c in back]
        add(0, q, dot(cat([s[c, members:deep] for _, c in back], 1), cat(blocks, 0), NN))
    gram = dot(corner[1, :members], jnp.where(even, u[0, 0], u[0, last]), TN)
    at = jnp.where(even, which[0][0, 0], which[0][last, 2])
    block = tapered(gram, tapers[at], jnp.where(even, on[0][0, 0], on[0][last, 2]))
    far = dot(corner[1, members:deep], block, NN)
    blank = jnp.zeros_like(far)
    add(0, 0, jnp.where(even, far, blank))
    add(0, last, jnp.where(even, blank, far))

    for a in range(rows):
        near = [(5, a)] + ([(8, a + 1)] if a + 1 < rows else [])
        gram = dot(left(a, slice(0, members)), cat([u[p, 0] for _, p in near], 1), TN)
        blocks = cat(
            [
                tapered(gram[:, n * cells : (n + 1) * cells], tapers[which[p][0, 8 - k]], on[p][0, 8 - k])
                for n, (k, p) in enumerate(near)
            ],
            1,
        )
        both = dot(left(a, slice(members, deep)), blocks, NN)
        for n, (_, p) in enumerate(near):
            add(p, 0, both[:, n * cells : (n + 1) * cells])
        gram = dot(u[a, last], cat([right(p, slice(0, members)) for _, p in near], 1), TN)
        blocks = cat(
            [
                tapered(gram[:, n * cells : (n + 1) * cells], tapers[which[a][last, k]], on[a][last, k])
                for n, (k, _) in enumerate(near)
            ],
            1,
        )
        add(a, last, dot(cat([right(p, slice(members, deep)) for _, p in near], 1), blocks, NT))
        if a + 1 < rows:
            gram = dot(u[a, 0], left(a + 1, slice(0, members)), TN)
            block = tapered(gram, tapers[which[a][0, 6]], on[a][0, 6])
            add(a, 0, dot(left(a + 1, slice(members, deep)), block, NT))
            gram = dot(right(a, slice(0, members)), u[a + 1, last], TN)
            block = tapered(gram, tapers[which[a + 1][last, 2]], on[a + 1][last, 2])
            add(a + 1, last, dot(right(a, slice(members, deep)), block, NN))

    for a in range(rows):
        for q in range(cols):
            value = inc[a, q] + total[a, q] if (a, q) in total else inc[a, q]
            out[a, q] = value
            if a == 0 and q in (0, last):
                top[q // last] = value
            if a == rows - 1:
                low[q] = value


def outer(inc, held, s, corner, u, w, inside, outside, live, index, tapers):
    rows, cols, members, cells = u.shape
    columns = w.shape[2]
    return pl.pallas_call(
        outer_kernel,
        out_shape=(
            jax.ShapeDtypeStruct(inc.shape, inc.dtype),
            jax.ShapeDtypeStruct((2, columns, cells), inc.dtype),
            jax.ShapeDtypeStruct(inc.shape[1:], inc.dtype),
        ),
        in_specs=[VMEM] * 11,
        out_specs=(VMEM,) * 3,
        compiler_params=pltpu.CompilerParams(vmem_limit_bytes=GRANT),
        cost_estimate=pl.CostEstimate(
            flops=2 * (6 * rows + 3 * cols) * cells * cells * (members + columns),
            bytes_accessed=4 << 20,
            transcendentals=0,
        ),
        name="outer",
    )(inc, held, s, corner, u, w, inside, outside, live, index, tapers)


def finish_kernel(inc, top, low, back, from_inside, out, end, total, sem):
    del inc
    rows, cols = out.shape[:2]
    half = cols // 2
    side = even_column().astype(jnp.int32)
    copies = []
    for n, part in enumerate((slice(0, half), slice(half, cols))):
        total[part] = low[part] + back[part].astype(jnp.float32)
        copies.append(pltpu.make_async_copy(total.at[part], out.at[rows - 1, part], sem.at[n]))
        copies[-1].start()
    end[...] = top[side] + from_inside[...]
    copies.append(pltpu.make_async_copy(end, out.at[0, side * (cols - 1)], sem.at[2]))
    copies[-1].start()
    for copy in copies:
        copy.wait()


def finish(inc, top, low, back, from_inside):
    return pl.pallas_call(
        finish_kernel,
        out_shape=jax.ShapeDtypeStruct(inc.shape, inc.dtype),
        in_specs=[ANY] + [VMEM] * 4,
        out_specs=ANY,
        scratch_shapes=[
            pltpu.VMEM(top.shape[1:], top.dtype),
            pltpu.VMEM(low.shape, low.dtype),
            pltpu.SemaphoreType.DMA((3,)),
        ],
        input_output_aliases={0: 0},
        compiler_params=pltpu.CompilerParams(vmem_limit_bytes=GRANT),
        cost_estimate=pl.CostEstimate(flops=low.size, bytes_accessed=10 * low.size, transcendentals=0),
        name="finish",
    )(inc, top, low, back, from_inside)


def forward(axis):
    return [(i, i + 1) for i in range(lax.axis_size(axis) - 1)]


def swaps(axis, start):
    pairs = [(i, i + 1) for i in range(start, lax.axis_size(axis) - 1, 2)]
    return pairs + [(b, a) for a, b in pairs]


def backward(axis):
    return [(i + 1, i) for i in range(lax.axis_size(axis) - 1)]


def pack_row_kernel(u, w, out, sem):
    rows, _, members, _ = u.shape
    deep = members + w.shape[2]
    copies = [
        pltpu.make_async_copy(u.at[rows - 1], out.at[:, :members], sem.at[0]),
        pltpu.make_async_copy(w.at[rows - 1], out.at[:, members:deep], sem.at[1]),
    ]
    for copy in copies:
        copy.start()
    for copy in copies:
        copy.wait()


def pack_row(u, w):
    cols, members, cells = u.shape[1:]
    shape = (cols, members + w.shape[2], cells)
    return pl.pallas_call(
        pack_row_kernel,
        out_shape=pltpu.VMEM(shape, u.dtype),
        in_specs=[HBM, HBM],
        out_specs=VMEM,
        scratch_shapes=[pltpu.SemaphoreType.DMA((2,))],
        cost_estimate=pl.CostEstimate(flops=0, bytes_accessed=4 * cols * shape[1] * cells, transcendentals=0),
        name="pack_row",
    )(u, w)


def pack_columns_kernel(u, w, live, index, packed, inner_side, outer_side, sem):
    del packed
    rows, cols, members, cells = u.shape
    deep = members + w.shape[2]
    turn = (cols - 1) * even_column().astype(jnp.int32)
    copies = []
    for n, (out, b) in enumerate(((inner_side, turn), (outer_side, cols - 1 - turn))):
        copies.append(pltpu.make_async_copy(u.at[:, b], out.at[:, :members], sem.at[n, 0]))
        copies.append(pltpu.make_async_copy(w.at[:, b], out.at[:, members:deep], sem.at[n, 1]))
    for copy in copies:
        copy.start()
    for a in range(rows):
        lines = jnp.concatenate([live[a], index[a]], 0).astype(jnp.float32)
        blank = jnp.zeros((2 * cols, cells - live.shape[2]), jnp.float32)
        note = jnp.concatenate([lines, blank], 1).astype(jnp.bfloat16)
        inner_side[a, deep:] = note
        outer_side[a, deep:] = note
    for copy in copies:
        copy.wait()


def pack_columns(u, w, live, index, packed):
    rows, cols, members, cells = u.shape
    shape = (rows, members + w.shape[2] + 2 * cols, cells)
    return pl.pallas_call(
        pack_columns_kernel,
        out_shape=(jax.ShapeDtypeStruct(shape, u.dtype),) * 2,
        in_specs=[ANY, ANY, VMEM, VMEM, VMEM],
        out_specs=(VMEM, VMEM),
        scratch_shapes=[pltpu.SemaphoreType.DMA((2, 2))],
        compiler_params=pltpu.CompilerParams(vmem_limit_bytes=GRANT),
        cost_estimate=pl.CostEstimate(flops=0, bytes_accessed=8 * rows * shape[1] * cells, transcendentals=0),
        name="pack_columns",
    )(u, w, live, index, packed)


def inward(row, col):
    wide = lax.axis_size(col)
    return [
        (r * wide + c, (r + 1) * wide + c) for r in range(lax.axis_size(row) - 1) for c in range(1, wide - 1)
    ]


def body(u, w, live, index, tapers):
    rows = u.shape[0]
    packed = pack_row(u, w)
    s = lax.ppermute(packed, "row", forward("row"))
    inner_side, outer_side = pack_columns(u, w, live, index, packed)
    inside = lax.ppermute(inner_side, "col", swaps("col", 0))
    outside = lax.ppermute(outer_side, "col", swaps("col", 1))
    inc, inside, outside = lax.optimization_barrier((inner(u, w, live, index, tapers), inside, outside))
    corner = lax.ppermute(outside[rows - 2 :], ("row", "col"), inward("row", "col"))
    back, held, to_inside = above(s, u, w, inside, outside, live, index, tapers)
    back = lax.ppermute(back, "row", backward("row"))
    from_inside = lax.ppermute(to_inside, "col", swaps("col", 0))
    inc, top, low = outer(inc, held, s, corner, u, w, inside, outside, live, index, tapers)
    return finish(inc, top, low, back, from_inside)


def solution(mesh):
    return jax.shard_map(
        body,
        mesh=mesh,
        in_specs=(
            P("row", "col", None, None),
            P("row", "col", None, None),
            P("row", "col", None),
            P("row", "col", None),
            P(),
        ),
        out_specs=P("row", "col", None, None),
        check_vma=False,
    )
```

```python
import jax
import jax.numpy as jnp
from jax import lax
from jax.experimental import pallas as pl
from jax.experimental.pallas import tpu as pltpu
from jax.sharding import PartitionSpec as P

MEMBERS = 256
GRANT = 16 << 20
SCALE = 1.0 / (MEMBERS - 1)
TN = (((0,), (0,)), ((), ()))
NT = (((1,), (1,)), ((), ()))
NN = (((1,), (0,)), ((), ()))
VMEM = pl.BlockSpec(memory_space=pltpu.VMEM)
ANY = pl.BlockSpec(memory_space=pl.ANY)
HBM = pl.BlockSpec(memory_space=pltpu.HBM)


def dot(a, b, dims):
    return lax.dot_general(a, b, dims, preferred_element_type=jnp.float32)


def cat(parts, axis):
    return parts[0] if len(parts) == 1 else jnp.concatenate(parts, axis=axis)


def tapered(gram, rho, live):
    factor = live.astype(jnp.float32) * SCALE
    return (rho.astype(jnp.float32) * gram * factor).astype(jnp.bfloat16)


def even_column():
    return lax.rem(lax.axis_index("col"), 2) == 0


def sides(inside, outside):
    even = even_column()
    return (
        lambda *at: jnp.where(even, outside[at], inside[at]),
        lambda *at: jnp.where(even, inside[at], outside[at]),
    )


def inner_kernel(u, w, live, index, tapers, out, sym, held):
    rows, cols, _, cells = u.shape
    for n in range(tapers.shape[0]):
        t = tapers[n].astype(jnp.float32)
        sym[n] = 0.5 * (t + t.T)

    def ahead(a, b, last):
        near = [(4, a, b)]
        if b + 1 < cols:
            near.append((5, a, b + 1))
        if not last:
            for k in (6, 7, 8):
                if 0 <= b + k - 7 < cols:
                    near.append((k, a + 1, b + k - 7))
        return near

    def row(a, last):
        on, which = live[a], index[a]
        for b in range(cols):
            near = ahead(a, b, last)
            gram = dot(u[a, b], cat([u[p, q] for _, p, q in near], 1), TN)
            for n, (k, _, _) in enumerate(near):
                at = which[b, k]
                rho = sym[at] if k == 4 else tapers[at]
                held[b, :, (k - 4) * cells : (k - 3) * cells] = tapered(
                    gram[:, n * cells : (n + 1) * cells], rho, on[b, k]
                )
        for b in range(cols):
            near = ahead(a, b, last)
            total = dot(
                cat([w[p, q] for _, p, q in near], 1),
                cat([held[b, :, (k - 4) * cells : (k - 3) * cells] for k, _, _ in near], 1),
                NT,
            )
            if b > 0:
                total += dot(w[a, b - 1], held[b - 1, :, cells : 2 * cells], NN)
            out[a, b] += total
            if not last:
                back = [(k, b - (k - 7)) for k in (6, 7, 8) if 0 <= b - (k - 7) < cols]
                out[a + 1, b] = dot(
                    cat([w[a, q] for _, q in back], 1),
                    cat([held[q, :, (k - 4) * cells : (k - 3) * cells] for k, q in back], 0),
                    NN,
                )

    out[0] = jnp.zeros_like(out[0])

    @pl.loop(0, rows - 1)
    def _(a):
        row(a, False)

    row(rows - 1, True)


def inner(u, w, live, index, tapers):
    rows, cols, members, cells = u.shape
    columns = w.shape[2]
    pairs = 5 * rows * cols
    return pl.pallas_call(
        inner_kernel,
        out_shape=jax.ShapeDtypeStruct((rows, cols, columns, cells), jnp.float32),
        in_specs=[VMEM] * 5,
        out_specs=VMEM,
        scratch_shapes=[
            pltpu.VMEM(tapers.shape, jnp.float32),
            pltpu.VMEM((cols, cells, 5 * cells), jnp.bfloat16),
        ],
        compiler_params=pltpu.CompilerParams(vmem_limit_bytes=GRANT),
        cost_estimate=pl.CostEstimate(
            flops=2 * pairs * cells * cells * (members + 2 * columns),
            bytes_accessed=4 << 20,
            transcendentals=0,
        ),
        name="inner",
    )(u, w, live, index, tapers)


def above_kernel(s, u, w, inside, outside, live, index, tapers, back, held, to_inside):
    cols, members, cells = u.shape[1:]
    deep = members + w.shape[2]
    last = cols - 1
    left, right = sides(inside, outside)
    on, which = live[0], index[0]
    beyond = {}
    for q, near, k, line in ((-1, left, 2, last), (cols, right, 0, 0)):
        note = near(0, slice(deep, None)).astype(jnp.int32)
        beyond[q] = near, note[line, k], note[cols + line, k]
    sources = []
    for c in range(cols):
        grams, weights, lives, rhos = [], [], [], []
        for k in (6, 7, 8):
            q = c + k - 7
            if q in beyond:
                near, lively, at = beyond[q]
                grams.append(near(0, slice(0, members)))
                weights.append(near(0, slice(members, deep)))
            else:
                lively, at = on[q, 8 - k], which[q, 8 - k]
                grams.append(u[0, q])
                weights.append(w[0, q])
            lives.append(lively)
            rhos.append(tapers[at])
        gram = dot(s[c * members : (c + 1) * members], cat(grams, 1), TN)
        held[c] = cat([tapered(gram[:, m * cells : (m + 1) * cells], rhos[m], lives[m]) for m in range(3)], 1)
        sources.append(cat(weights, 1))
    for c in range(cols):
        back[c] = dot(sources[c], held[c], NT).astype(jnp.bfloat16)
    even = even_column()
    to_inside[...] = dot(s[cols * members :], jnp.where(even, held[last, :, 2 * cells :], held[0, :, :cells]), NN)


def above(s, u, w, inside, outside, live, index, tapers):
    cols, members, cells = u.shape[1:]
    columns = w.shape[2]
    return pl.pallas_call(
        above_kernel,
        out_shape=(
            jax.ShapeDtypeStruct((cols, columns, cells), jnp.bfloat16),
            jax.ShapeDtypeStruct((cols, cells, 3 * cells), jnp.bfloat16),
            jax.ShapeDtypeStruct((columns, cells), jnp.float32),
        ),
        in_specs=[VMEM] * 8,
        out_specs=(VMEM,) * 3,
        compiler_params=pltpu.CompilerParams(vmem_limit_bytes=GRANT),
        cost_estimate=pl.CostEstimate(
            flops=2 * 3 * cols * cells * cells * (members + columns),
            bytes_accessed=2 << 20,
            transcendentals=0,
        ),
        name="above",
    )(s, u, w, inside, outside, live, index, tapers)


def columns_kernel(u, w, inside, outside, live, index, tapers, side):
    rows, cols, members, cells = u.shape
    deep = members + w.shape[2]
    last = cols - 1
    left, right = sides(inside, outside)
    on = [live[a] for a in range(rows)]
    which = [index[a] for a in range(rows)]
    total = {}

    def add(a, q, value):
        total[a, q] = total[a, q] + value if (a, q) in total else value

    for a in range(rows):
        near = [(5, a)] + ([(8, a + 1)] if a + 1 < rows else [])
        gram = dot(left(a, slice(0, members)), cat([u[p, 0] for _, p in near], 1), TN)
        blocks = cat(
            [
                tapered(gram[:, n * cells : (n + 1) * cells], tapers[which[p][0, 8 - k]], on[p][0, 8 - k])
                for n, (k, p) in enumerate(near)
            ],
            1,
        )
        both = dot(left(a, slice(members, deep)), blocks, NN)
        for n, (_, p) in enumerate(near):
            add(p, 0, both[:, n * cells : (n + 1) * cells])
        gram = dot(u[a, last], cat([right(p, slice(0, members)) for _, p in near], 1), TN)
        blocks = cat(
            [
                tapered(gram[:, n * cells : (n + 1) * cells], tapers[which[a][last, k]], on[a][last, k])
                for n, (k, _) in enumerate(near)
            ],
            1,
        )
        add(a, last, dot(cat([right(p, slice(members, deep)) for _, p in near], 1), blocks, NT))
        if a + 1 < rows:
            gram = dot(u[a, 0], left(a + 1, slice(0, members)), TN)
            block = tapered(gram, tapers[which[a][0, 6]], on[a][0, 6])
            add(a, 0, dot(left(a + 1, slice(members, deep)), block, NT))
            gram = dot(right(a, slice(0, members)), u[a + 1, last], TN)
            block = tapered(gram, tapers[which[a + 1][last, 2]], on[a + 1][last, 2])
            add(a + 1, last, dot(right(a, slice(members, deep)), block, NN))

    for a in range(rows):
        side[0, a] = total[a, 0]
        side[1, a] = total[a, last]


def columns(u, w, inside, outside, live, index, tapers):
    rows, _, members, cells = u.shape
    width = w.shape[2]
    return pl.pallas_call(
        columns_kernel,
        out_shape=jax.ShapeDtypeStruct((2, rows, width, cells), jnp.float32),
        in_specs=[VMEM] * 7,
        out_specs=VMEM,
        compiler_params=pltpu.CompilerParams(vmem_limit_bytes=GRANT),
        cost_estimate=pl.CostEstimate(
            flops=12 * rows * cells * cells * (members + width), bytes_accessed=2 << 20, transcendentals=0
        ),
        name="columns",
    )(u, w, inside, outside, live, index, tapers)


def outer_kernel(inc, side, held, rest, u, live, index, tapers, out, top, low):
    rows, cols, members, cells = u.shape
    width = inc.shape[2]
    last = cols - 1
    even = even_column()
    on, which = live[0], index[0]
    start = cols * width
    gram = dot(rest[start : start + members], jnp.where(even, u[0, 0], u[0, last]), TN)
    at = jnp.where(even, which[0, 0], which[last, 2])
    block = tapered(gram, tapers[at], jnp.where(even, on[0, 0], on[last, 2]))
    far = dot(rest[start + members :], block, NN)
    blank = jnp.zeros_like(far)
    for q in range(cols):
        back = [(k, q - (k - 7)) for k in (6, 7, 8) if 0 <= q - (k - 7) < cols]
        blocks = [held[c, :, (k - 6) * cells : (k - 5) * cells] for k, c in back]
        value = inc[0, q] + dot(cat([rest[c * width : (c + 1) * width] for _, c in back], 1), cat(blocks, 0), NN)
        if q in (0, last):
            value += side[q // last, 0]
            value += jnp.where(even, far, blank) if q == 0 else jnp.where(even, blank, far)
            top[q // last] = value
        out[0, q] = value
    for a in range(1, rows):
        for q in range(cols):
            value = inc[a, q] + side[q // last, a] if q in (0, last) else inc[a, q]
            out[a, q] = value
            if a == rows - 1:
                low[q] = value


def outer(inc, side, held, rest, u, live, index, tapers):
    rows, cols, width, cells = inc.shape
    return pl.pallas_call(
        outer_kernel,
        out_shape=(
            jax.ShapeDtypeStruct(inc.shape, inc.dtype),
            jax.ShapeDtypeStruct((2, width, cells), inc.dtype),
            jax.ShapeDtypeStruct(inc.shape[1:], inc.dtype),
        ),
        in_specs=[VMEM] * 8,
        out_specs=(VMEM,) * 3,
        compiler_params=pltpu.CompilerParams(vmem_limit_bytes=GRANT),
        cost_estimate=pl.CostEstimate(flops=6 * cols * cells * cells * width, bytes_accessed=4 << 20, transcendentals=0),
        name="outer",
    )(inc, side, held, rest, u, live, index, tapers)


def finish_kernel(inc, top, low, back, from_inside, out, end, total, sem):
    del inc
    rows, cols = out.shape[:2]
    half = cols // 2
    side = even_column().astype(jnp.int32)
    copies = []
    for n, part in enumerate((slice(0, half), slice(half, cols))):
        total[part] = low[part] + back[part].astype(jnp.float32)
        copies.append(pltpu.make_async_copy(total.at[part], out.at[rows - 1, part], sem.at[n]))
        copies[-1].start()
    end[...] = top[side] + from_inside[...]
    copies.append(pltpu.make_async_copy(end, out.at[0, side * (cols - 1)], sem.at[2]))
    copies[-1].start()
    for copy in copies:
        copy.wait()


def finish(inc, top, low, back, from_inside):
    return pl.pallas_call(
        finish_kernel,
        out_shape=jax.ShapeDtypeStruct(inc.shape, inc.dtype),
        in_specs=[ANY] + [VMEM] * 4,
        out_specs=ANY,
        scratch_shapes=[
            pltpu.VMEM(top.shape[1:], top.dtype),
            pltpu.VMEM(low.shape, low.dtype),
            pltpu.SemaphoreType.DMA((3,)),
        ],
        input_output_aliases={0: 0},
        compiler_params=pltpu.CompilerParams(vmem_limit_bytes=GRANT),
        cost_estimate=pl.CostEstimate(flops=low.size, bytes_accessed=10 * low.size, transcendentals=0),
        name="finish",
    )(inc, top, low, back, from_inside)


def forward(axis):
    return [(i, i + 1) for i in range(lax.axis_size(axis) - 1)]


def swaps(axis, start):
    pairs = [(i, i + 1) for i in range(start, lax.axis_size(axis) - 1, 2)]
    return pairs + [(b, a) for a, b in pairs]


def backward(axis):
    return [(i + 1, i) for i in range(lax.axis_size(axis) - 1)]


def pack_row_kernel(u, w, out, sem):
    rows, cols, members, _ = u.shape
    beside = (cols - 1) * even_column().astype(jnp.int32)
    copies = [
        pltpu.make_async_copy(u.at[rows - 1, q], out.at[q * members : (q + 1) * members], sem.at[q])
        for q in range(cols)
    ]
    copies.append(pltpu.make_async_copy(w.at[rows - 1, beside], out.at[cols * members :], sem.at[cols]))
    for copy in copies:
        copy.start()
    for copy in copies:
        copy.wait()


def pack_row(u, w):
    _, cols, members, cells = u.shape
    shape = (cols * members + w.shape[2], cells)
    return pl.pallas_call(
        pack_row_kernel,
        out_shape=pltpu.VMEM(shape, u.dtype),
        in_specs=[HBM, HBM],
        out_specs=VMEM,
        scratch_shapes=[pltpu.SemaphoreType.DMA((cols + 1,))],
        cost_estimate=pl.CostEstimate(flops=0, bytes_accessed=4 * shape[0] * cells, transcendentals=0),
        name="pack_row",
    )(u, w)


def pack_rest_kernel(w, outside, out):
    rows, cols, width, _ = w.shape
    for q in range(cols):
        out[q * width : (q + 1) * width] = w[rows - 1, q]
    deep = out.shape[0] - cols * width
    out[cols * width :] = outside[rows - 1, :deep]


def pack_rest(w, outside, members):
    _, cols, width, cells = w.shape
    return pl.pallas_call(
        pack_rest_kernel,
        out_shape=jax.ShapeDtypeStruct((cols * width + members + width, cells), w.dtype),
        in_specs=[VMEM, VMEM],
        out_specs=VMEM,
        compiler_params=pltpu.CompilerParams(vmem_limit_bytes=GRANT),
        cost_estimate=pl.CostEstimate(flops=0, bytes_accessed=8 * cols * width * cells, transcendentals=0),
        name="pack_rest",
    )(w, outside)


def pack_columns_kernel(u, w, live, index, packed, inner_side, outer_side, sem):
    del packed
    rows, cols, members, cells = u.shape
    deep = members + w.shape[2]
    turn = (cols - 1) * even_column().astype(jnp.int32)
    copies = []
    for n, (out, b) in enumerate(((inner_side, turn), (outer_side, cols - 1 - turn))):
        copies.append(pltpu.make_async_copy(u.at[:, b], out.at[:, :members], sem.at[n, 0]))
        copies.append(pltpu.make_async_copy(w.at[:, b], out.at[:, members:deep], sem.at[n, 1]))
    for copy in copies:
        copy.start()
    for a in range(rows):
        lines = jnp.concatenate([live[a], index[a]], 0).astype(jnp.float32)
        blank = jnp.zeros((2 * cols, cells - live.shape[2]), jnp.float32)
        note = jnp.concatenate([lines, blank], 1).astype(jnp.bfloat16)
        inner_side[a, deep:] = note
        outer_side[a, deep:] = note
    for copy in copies:
        copy.wait()


def pack_columns(u, w, live, index, packed):
    rows, cols, members, cells = u.shape
    shape = (rows, members + w.shape[2] + 2 * cols, cells)
    return pl.pallas_call(
        pack_columns_kernel,
        out_shape=(jax.ShapeDtypeStruct(shape, u.dtype),) * 2,
        in_specs=[ANY, ANY, VMEM, VMEM, VMEM],
        out_specs=(VMEM, VMEM),
        scratch_shapes=[pltpu.SemaphoreType.DMA((2, 2))],
        compiler_params=pltpu.CompilerParams(vmem_limit_bytes=GRANT),
        cost_estimate=pl.CostEstimate(flops=0, bytes_accessed=8 * rows * shape[1] * cells, transcendentals=0),
        name="pack_columns",
    )(u, w, live, index, packed)


def body(u, w, live, index, tapers):
    packed = pack_row(u, w)
    s = lax.ppermute(packed, "row", forward("row"))
    inner_side, outer_side = pack_columns(u, w, live, index, packed)
    inside = lax.ppermute(inner_side, "col", swaps("col", 0))
    outside = lax.ppermute(outer_side, "col", swaps("col", 1))
    inc, inside, outside = lax.optimization_barrier((inner(u, w, live, index, tapers), inside, outside))
    rest = lax.ppermute(pack_rest(w, outside, u.shape[2]), "row", forward("row"))
    back, held, to_inside = above(s, u, w, inside, outside, live, index, tapers)
    back = lax.ppermute(back, "row", backward("row"))
    from_inside = lax.ppermute(to_inside, "col", swaps("col", 0))
    side = columns(u, w, inside, outside, live, index, tapers)
    inc, top, low = outer(inc, side, held, rest, u, live, index, tapers)
    return finish(inc, top, low, back, from_inside)


def solution(mesh):
    return jax.shard_map(
        body,
        mesh=mesh,
        in_specs=(
            P("row", "col", None, None),
            P("row", "col", None, None),
            P("row", "col", None),
            P("row", "col", None),
            P(),
        ),
        out_specs=P("row", "col", None, None),
        check_vma=False,
    )
```

```python
import jax
import jax.numpy as jnp
from jax import lax
from jax.experimental import pallas as pl
from jax.experimental.pallas import tpu as pltpu
from jax.sharding import PartitionSpec as P

MEMBERS = 256
GRANT = 16 << 20
WIDE = 52 << 20
SCALE = 1.0 / (MEMBERS - 1)
TN = (((0,), (0,)), ((), ()))
NT = (((1,), (1,)), ((), ()))
NN = (((1,), (0,)), ((), ()))
VMEM = pl.BlockSpec(memory_space=pltpu.VMEM)
ANY = pl.BlockSpec(memory_space=pl.ANY)
HBM = pl.BlockSpec(memory_space=pltpu.HBM)


def dot(a, b, dims):
    return lax.dot_general(a, b, dims, preferred_element_type=jnp.float32)


def cat(parts, axis):
    return parts[0] if len(parts) == 1 else jnp.concatenate(parts, axis=axis)


def tapered(gram, rho, live):
    factor = live.astype(jnp.float32) * SCALE
    return (rho.astype(jnp.float32) * gram * factor).astype(jnp.bfloat16)


def even_column():
    return lax.rem(lax.axis_index("col"), 2) == 0


def sides(inside, outside):
    even = even_column()
    return (
        lambda *at: jnp.where(even, outside[at], inside[at]),
        lambda *at: jnp.where(even, inside[at], outside[at]),
    )


def inner_kernel(u, w, live, index, tapers, out, sym, held):
    rows, cols, _, cells = u.shape
    for n in range(tapers.shape[0]):
        t = tapers[n].astype(jnp.float32)
        sym[n] = 0.5 * (t + t.T)

    def ahead(a, b, last):
        near = [(4, a, b)]
        if b + 1 < cols:
            near.append((5, a, b + 1))
        if not last:
            for k in (6, 7, 8):
                if 0 <= b + k - 7 < cols:
                    near.append((k, a + 1, b + k - 7))
        return near

    def row(a, last):
        on, which = live[a], index[a]
        for b in range(cols):
            near = ahead(a, b, last)
            gram = dot(u[a, b], cat([u[p, q] for _, p, q in near], 1), TN)
            for n, (k, _, _) in enumerate(near):
                at = which[b, k]
                rho = sym[at] if k == 4 else tapers[at]
                held[b, :, (k - 4) * cells : (k - 3) * cells] = tapered(
                    gram[:, n * cells : (n + 1) * cells], rho, on[b, k]
                )
        for b in range(cols):
            near = ahead(a, b, last)
            total = dot(
                cat([w[p, q] for _, p, q in near], 1),
                cat([held[b, :, (k - 4) * cells : (k - 3) * cells] for k, _, _ in near], 1),
                NT,
            )
            if b > 0:
                total += dot(w[a, b - 1], held[b - 1, :, cells : 2 * cells], NN)
            out[a, b] += total
            if not last:
                back = [(k, b - (k - 7)) for k in (6, 7, 8) if 0 <= b - (k - 7) < cols]
                out[a + 1, b] = dot(
                    cat([w[a, q] for _, q in back], 1),
                    cat([held[q, :, (k - 4) * cells : (k - 3) * cells] for k, q in back], 0),
                    NN,
                )

    out[0] = jnp.zeros_like(out[0])

    @pl.loop(0, rows - 1)
    def _(a):
        row(a, False)

    row(rows - 1, True)


def inner(u, w, live, index, tapers):
    rows, cols, members, cells = u.shape
    columns = w.shape[2]
    pairs = 5 * rows * cols
    return pl.pallas_call(
        inner_kernel,
        out_shape=jax.ShapeDtypeStruct((rows, cols, columns, cells), jnp.float32),
        in_specs=[VMEM] * 5,
        out_specs=VMEM,
        scratch_shapes=[
            pltpu.VMEM(tapers.shape, jnp.float32),
            pltpu.VMEM((cols, cells, 5 * cells), jnp.bfloat16),
        ],
        compiler_params=pltpu.CompilerParams(vmem_limit_bytes=GRANT),
        cost_estimate=pl.CostEstimate(
            flops=2 * pairs * cells * cells * (members + 2 * columns),
            bytes_accessed=4 << 20,
            transcendentals=0,
        ),
        name="inner",
    )(u, w, live, index, tapers)


def above_kernel(s, u, w, inside, outside, live, index, tapers, back, held, to_inside, tail):
    cols, members, cells = u.shape[1:]
    deep = members + w.shape[2]
    last = cols - 1
    left, right = sides(inside, outside)
    on, which = live[0], index[0]
    beyond = {}
    for q, near, k, line in ((-1, left, 2, last), (cols, right, 0, 0)):
        note = near(0, slice(deep, None)).astype(jnp.int32)
        beyond[q] = near, note[line, k], note[cols + line, k]
    sources = []
    for c in range(cols):
        grams, weights, lives, rhos = [], [], [], []
        for k in (6, 7, 8):
            q = c + k - 7
            if q in beyond:
                near, lively, at = beyond[q]
                grams.append(near(0, slice(0, members)))
                weights.append(near(0, slice(members, deep)))
            else:
                lively, at = on[q, 8 - k], which[q, 8 - k]
                grams.append(u[0, q])
                weights.append(w[0, q])
            lives.append(lively)
            rhos.append(tapers[at])
        gram = dot(s[c * members : (c + 1) * members], cat(grams, 1), TN)
        held[c] = cat([tapered(gram[:, m * cells : (m + 1) * cells], rhos[m], lives[m]) for m in range(3)], 1)
        sources.append(cat(weights, 1))
    for c in range(cols):
        back[c] = dot(sources[c], held[c], NT).astype(jnp.bfloat16)
    even = even_column()
    tail[...] = s[cols * members :]
    to_inside[...] = dot(s[cols * members :], jnp.where(even, held[last, :, 2 * cells :], held[0, :, :cells]), NN)


def above(s, u, w, inside, outside, live, index, tapers):
    cols, members, cells = u.shape[1:]
    columns = w.shape[2]
    return pl.pallas_call(
        above_kernel,
        out_shape=(
            jax.ShapeDtypeStruct((cols, columns, cells), jnp.bfloat16),
            jax.ShapeDtypeStruct((cols, cells, 3 * cells), jnp.bfloat16),
            jax.ShapeDtypeStruct((columns, cells), jnp.float32),
            jax.ShapeDtypeStruct((columns, cells), jnp.bfloat16),
        ),
        in_specs=[VMEM] * 8,
        out_specs=(VMEM,) * 4,
        compiler_params=pltpu.CompilerParams(vmem_limit_bytes=GRANT),
        cost_estimate=pl.CostEstimate(
            flops=2 * 3 * cols * cells * cells * (members + columns),
            bytes_accessed=2 << 20,
            transcendentals=0,
        ),
        name="above",
    )(s, u, w, inside, outside, live, index, tapers)


def columns_kernel(u, w, inside, outside, live, index, tapers, side):
    rows, cols, members, cells = u.shape
    deep = members + w.shape[2]
    last = cols - 1
    left, right = sides(inside, outside)
    on = [live[a] for a in range(rows)]
    which = [index[a] for a in range(rows)]
    total = {}

    def add(a, q, value):
        total[a, q] = total[a, q] + value if (a, q) in total else value

    for a in range(rows):
        near = [(5, a)] + ([(8, a + 1)] if a + 1 < rows else [])
        gram = dot(left(a, slice(0, members)), cat([u[p, 0] for _, p in near], 1), TN)
        blocks = cat(
            [
                tapered(gram[:, n * cells : (n + 1) * cells], tapers[which[p][0, 8 - k]], on[p][0, 8 - k])
                for n, (k, p) in enumerate(near)
            ],
            1,
        )
        both = dot(left(a, slice(members, deep)), blocks, NN)
        for n, (_, p) in enumerate(near):
            add(p, 0, both[:, n * cells : (n + 1) * cells])
        gram = dot(u[a, last], cat([right(p, slice(0, members)) for _, p in near], 1), TN)
        blocks = cat(
            [
                tapered(gram[:, n * cells : (n + 1) * cells], tapers[which[a][last, k]], on[a][last, k])
                for n, (k, _) in enumerate(near)
            ],
            1,
        )
        add(a, last, dot(cat([right(p, slice(members, deep)) for _, p in near], 1), blocks, NT))
        if a + 1 < rows:
            gram = dot(u[a, 0], left(a + 1, slice(0, members)), TN)
            block = tapered(gram, tapers[which[a][0, 6]], on[a][0, 6])
            add(a, 0, dot(left(a + 1, slice(members, deep)), block, NT))
            gram = dot(right(a, slice(0, members)), u[a + 1, last], TN)
            block = tapered(gram, tapers[which[a + 1][last, 2]], on[a + 1][last, 2])
            add(a + 1, last, dot(right(a, slice(members, deep)), block, NN))

    for a in range(rows):
        side[0, a] = total[a, 0]
        side[1, a] = total[a, last]


def columns(u, w, inside, outside, live, index, tapers):
    rows, _, members, cells = u.shape
    width = w.shape[2]
    return pl.pallas_call(
        columns_kernel,
        out_shape=jax.ShapeDtypeStruct((2, rows, width, cells), jnp.float32),
        in_specs=[VMEM] * 7,
        out_specs=VMEM,
        compiler_params=pltpu.CompilerParams(vmem_limit_bytes=GRANT),
        cost_estimate=pl.CostEstimate(
            flops=12 * rows * cells * cells * (members + width), bytes_accessed=2 << 20, transcendentals=0
        ),
        name="columns",
    )(u, w, inside, outside, live, index, tapers)


def outer_kernel(inc, side, held, tail, rest, u, live, index, tapers, out, top, low):
    rows, cols, members, cells = u.shape
    width = inc.shape[2]
    last = cols - 1
    even = even_column()
    on, which = live[0], index[0]
    start = (cols - 1) * width
    gram = dot(rest[start : start + members], jnp.where(even, u[0, 0], u[0, last]), TN)
    at = jnp.where(even, which[0, 0], which[last, 2])
    block = tapered(gram, tapers[at], jnp.where(even, on[0, 0], on[last, 2]))
    far = dot(rest[start + members :], block, NN)
    blank = jnp.zeros_like(far)
    parts = [rest[c * width : (c + 1) * width] for c in range(cols - 1)]
    tail = tail[...]
    weights = [jnp.where(even, parts[0], tail)]
    weights += [jnp.where(even, parts[c], parts[c - 1]) for c in range(1, last)]
    weights.append(jnp.where(even, tail, parts[last - 1]))
    for q in range(cols):
        back = [(k, q - (k - 7)) for k in (6, 7, 8) if 0 <= q - (k - 7) < cols]
        blocks = [held[c, :, (k - 6) * cells : (k - 5) * cells] for k, c in back]
        value = inc[0, q] + dot(cat([weights[c] for _, c in back], 1), cat(blocks, 0), NN)
        if q in (0, last):
            value += side[q // last, 0]
            value += jnp.where(even, far, blank) if q == 0 else jnp.where(even, blank, far)
            top[q // last] = value
        out[0, q] = value
    for a in range(1, rows):
        for q in range(cols):
            value = inc[a, q] + side[q // last, a] if q in (0, last) else inc[a, q]
            out[a, q] = value
            if a == rows - 1:
                low[q] = value


def outer(inc, side, held, tail, rest, u, live, index, tapers):
    rows, cols, width, cells = inc.shape
    return pl.pallas_call(
        outer_kernel,
        out_shape=(
            jax.ShapeDtypeStruct(inc.shape, inc.dtype),
            jax.ShapeDtypeStruct((2, width, cells), inc.dtype),
            jax.ShapeDtypeStruct(inc.shape[1:], inc.dtype),
        ),
        in_specs=[VMEM] * 9,
        out_specs=(VMEM,) * 3,
        compiler_params=pltpu.CompilerParams(vmem_limit_bytes=GRANT),
        cost_estimate=pl.CostEstimate(flops=6 * cols * cells * cells * width, bytes_accessed=4 << 20, transcendentals=0),
        name="outer",
    )(inc, side, held, tail, rest, u, live, index, tapers)


def finish_kernel(inc, top, low, back, from_inside, out, end, total, sem):
    del inc
    rows, cols = out.shape[:2]
    half = cols // 2
    side = even_column().astype(jnp.int32)
    copies = []
    for n, part in enumerate((slice(0, half), slice(half, cols))):
        total[part] = low[part] + back[part].astype(jnp.float32)
        copies.append(pltpu.make_async_copy(total.at[part], out.at[rows - 1, part], sem.at[n]))
        copies[-1].start()
    end[...] = top[side] + from_inside[...]
    copies.append(pltpu.make_async_copy(end, out.at[0, side * (cols - 1)], sem.at[2]))
    copies[-1].start()
    for copy in copies:
        copy.wait()


def finish(inc, top, low, back, from_inside):
    return pl.pallas_call(
        finish_kernel,
        out_shape=jax.ShapeDtypeStruct(inc.shape, inc.dtype),
        in_specs=[ANY] + [VMEM] * 4,
        out_specs=ANY,
        scratch_shapes=[
            pltpu.VMEM(top.shape[1:], top.dtype),
            pltpu.VMEM(low.shape, low.dtype),
            pltpu.SemaphoreType.DMA((3,)),
        ],
        input_output_aliases={0: 0},
        compiler_params=pltpu.CompilerParams(vmem_limit_bytes=GRANT),
        cost_estimate=pl.CostEstimate(flops=low.size, bytes_accessed=10 * low.size, transcendentals=0),
        name="finish",
    )(inc, top, low, back, from_inside)


def forward(axis):
    return [(i, i + 1) for i in range(lax.axis_size(axis) - 1)]


def swaps(axis, start):
    pairs = [(i, i + 1) for i in range(start, lax.axis_size(axis) - 1, 2)]
    return pairs + [(b, a) for a, b in pairs]


def backward(axis):
    return [(i + 1, i) for i in range(lax.axis_size(axis) - 1)]


def pack_row_kernel(u, w, out, done, sem):
    rows, cols, members, _ = u.shape
    beside = (cols - 1) * even_column().astype(jnp.int32)
    copies = [
        pltpu.make_async_copy(u.at[rows - 1, q], out.at[q * members : (q + 1) * members], sem.at[q])
        for q in range(cols)
    ]
    copies.append(pltpu.make_async_copy(w.at[rows - 1, beside], out.at[cols * members :], sem.at[cols]))
    for copy in copies:
        copy.start()
    for copy in copies:
        copy.wait()
    done[...] = jnp.zeros_like(done)


def pack_row(u, w):
    _, cols, members, cells = u.shape
    shape = (cols * members + w.shape[2], cells)
    return pl.pallas_call(
        pack_row_kernel,
        out_shape=(pltpu.VMEM(shape, u.dtype), jax.ShapeDtypeStruct((8, cells), jnp.float32)),
        in_specs=[HBM, HBM],
        out_specs=(VMEM, VMEM),
        scratch_shapes=[pltpu.SemaphoreType.DMA((cols + 1,))],
        cost_estimate=pl.CostEstimate(flops=0, bytes_accessed=4 * shape[0] * cells, transcendentals=0),
        name="pack_row",
    )(u, w)


def pack_rest_kernel(w, outside, out):
    rows, cols, width, _ = w.shape
    skip = 1 - even_column().astype(jnp.int32)
    for q in range(cols - 1):
        out[q * width : (q + 1) * width] = w[rows - 1, q + skip]
    start = (cols - 1) * width
    out[start:] = outside[rows - 1, : out.shape[0] - start]


def pack_rest(w, outside, members):
    _, cols, width, cells = w.shape
    return pl.pallas_call(
        pack_rest_kernel,
        out_shape=jax.ShapeDtypeStruct(((cols - 1) * width + members + width, cells), w.dtype),
        in_specs=[VMEM, VMEM],
        out_specs=VMEM,
        compiler_params=pltpu.CompilerParams(vmem_limit_bytes=GRANT),
        cost_estimate=pl.CostEstimate(flops=0, bytes_accessed=8 * cols * width * cells, transcendentals=0),
        name="pack_rest",
    )(w, outside)


def load_kernel(u, w, live, index, done, u_here, w_here, inner_side, outer_side, sem):
    del done
    rows, cols, members, cells = u.shape
    deep = members + w.shape[2]
    turn = (cols - 1) * even_column().astype(jnp.int32)
    copies = [pltpu.make_async_copy(w, w_here, sem.at[rows])]
    copies += [pltpu.make_async_copy(u.at[a], u_here.at[a], sem.at[a]) for a in range(rows)]
    for copy in copies:
        copy.start()
    for a in range(rows):
        lines = jnp.concatenate([live[a], index[a]], 0).astype(jnp.float32)
        blank = jnp.zeros((2 * cols, cells - live.shape[2]), jnp.float32)
        note = jnp.concatenate([lines, blank], 1).astype(jnp.bfloat16)
        inner_side[a, deep:] = note
        outer_side[a, deep:] = note
    copies[0].wait()
    for a in range(rows):
        copies[1 + a].wait()
        for side, b in ((inner_side, turn), (outer_side, cols - 1 - turn)):
            side[a, :members] = u_here[a, b]
            side[a, members:deep] = w_here[a, b]


def load(u, w, live, index, done):
    rows, cols, members, cells = u.shape
    side = pltpu.VMEM((rows, members + w.shape[2] + 2 * cols, cells), u.dtype)
    return pl.pallas_call(
        load_kernel,
        out_shape=(pltpu.VMEM(u.shape, u.dtype), pltpu.VMEM(w.shape, w.dtype), side, side),
        in_specs=[HBM, HBM, VMEM, VMEM, VMEM],
        out_specs=(VMEM,) * 4,
        scratch_shapes=[pltpu.SemaphoreType.DMA((rows + 1,))],
        compiler_params=pltpu.CompilerParams(vmem_limit_bytes=WIDE),
        cost_estimate=pl.CostEstimate(flops=0, bytes_accessed=4 * u.size + 4 * w.size, transcendentals=0),
        name="load",
    )(u, w, live, index, done)


def body(perturbations, weights, live, index, tapers):
    packed, done = pack_row(perturbations, weights)
    s = lax.ppermute(packed, "row", forward("row"))
    u, w, inner_side, outer_side = load(perturbations, weights, live, index, done)
    inside = lax.ppermute(inner_side, "col", swaps("col", 0))
    outside = lax.ppermute(outer_side, "col", swaps("col", 1))
    inc, inside, outside = lax.optimization_barrier((inner(u, w, live, index, tapers), inside, outside))
    rest = lax.ppermute(pack_rest(w, outside, u.shape[2]), "row", forward("row"))
    back, held, to_inside, tail = above(s, u, w, inside, outside, live, index, tapers)
    back = lax.ppermute(back, "row", backward("row"))
    from_inside = lax.ppermute(to_inside, "col", swaps("col", 0))
    side = columns(u, w, inside, outside, live, index, tapers)
    inc, top, low = outer(inc, side, held, tail, rest, u, live, index, tapers)
    return finish(inc, top, low, back, from_inside)


def solution(mesh):
    return jax.shard_map(
        body,
        mesh=mesh,
        in_specs=(
            P("row", "col", None, None),
            P("row", "col", None, None),
            P("row", "col", None),
            P("row", "col", None),
            P(),
        ),
        out_specs=P("row", "col", None, None),
        check_vma=False,
    )
```

```python
import jax
import jax.numpy as jnp
from jax import lax
from jax.experimental import pallas as pl
from jax.experimental.pallas import tpu as pltpu
from jax.sharding import PartitionSpec as P

MEMBERS = 256
GRANT = 16 << 20
SCALE = 1.0 / (MEMBERS - 1)
TN = (((0,), (0,)), ((), ()))
NT = (((1,), (1,)), ((), ()))
NN = (((1,), (0,)), ((), ()))
VMEM = pl.BlockSpec(memory_space=pltpu.VMEM)
ANY = pl.BlockSpec(memory_space=pl.ANY)
HBM = pl.BlockSpec(memory_space=pltpu.HBM)


def dot(a, b, dims):
    return lax.dot_general(a, b, dims, preferred_element_type=jnp.float32)


def cat(parts, axis):
    return parts[0] if len(parts) == 1 else jnp.concatenate(parts, axis=axis)


def tapered(gram, rho, live):
    factor = live.astype(jnp.float32) * SCALE
    return (rho.astype(jnp.float32) * gram * factor).astype(jnp.bfloat16)


def even_column():
    return lax.rem(lax.axis_index("col"), 2) == 0


def sides(inside, outside):
    even = even_column()
    return (
        lambda *at: jnp.where(even, outside[at], inside[at]),
        lambda *at: jnp.where(even, inside[at], outside[at]),
    )


def inner_kernel(u, w, live, index, tapers, out, sym, held):
    rows, cols, _, cells = u.shape
    for n in range(tapers.shape[0]):
        t = tapers[n].astype(jnp.float32)
        sym[n] = 0.5 * (t + t.T)

    def ahead(a, b, last):
        near = [(4, a, b)]
        if b + 1 < cols:
            near.append((5, a, b + 1))
        if not last:
            for k in (6, 7, 8):
                if 0 <= b + k - 7 < cols:
                    near.append((k, a + 1, b + k - 7))
        return near

    def row(a, last):
        on, which = live[a], index[a]
        for b in range(cols):
            near = ahead(a, b, last)
            gram = dot(u[a, b], cat([u[p, q] for _, p, q in near], 1), TN)
            for n, (k, _, _) in enumerate(near):
                at = which[b, k]
                rho = sym[at] if k == 4 else tapers[at]
                held[b, :, (k - 4) * cells : (k - 3) * cells] = tapered(
                    gram[:, n * cells : (n + 1) * cells], rho, on[b, k]
                )
        for b in range(cols):
            near = ahead(a, b, last)
            total = dot(
                cat([w[p, q] for _, p, q in near], 1),
                cat([held[b, :, (k - 4) * cells : (k - 3) * cells] for k, _, _ in near], 1),
                NT,
            )
            if b > 0:
                total += dot(w[a, b - 1], held[b - 1, :, cells : 2 * cells], NN)
            out[a, b] += total
            if not last:
                back = [(k, b - (k - 7)) for k in (6, 7, 8) if 0 <= b - (k - 7) < cols]
                out[a + 1, b] = dot(
                    cat([w[a, q] for _, q in back], 1),
                    cat([held[q, :, (k - 4) * cells : (k - 3) * cells] for k, q in back], 0),
                    NN,
                )

    out[0] = jnp.zeros_like(out[0])

    @pl.loop(0, rows - 1)
    def _(a):
        row(a, False)

    row(rows - 1, True)


def inner(u, w, live, index, tapers):
    rows, cols, members, cells = u.shape
    columns = w.shape[2]
    pairs = 5 * rows * cols
    return pl.pallas_call(
        inner_kernel,
        out_shape=jax.ShapeDtypeStruct((rows, cols, columns, cells), jnp.float32),
        in_specs=[VMEM] * 5,
        out_specs=VMEM,
        scratch_shapes=[
            pltpu.VMEM(tapers.shape, jnp.float32),
            pltpu.VMEM((cols, cells, 5 * cells), jnp.bfloat16),
        ],
        compiler_params=pltpu.CompilerParams(vmem_limit_bytes=GRANT),
        cost_estimate=pl.CostEstimate(
            flops=2 * pairs * cells * cells * (members + 2 * columns),
            bytes_accessed=4 << 20,
            transcendentals=0,
        ),
        name="inner",
    )(u, w, live, index, tapers)


def above_kernel(s, u, w, inside, outside, live, index, tapers, back, held, to_inside, tail):
    cols, members, cells = u.shape[1:]
    deep = members + w.shape[2]
    last = cols - 1
    left, right = sides(inside, outside)
    on, which = live[0], index[0]
    beyond = {}
    for q, near, k, line in ((-1, left, 2, last), (cols, right, 0, 0)):
        note = near(0, slice(deep, None)).astype(jnp.int32)
        beyond[q] = near, note[line, k], note[cols + line, k]
    sources = []
    for c in range(cols):
        grams, weights, lives, rhos = [], [], [], []
        for k in (6, 7, 8):
            q = c + k - 7
            if q in beyond:
                near, lively, at = beyond[q]
                grams.append(near(0, slice(0, members)))
                weights.append(near(0, slice(members, deep)))
            else:
                lively, at = on[q, 8 - k], which[q, 8 - k]
                grams.append(u[0, q])
                weights.append(w[0, q])
            lives.append(lively)
            rhos.append(tapers[at])
        gram = dot(s[c * members : (c + 1) * members], cat(grams, 1), TN)
        held[c] = cat([tapered(gram[:, m * cells : (m + 1) * cells], rhos[m], lives[m]) for m in range(3)], 1)
        sources.append(cat(weights, 1))
    for c in range(cols):
        back[c] = dot(sources[c], held[c], NT).astype(jnp.bfloat16)
    even = even_column()
    tail[...] = s[cols * members :]
    to_inside[...] = dot(s[cols * members :], jnp.where(even, held[last, :, 2 * cells :], held[0, :, :cells]), NN)


def above(s, u, w, inside, outside, live, index, tapers):
    cols, members, cells = u.shape[1:]
    columns = w.shape[2]
    return pl.pallas_call(
        above_kernel,
        out_shape=(
            jax.ShapeDtypeStruct((cols, columns, cells), jnp.bfloat16),
            jax.ShapeDtypeStruct((cols, cells, 3 * cells), jnp.bfloat16),
            jax.ShapeDtypeStruct((columns, cells), jnp.float32),
            jax.ShapeDtypeStruct((columns, cells), jnp.bfloat16),
        ),
        in_specs=[VMEM] * 8,
        out_specs=(VMEM,) * 4,
        compiler_params=pltpu.CompilerParams(vmem_limit_bytes=GRANT),
        cost_estimate=pl.CostEstimate(
            flops=2 * 3 * cols * cells * cells * (members + columns),
            bytes_accessed=2 << 20,
            transcendentals=0,
        ),
        name="above",
    )(s, u, w, inside, outside, live, index, tapers)


def columns_kernel(u, w, inside, outside, live, index, tapers, side):
    rows, cols, members, cells = u.shape
    deep = members + w.shape[2]
    last = cols - 1
    left, right = sides(inside, outside)
    on = [live[a] for a in range(rows)]
    which = [index[a] for a in range(rows)]
    total = {}

    def add(a, q, value):
        total[a, q] = total[a, q] + value if (a, q) in total else value

    for a in range(rows):
        near = [(5, a)] + ([(8, a + 1)] if a + 1 < rows else [])
        gram = dot(left(a, slice(0, members)), cat([u[p, 0] for _, p in near], 1), TN)
        blocks = cat(
            [
                tapered(gram[:, n * cells : (n + 1) * cells], tapers[which[p][0, 8 - k]], on[p][0, 8 - k])
                for n, (k, p) in enumerate(near)
            ],
            1,
        )
        both = dot(left(a, slice(members, deep)), blocks, NN)
        for n, (_, p) in enumerate(near):
            add(p, 0, both[:, n * cells : (n + 1) * cells])
        gram = dot(u[a, last], cat([right(p, slice(0, members)) for _, p in near], 1), TN)
        blocks = cat(
            [
                tapered(gram[:, n * cells : (n + 1) * cells], tapers[which[a][last, k]], on[a][last, k])
                for n, (k, _) in enumerate(near)
            ],
            1,
        )
        add(a, last, dot(cat([right(p, slice(members, deep)) for _, p in near], 1), blocks, NT))
        if a + 1 < rows:
            gram = dot(u[a, 0], left(a + 1, slice(0, members)), TN)
            block = tapered(gram, tapers[which[a][0, 6]], on[a][0, 6])
            add(a, 0, dot(left(a + 1, slice(members, deep)), block, NT))
            gram = dot(right(a, slice(0, members)), u[a + 1, last], TN)
            block = tapered(gram, tapers[which[a + 1][last, 2]], on[a + 1][last, 2])
            add(a + 1, last, dot(right(a, slice(members, deep)), block, NN))

    for a in range(rows):
        side[0, a] = total[a, 0]
        side[1, a] = total[a, last]


def columns(u, w, inside, outside, live, index, tapers):
    rows, _, members, cells = u.shape
    width = w.shape[2]
    return pl.pallas_call(
        columns_kernel,
        out_shape=jax.ShapeDtypeStruct((2, rows, width, cells), jnp.float32),
        in_specs=[VMEM] * 7,
        out_specs=VMEM,
        compiler_params=pltpu.CompilerParams(vmem_limit_bytes=GRANT),
        cost_estimate=pl.CostEstimate(
            flops=12 * rows * cells * cells * (members + width), bytes_accessed=2 << 20, transcendentals=0
        ),
        name="columns",
    )(u, w, inside, outside, live, index, tapers)


def outer_kernel(inc, side, held, tail, rest, u, live, index, tapers, out, top, low):
    rows, cols, members, cells = u.shape
    width = inc.shape[2]
    last = cols - 1
    even = even_column()
    on, which = live[0], index[0]
    start = (cols - 1) * width
    gram = dot(rest[start : start + members], jnp.where(even, u[0, 0], u[0, last]), TN)
    at = jnp.where(even, which[0, 0], which[last, 2])
    block = tapered(gram, tapers[at], jnp.where(even, on[0, 0], on[last, 2]))
    far = dot(rest[start + members :], block, NN)
    blank = jnp.zeros_like(far)
    parts = [rest[c * width : (c + 1) * width] for c in range(cols - 1)]
    tail = tail[...]
    weights = [jnp.where(even, parts[0], tail)]
    weights += [jnp.where(even, parts[c], parts[c - 1]) for c in range(1, last)]
    weights.append(jnp.where(even, tail, parts[last - 1]))
    for q in range(cols):
        back = [(k, q - (k - 7)) for k in (6, 7, 8) if 0 <= q - (k - 7) < cols]
        blocks = [held[c, :, (k - 6) * cells : (k - 5) * cells] for k, c in back]
        value = inc[0, q] + dot(cat([weights[c] for _, c in back], 1), cat(blocks, 0), NN)
        if q in (0, last):
            value += side[q // last, 0]
            value += jnp.where(even, far, blank) if q == 0 else jnp.where(even, blank, far)
            top[q // last] = value
        out[0, q] = value
    for a in range(1, rows):
        for q in range(cols):
            value = inc[a, q] + side[q // last, a] if q in (0, last) else inc[a, q]
            out[a, q] = value
            if a == rows - 1:
                low[q] = value


def outer(inc, side, held, tail, rest, u, live, index, tapers):
    rows, cols, width, cells = inc.shape
    return pl.pallas_call(
        outer_kernel,
        out_shape=(
            jax.ShapeDtypeStruct(inc.shape, inc.dtype),
            jax.ShapeDtypeStruct((2, width, cells), inc.dtype),
            jax.ShapeDtypeStruct(inc.shape[1:], inc.dtype),
        ),
        in_specs=[VMEM] * 9,
        out_specs=(VMEM,) * 3,
        compiler_params=pltpu.CompilerParams(vmem_limit_bytes=GRANT),
        cost_estimate=pl.CostEstimate(flops=6 * cols * cells * cells * width, bytes_accessed=4 << 20, transcendentals=0),
        name="outer",
    )(inc, side, held, tail, rest, u, live, index, tapers)


def finish_kernel(inc, top, low, back, from_inside, out, end, total, sem):
    del inc
    rows, cols = out.shape[:2]
    half = cols // 2
    side = even_column().astype(jnp.int32)
    copies = []
    for n, part in enumerate((slice(0, half), slice(half, cols))):
        total[part] = low[part] + back[part].astype(jnp.float32)
        copies.append(pltpu.make_async_copy(total.at[part], out.at[rows - 1, part], sem.at[n]))
        copies[-1].start()
    end[...] = top[side] + from_inside[...]
    copies.append(pltpu.make_async_copy(end, out.at[0, side * (cols - 1)], sem.at[2]))
    copies[-1].start()
    for copy in copies:
        copy.wait()


def finish(inc, top, low, back, from_inside):
    return pl.pallas_call(
        finish_kernel,
        out_shape=jax.ShapeDtypeStruct(inc.shape, inc.dtype),
        in_specs=[ANY] + [VMEM] * 4,
        out_specs=ANY,
        scratch_shapes=[
            pltpu.VMEM(top.shape[1:], top.dtype),
            pltpu.VMEM(low.shape, low.dtype),
            pltpu.SemaphoreType.DMA((3,)),
        ],
        input_output_aliases={0: 0},
        compiler_params=pltpu.CompilerParams(vmem_limit_bytes=GRANT),
        cost_estimate=pl.CostEstimate(flops=low.size, bytes_accessed=10 * low.size, transcendentals=0),
        name="finish",
    )(inc, top, low, back, from_inside)


def forward(axis):
    return [(i, i + 1) for i in range(lax.axis_size(axis) - 1)]


def swaps(axis, start):
    pairs = [(i, i + 1) for i in range(start, lax.axis_size(axis) - 1, 2)]
    return pairs + [(b, a) for a, b in pairs]


def backward(axis):
    return [(i + 1, i) for i in range(lax.axis_size(axis) - 1)]


def pack_row_kernel(u, w, out, sem):
    rows, cols, members, cells = u.shape
    beside = (cols - 1) * even_column().astype(jnp.int32)
    deep = cols * members
    copies = [
        pltpu.make_async_copy(u.at[rows - 1].reshape(deep, cells), out.at[:deep], sem.at[0]),
        pltpu.make_async_copy(w.at[rows - 1, beside], out.at[deep:], sem.at[1]),
    ]
    for copy in copies:
        copy.start()
    for copy in copies:
        copy.wait()


def pack_row(u, w):
    _, cols, members, cells = u.shape
    shape = (cols * members + w.shape[2], cells)
    return pl.pallas_call(
        pack_row_kernel,
        out_shape=pltpu.VMEM(shape, u.dtype),
        in_specs=[HBM, HBM],
        out_specs=VMEM,
        scratch_shapes=[pltpu.SemaphoreType.DMA((2,))],
        cost_estimate=pl.CostEstimate(flops=0, bytes_accessed=4 * shape[0] * cells, transcendentals=0),
        name="pack_row",
    )(u, w)


def pack_rest_kernel(w, outside, out):
    rows, cols, width, _ = w.shape
    skip = 1 - even_column().astype(jnp.int32)
    for q in range(cols - 1):
        out[q * width : (q + 1) * width] = w[rows - 1, q + skip]
    start = (cols - 1) * width
    out[start:] = outside[rows - 1, : out.shape[0] - start]


def pack_rest(w, outside, members):
    _, cols, width, cells = w.shape
    return pl.pallas_call(
        pack_rest_kernel,
        out_shape=jax.ShapeDtypeStruct(((cols - 1) * width + members + width, cells), w.dtype),
        in_specs=[VMEM, VMEM],
        out_specs=VMEM,
        compiler_params=pltpu.CompilerParams(vmem_limit_bytes=GRANT),
        cost_estimate=pl.CostEstimate(flops=0, bytes_accessed=8 * cols * width * cells, transcendentals=0),
        name="pack_rest",
    )(w, outside)


def pack_columns_kernel(u, w, live, index, packed, inner_side, outer_side, sem):
    del packed
    rows, cols, members, cells = u.shape
    deep = members + w.shape[2]
    turn = (cols - 1) * even_column().astype(jnp.int32)
    copies = []
    for n, (out, b) in enumerate(((inner_side, turn), (outer_side, cols - 1 - turn))):
        copies.append(pltpu.make_async_copy(u.at[:, b], out.at[:, :members], sem.at[n, 0]))
        copies.append(pltpu.make_async_copy(w.at[:, b], out.at[:, members:deep], sem.at[n, 1]))
    for copy in copies:
        copy.start()
    for a in range(rows):
        lines = jnp.concatenate([live[a], index[a]], 0).astype(jnp.float32)
        blank = jnp.zeros((2 * cols, cells - live.shape[2]), jnp.float32)
        note = jnp.concatenate([lines, blank], 1).astype(jnp.bfloat16)
        inner_side[a, deep:] = note
        outer_side[a, deep:] = note
    for copy in copies:
        copy.wait()


def pack_columns(u, w, live, index, packed):
    rows, cols, members, cells = u.shape
    shape = (rows, members + w.shape[2] + 2 * cols, cells)
    return pl.pallas_call(
        pack_columns_kernel,
        out_shape=(jax.ShapeDtypeStruct(shape, u.dtype),) * 2,
        in_specs=[ANY, ANY, VMEM, VMEM, VMEM],
        out_specs=(VMEM, VMEM),
        scratch_shapes=[pltpu.SemaphoreType.DMA((2, 2))],
        compiler_params=pltpu.CompilerParams(vmem_limit_bytes=GRANT),
        cost_estimate=pl.CostEstimate(flops=0, bytes_accessed=8 * rows * shape[1] * cells, transcendentals=0),
        name="pack_columns",
    )(u, w, live, index, packed)


def body(u, w, live, index, tapers):
    packed = pack_row(u, w)
    s = lax.ppermute(packed, "row", forward("row"))
    inner_side, outer_side = pack_columns(u, w, live, index, packed)
    outside = lax.ppermute(outer_side, "col", swaps("col", 1))
    inside = lax.ppermute(inner_side, "col", swaps("col", 0))
    inc, outside, inside = lax.optimization_barrier((inner(u, w, live, index, tapers), outside, inside))
    rest = lax.ppermute(pack_rest(w, outside, u.shape[2]), "row", forward("row"))
    back, held, to_inside, tail = above(s, u, w, inside, outside, live, index, tapers)
    back = lax.ppermute(back, "row", backward("row"))
    from_inside = lax.ppermute(to_inside, "col", swaps("col", 0))
    side = columns(u, w, inside, outside, live, index, tapers)
    inc, top, low = outer(inc, side, held, tail, rest, u, live, index, tapers)
    return finish(inc, top, low, back, from_inside)


def solution(mesh):
    return jax.shard_map(
        body,
        mesh=mesh,
        in_specs=(
            P("row", "col", None, None),
            P("row", "col", None, None),
            P("row", "col", None),
            P("row", "col", None),
            P(),
        ),
        out_specs=P("row", "col", None, None),
        check_vma=False,
    )
```

```python
import jax
import jax.numpy as jnp
from jax import lax
from jax.experimental import pallas as pl
from jax.experimental.pallas import tpu as pltpu
from jax.sharding import PartitionSpec as P

MEMBERS = 256
GRANT = 16 << 20
SCALE = 1.0 / (MEMBERS - 1)
TN = (((0,), (0,)), ((), ()))
NT = (((1,), (1,)), ((), ()))
NN = (((1,), (0,)), ((), ()))
VMEM = pl.BlockSpec(memory_space=pltpu.VMEM)
ANY = pl.BlockSpec(memory_space=pl.ANY)
HBM = pl.BlockSpec(memory_space=pltpu.HBM)


def dot(a, b, dims):
    return lax.dot_general(a, b, dims, preferred_element_type=jnp.float32)


def cat(parts, axis):
    return parts[0] if len(parts) == 1 else jnp.concatenate(parts, axis=axis)


def tapered(gram, rho, live):
    factor = live.astype(jnp.float32) * SCALE
    return (rho.astype(jnp.float32) * gram * factor).astype(jnp.bfloat16)


def even_column():
    return lax.rem(lax.axis_index("col"), 2) == 0


def sides(inside, outside):
    even = even_column()
    return (
        lambda *at: jnp.where(even, outside[at], inside[at]),
        lambda *at: jnp.where(even, inside[at], outside[at]),
    )


def inner_kernel(u, w, live, index, tapers, out, sym, held):
    rows, cols, _, cells = u.shape
    for n in range(tapers.shape[0]):
        t = tapers[n].astype(jnp.float32)
        sym[n] = 0.5 * (t + t.T)

    def ahead(a, b, last):
        near = [(4, a, b)]
        if b + 1 < cols:
            near.append((5, a, b + 1))
        if not last:
            for k in (6, 7, 8):
                if 0 <= b + k - 7 < cols:
                    near.append((k, a + 1, b + k - 7))
        return near

    def row(a, last):
        on, which = live[a], index[a]
        for b in range(cols):
            near = ahead(a, b, last)
            gram = dot(u[a, b], cat([u[p, q] for _, p, q in near], 1), TN)
            for n, (k, _, _) in enumerate(near):
                at = which[b, k]
                rho = sym[at] if k == 4 else tapers[at]
                held[b, :, (k - 4) * cells : (k - 3) * cells] = tapered(
                    gram[:, n * cells : (n + 1) * cells], rho, on[b, k]
                )
        for b in range(cols):
            near = ahead(a, b, last)
            total = dot(
                cat([w[p, q] for _, p, q in near], 1),
                cat([held[b, :, (k - 4) * cells : (k - 3) * cells] for k, _, _ in near], 1),
                NT,
            )
            if b > 0:
                total += dot(w[a, b - 1], held[b - 1, :, cells : 2 * cells], NN)
            out[a, b] += total
            if not last:
                back = [(k, b - (k - 7)) for k in (6, 7, 8) if 0 <= b - (k - 7) < cols]
                out[a + 1, b] = dot(
                    cat([w[a, q] for _, q in back], 1),
                    cat([held[q, :, (k - 4) * cells : (k - 3) * cells] for k, q in back], 0),
                    NN,
                )

    out[0] = jnp.zeros_like(out[0])

    @pl.loop(0, rows - 1)
    def _(a):
        row(a, False)

    row(rows - 1, True)


def inner(u, w, live, index, tapers):
    rows, cols, members, cells = u.shape
    columns = w.shape[2]
    pairs = 5 * rows * cols
    return pl.pallas_call(
        inner_kernel,
        out_shape=jax.ShapeDtypeStruct((rows, cols, columns, cells), jnp.float32),
        in_specs=[VMEM] * 5,
        out_specs=VMEM,
        scratch_shapes=[
            pltpu.VMEM(tapers.shape, jnp.float32),
            pltpu.VMEM((cols, cells, 5 * cells), jnp.bfloat16),
        ],
        compiler_params=pltpu.CompilerParams(vmem_limit_bytes=GRANT),
        cost_estimate=pl.CostEstimate(
            flops=2 * pairs * cells * cells * (members + 2 * columns),
            bytes_accessed=4 << 20,
            transcendentals=0,
        ),
        name="inner",
    )(u, w, live, index, tapers)


def above_kernel(s, u, w, inside, outside, live, index, tapers, back, held, to_inside, tail):
    cols, members, cells = u.shape[1:]
    deep = members + w.shape[2]
    last = cols - 1
    left, right = sides(inside, outside)
    on, which = live[0], index[0]
    beyond = {}
    for q, near, k, line in ((-1, left, 2, last), (cols, right, 0, 0)):
        note = near(0, slice(deep, None)).astype(jnp.int32)
        beyond[q] = near, note[line, k], note[cols + line, k]
    sources = []
    for c in range(cols):
        grams, weights, lives, rhos = [], [], [], []
        for k in (6, 7, 8):
            q = c + k - 7
            if q in beyond:
                near, lively, at = beyond[q]
                grams.append(near(0, slice(0, members)))
                weights.append(near(0, slice(members, deep)))
            else:
                lively, at = on[q, 8 - k], which[q, 8 - k]
                grams.append(u[0, q])
                weights.append(w[0, q])
            lives.append(lively)
            rhos.append(tapers[at])
        gram = dot(s[c * members : (c + 1) * members], cat(grams, 1), TN)
        held[c] = cat([tapered(gram[:, m * cells : (m + 1) * cells], rhos[m], lives[m]) for m in range(3)], 1)
        sources.append(cat(weights, 1))
    for c in range(cols):
        back[c] = dot(sources[c], held[c], NT).astype(jnp.bfloat16)
    even = even_column()
    tail[...] = s[cols * members :]
    to_inside[...] = dot(s[cols * members :], jnp.where(even, held[last, :, 2 * cells :], held[0, :, :cells]), NN)


def above(s, u, w, inside, outside, live, index, tapers):
    cols, members, cells = u.shape[1:]
    columns = w.shape[2]
    return pl.pallas_call(
        above_kernel,
        out_shape=(
            jax.ShapeDtypeStruct((cols, columns, cells), jnp.bfloat16),
            jax.ShapeDtypeStruct((cols, cells, 3 * cells), jnp.bfloat16),
            jax.ShapeDtypeStruct((columns, cells), jnp.float32),
            jax.ShapeDtypeStruct((columns, cells), jnp.bfloat16),
        ),
        in_specs=[VMEM] * 8,
        out_specs=(VMEM,) * 4,
        compiler_params=pltpu.CompilerParams(vmem_limit_bytes=GRANT),
        cost_estimate=pl.CostEstimate(
            flops=2 * 3 * cols * cells * cells * (members + columns),
            bytes_accessed=2 << 20,
            transcendentals=0,
        ),
        name="above",
    )(s, u, w, inside, outside, live, index, tapers)


def columns_kernel(u, w, inside, outside, live, index, tapers, side):
    rows, cols, members, cells = u.shape
    deep = members + w.shape[2]
    last = cols - 1
    left, right = sides(inside, outside)
    on = [live[a] for a in range(rows)]
    which = [index[a] for a in range(rows)]
    total = {}

    def add(a, q, value):
        total[a, q] = total[a, q] + value if (a, q) in total else value

    for a in range(rows):
        near = [(5, a)] + ([(8, a + 1)] if a + 1 < rows else [])
        gram = dot(left(a, slice(0, members)), cat([u[p, 0] for _, p in near], 1), TN)
        blocks = cat(
            [
                tapered(gram[:, n * cells : (n + 1) * cells], tapers[which[p][0, 8 - k]], on[p][0, 8 - k])
                for n, (k, p) in enumerate(near)
            ],
            1,
        )
        both = dot(left(a, slice(members, deep)), blocks, NN)
        for n, (_, p) in enumerate(near):
            add(p, 0, both[:, n * cells : (n + 1) * cells])
        gram = dot(u[a, last], cat([right(p, slice(0, members)) for _, p in near], 1), TN)
        blocks = cat(
            [
                tapered(gram[:, n * cells : (n + 1) * cells], tapers[which[a][last, k]], on[a][last, k])
                for n, (k, _) in enumerate(near)
            ],
            1,
        )
        add(a, last, dot(cat([right(p, slice(members, deep)) for _, p in near], 1), blocks, NT))
        if a + 1 < rows:
            gram = dot(u[a, 0], left(a + 1, slice(0, members)), TN)
            block = tapered(gram, tapers[which[a][0, 6]], on[a][0, 6])
            add(a, 0, dot(left(a + 1, slice(members, deep)), block, NT))
            gram = dot(right(a, slice(0, members)), u[a + 1, last], TN)
            block = tapered(gram, tapers[which[a + 1][last, 2]], on[a + 1][last, 2])
            add(a + 1, last, dot(right(a, slice(members, deep)), block, NN))

    for a in range(rows):
        side[0, a] = total[a, 0]
        side[1, a] = total[a, last]


def columns(u, w, inside, outside, live, index, tapers):
    rows, _, members, cells = u.shape
    width = w.shape[2]
    return pl.pallas_call(
        columns_kernel,
        out_shape=jax.ShapeDtypeStruct((2, rows, width, cells), jnp.float32),
        in_specs=[VMEM] * 7,
        out_specs=VMEM,
        compiler_params=pltpu.CompilerParams(vmem_limit_bytes=GRANT),
        cost_estimate=pl.CostEstimate(
            flops=12 * rows * cells * cells * (members + width), bytes_accessed=2 << 20, transcendentals=0
        ),
        name="columns",
    )(u, w, inside, outside, live, index, tapers)


def outer_kernel(inc, side, held, tail, rest, plain, u, live, index, tapers, out, top, low):
    rows, cols, members, cells = u.shape
    width = inc.shape[2]
    last = cols - 1
    even = even_column()
    on, which = live[0], index[0]
    start = (cols - 1) * width
    gram = dot(rest[start : start + members], jnp.where(even, u[0, 0], u[0, last]), TN)
    at = jnp.where(even, which[0, 0], which[last, 2])
    block = tapered(gram, tapers[at], jnp.where(even, on[0, 0], on[last, 2]))
    far = dot(rest[start + members :], block, NN)
    blank = jnp.zeros_like(far)
    parts = [rest[c * width : (c + 1) * width] for c in range(cols - 1)]
    tail = tail[...]
    weights = [jnp.where(even, parts[0], tail)]
    weights += [jnp.where(even, parts[c], parts[c - 1]) for c in range(1, last)]
    weights.append(jnp.where(even, tail, parts[last - 1]))
    place = lax.axis_index("col")
    alone = jnp.logical_or(place == 0, place == lax.axis_size("col") - 1)
    weights = [jnp.where(alone, plain[c], weight) for c, weight in enumerate(weights)]
    for q in range(cols):
        back = [(k, q - (k - 7)) for k in (6, 7, 8) if 0 <= q - (k - 7) < cols]
        blocks = [held[c, :, (k - 6) * cells : (k - 5) * cells] for k, c in back]
        value = inc[0, q] + dot(cat([weights[c] for _, c in back], 1), cat(blocks, 0), NN)
        if q in (0, last):
            value += side[q // last, 0]
            value += jnp.where(even, far, blank) if q == 0 else jnp.where(even, blank, far)
            top[q // last] = value
        out[0, q] = value
    for a in range(1, rows):
        for q in range(cols):
            value = inc[a, q] + side[q // last, a] if q in (0, last) else inc[a, q]
            out[a, q] = value
            if a == rows - 1:
                low[q] = value


def outer(inc, side, held, tail, rest, plain, u, live, index, tapers):
    rows, cols, width, cells = inc.shape
    return pl.pallas_call(
        outer_kernel,
        out_shape=(
            jax.ShapeDtypeStruct(inc.shape, inc.dtype),
            jax.ShapeDtypeStruct((2, width, cells), inc.dtype),
            jax.ShapeDtypeStruct(inc.shape[1:], inc.dtype),
        ),
        in_specs=[VMEM] * 10,
        out_specs=(VMEM,) * 3,
        compiler_params=pltpu.CompilerParams(vmem_limit_bytes=GRANT),
        cost_estimate=pl.CostEstimate(flops=6 * cols * cells * cells * width, bytes_accessed=4 << 20, transcendentals=0),
        name="outer",
    )(inc, side, held, tail, rest, plain, u, live, index, tapers)


def finish_kernel(inc, top, low, back, from_inside, out, end, total, sem):
    del inc
    rows, cols = out.shape[:2]
    half = cols // 2
    side = even_column().astype(jnp.int32)
    copies = []
    for n, part in enumerate((slice(0, half), slice(half, cols))):
        total[part] = low[part] + back[part].astype(jnp.float32)
        copies.append(pltpu.make_async_copy(total.at[part], out.at[rows - 1, part], sem.at[n]))
        copies[-1].start()
    end[...] = top[side] + from_inside[...]
    copies.append(pltpu.make_async_copy(end, out.at[0, side * (cols - 1)], sem.at[2]))
    copies[-1].start()
    for copy in copies:
        copy.wait()


def finish(inc, top, low, back, from_inside):
    return pl.pallas_call(
        finish_kernel,
        out_shape=jax.ShapeDtypeStruct(inc.shape, inc.dtype),
        in_specs=[ANY] + [VMEM] * 4,
        out_specs=ANY,
        scratch_shapes=[
            pltpu.VMEM(top.shape[1:], top.dtype),
            pltpu.VMEM(low.shape, low.dtype),
            pltpu.SemaphoreType.DMA((3,)),
        ],
        input_output_aliases={0: 0},
        compiler_params=pltpu.CompilerParams(vmem_limit_bytes=GRANT),
        cost_estimate=pl.CostEstimate(flops=low.size, bytes_accessed=10 * low.size, transcendentals=0),
        name="finish",
    )(inc, top, low, back, from_inside)


def forward(axis):
    return [(i, i + 1) for i in range(lax.axis_size(axis) - 1)]


def swaps(axis, start):
    pairs = [(i, i + 1) for i in range(start, lax.axis_size(axis) - 1, 2)]
    return pairs + [(b, a) for a, b in pairs]


def backward(axis):
    return [(i + 1, i) for i in range(lax.axis_size(axis) - 1)]


def pack_row_kernel(u, w, out, sem):
    rows, cols, members, cells = u.shape
    beside = (cols - 1) * even_column().astype(jnp.int32)
    deep = cols * members
    copies = [
        pltpu.make_async_copy(u.at[rows - 1].reshape(deep, cells), out.at[:deep], sem.at[0]),
        pltpu.make_async_copy(w.at[rows - 1, beside], out.at[deep:], sem.at[1]),
    ]
    for copy in copies:
        copy.start()
    for copy in copies:
        copy.wait()


def pack_row(u, w):
    _, cols, members, cells = u.shape
    shape = (cols * members + w.shape[2], cells)
    return pl.pallas_call(
        pack_row_kernel,
        out_shape=pltpu.VMEM(shape, u.dtype),
        in_specs=[HBM, HBM],
        out_specs=VMEM,
        scratch_shapes=[pltpu.SemaphoreType.DMA((2,))],
        cost_estimate=pl.CostEstimate(flops=0, bytes_accessed=4 * shape[0] * cells, transcendentals=0),
        name="pack_row",
    )(u, w)


def pack_rest_kernel(w, outside, out, plain):
    rows, cols, width, _ = w.shape
    skip = 1 - even_column().astype(jnp.int32)
    for q in range(cols - 1):
        out[q * width : (q + 1) * width] = w[rows - 1, q + skip]
    start = (cols - 1) * width
    out[start:] = outside[rows - 1, : out.shape[0] - start]
    plain[...] = w[rows - 1]


def pack_rest(w, outside, members):
    _, cols, width, cells = w.shape
    return pl.pallas_call(
        pack_rest_kernel,
        out_shape=(
            jax.ShapeDtypeStruct(((cols - 1) * width + members + width, cells), w.dtype),
            jax.ShapeDtypeStruct((cols, width, cells), w.dtype),
        ),
        in_specs=[VMEM, VMEM],
        out_specs=(VMEM, VMEM),
        compiler_params=pltpu.CompilerParams(vmem_limit_bytes=GRANT),
        cost_estimate=pl.CostEstimate(flops=0, bytes_accessed=8 * cols * width * cells, transcendentals=0),
        name="pack_rest",
    )(w, outside)


def pack_columns_kernel(u, w, live, index, packed, inner_side, outer_side, sem):
    del packed
    rows, cols, members, cells = u.shape
    deep = members + w.shape[2]
    turn = (cols - 1) * even_column().astype(jnp.int32)
    copies = []
    for n, (out, b) in enumerate(((inner_side, turn), (outer_side, cols - 1 - turn))):
        copies.append(pltpu.make_async_copy(u.at[:, b], out.at[:, :members], sem.at[n, 0]))
        copies.append(pltpu.make_async_copy(w.at[:, b], out.at[:, members:deep], sem.at[n, 1]))
    for copy in copies:
        copy.start()
    for a in range(rows):
        lines = jnp.concatenate([live[a], index[a]], 0).astype(jnp.float32)
        blank = jnp.zeros((2 * cols, cells - live.shape[2]), jnp.float32)
        note = jnp.concatenate([lines, blank], 1).astype(jnp.bfloat16)
        inner_side[a, deep:] = note
        outer_side[a, deep:] = note
    for copy in copies:
        copy.wait()


def pack_columns(u, w, live, index, packed):
    rows, cols, members, cells = u.shape
    shape = (rows, members + w.shape[2] + 2 * cols, cells)
    return pl.pallas_call(
        pack_columns_kernel,
        out_shape=(jax.ShapeDtypeStruct(shape, u.dtype),) * 2,
        in_specs=[ANY, ANY, VMEM, VMEM, VMEM],
        out_specs=(VMEM, VMEM),
        scratch_shapes=[pltpu.SemaphoreType.DMA((2, 2))],
        compiler_params=pltpu.CompilerParams(vmem_limit_bytes=GRANT),
        cost_estimate=pl.CostEstimate(flops=0, bytes_accessed=8 * rows * shape[1] * cells, transcendentals=0),
        name="pack_columns",
    )(u, w, live, index, packed)


def down(row, col, chosen):
    wide = lax.axis_size(col)
    return [(r * wide + c, (r + 1) * wide + c) for r in range(lax.axis_size(row) - 1) for c in chosen]


def body(u, w, live, index, tapers):
    wide = lax.axis_size("col")
    packed = pack_row(u, w)
    s = lax.ppermute(packed, "row", forward("row"))
    inner_side, outer_side = pack_columns(u, w, live, index, packed)
    outside = lax.ppermute(outer_side, "col", swaps("col", 1))
    inside = lax.ppermute(inner_side, "col", swaps("col", 0))
    inc, outside, inside = lax.optimization_barrier((inner(u, w, live, index, tapers), outside, inside))
    rest, plain = pack_rest(w, outside, u.shape[2])
    rest = lax.ppermute(rest, ("row", "col"), down("row", "col", range(1, wide - 1)))
    plain = lax.ppermute(plain, ("row", "col"), down("row", "col", sorted({0, wide - 1})))
    back, held, to_inside, tail = above(s, u, w, inside, outside, live, index, tapers)
    back = lax.ppermute(back, "row", backward("row"))
    from_inside = lax.ppermute(to_inside, "col", swaps("col", 0))
    side = columns(u, w, inside, outside, live, index, tapers)
    inc, top, low = outer(inc, side, held, tail, rest, plain, u, live, index, tapers)
    return finish(inc, top, low, back, from_inside)


def solution(mesh):
    return jax.shard_map(
        body,
        mesh=mesh,
        in_specs=(
            P("row", "col", None, None),
            P("row", "col", None, None),
            P("row", "col", None),
            P("row", "col", None),
            P(),
        ),
        out_specs=P("row", "col", None, None),
        check_vma=False,
    )
```

```python
import jax
import jax.numpy as jnp
from jax import lax
from jax.experimental import pallas as pl
from jax.experimental.pallas import tpu as pltpu
from jax.sharding import PartitionSpec as P

MEMBERS = 256
GRANT = 16 << 20
SCALE = 1.0 / (MEMBERS - 1)
TN = (((0,), (0,)), ((), ()))
NT = (((1,), (1,)), ((), ()))
NN = (((1,), (0,)), ((), ()))
VMEM = pl.BlockSpec(memory_space=pltpu.VMEM)
ANY = pl.BlockSpec(memory_space=pl.ANY)
HBM = pl.BlockSpec(memory_space=pltpu.HBM)


def dot(a, b, dims):
    return lax.dot_general(a, b, dims, preferred_element_type=jnp.float32)


def cat(parts, axis):
    return parts[0] if len(parts) == 1 else jnp.concatenate(parts, axis=axis)


def tapered(gram, rho, live):
    factor = live.astype(jnp.float32) * SCALE
    return (rho.astype(jnp.float32) * gram * factor).astype(jnp.bfloat16)


def even_column():
    return lax.rem(lax.axis_index("col"), 2) == 0


def sides(inside, outside):
    even = even_column()
    return (
        lambda *at: jnp.where(even, outside[at], inside[at]),
        lambda *at: jnp.where(even, inside[at], outside[at]),
    )


def inner_kernel(u, w, live, index, tapers, out, turned, flipped, sym, held):
    rows, cols, _, cells = u.shape
    for n in range(tapers.shape[0]):
        t = tapers[n].astype(jnp.float32)
        sym[n] = 0.5 * (t + t.T)
        flipped[n] = t.T.astype(jnp.bfloat16)

    def ahead(a, b, last):
        near = [(4, a, b)]
        if b + 1 < cols:
            near.append((5, a, b + 1))
        if not last:
            for k in (6, 7, 8):
                if 0 <= b + k - 7 < cols:
                    near.append((k, a + 1, b + k - 7))
        return near

    def row(a, last):
        on, which = live[a], index[a]
        for b in range(cols):
            near = ahead(a, b, last)
            side_on = u[a, b].T
            turned[a, b] = side_on
            gram = dot(side_on, cat([u[p, q] for _, p, q in near], 1), NN)
            for n, (k, _, _) in enumerate(near):
                at = which[b, k]
                rho = sym[at] if k == 4 else tapers[at]
                held[b, :, (k - 4) * cells : (k - 3) * cells] = tapered(
                    gram[:, n * cells : (n + 1) * cells], rho, on[b, k]
                )
        for b in range(cols):
            near = ahead(a, b, last)
            total = dot(
                cat([w[p, q] for _, p, q in near], 1),
                cat([held[b, :, (k - 4) * cells : (k - 3) * cells] for k, _, _ in near], 1),
                NT,
            )
            if b > 0:
                total += dot(w[a, b - 1], held[b - 1, :, cells : 2 * cells], NN)
            out[a, b] += total
            if not last:
                back = [(k, b - (k - 7)) for k in (6, 7, 8) if 0 <= b - (k - 7) < cols]
                out[a + 1, b] = dot(
                    cat([w[a, q] for _, q in back], 1),
                    cat([held[q, :, (k - 4) * cells : (k - 3) * cells] for k, q in back], 0),
                    NN,
                )

    out[0] = jnp.zeros_like(out[0])

    @pl.loop(0, rows - 1)
    def _(a):
        row(a, False)

    row(rows - 1, True)


def inner(u, w, live, index, tapers):
    rows, cols, members, cells = u.shape
    columns = w.shape[2]
    pairs = 5 * rows * cols
    return pl.pallas_call(
        inner_kernel,
        out_shape=(
            jax.ShapeDtypeStruct((rows, cols, columns, cells), jnp.float32),
            jax.ShapeDtypeStruct((rows, cols, cells, members), jnp.bfloat16),
            jax.ShapeDtypeStruct(tapers.shape, jnp.bfloat16),
        ),
        in_specs=[VMEM] * 5,
        out_specs=(VMEM,) * 3,
        scratch_shapes=[
            pltpu.VMEM(tapers.shape, jnp.float32),
            pltpu.VMEM((cols, cells, 5 * cells), jnp.bfloat16),
        ],
        compiler_params=pltpu.CompilerParams(vmem_limit_bytes=GRANT),
        cost_estimate=pl.CostEstimate(
            flops=2 * pairs * cells * cells * (members + 2 * columns),
            bytes_accessed=4 << 20,
            transcendentals=0,
        ),
        name="inner",
    )(u, w, live, index, tapers)


def above_kernel(s, turned, w, inside, outside, live, index, flipped, back, held, to_inside, tail):
    _, cols, cells, members = turned.shape
    deep = members + w.shape[2]
    last = cols - 1
    left, right = sides(inside, outside)
    on, which = live[0], index[0]

    def upper(c):
        return s[c * members : (c + 1) * members]

    beyond = {}
    for q, near, k, line in ((-1, left, 2, last), (cols, right, 0, 0)):
        note = near(0, slice(deep, None)).astype(jnp.int32)
        gram = dot(near(0, slice(0, members)), upper(min(max(q, 0), last)), TN)
        block = tapered(gram, flipped[note[cols + line, k]], note[line, k])
        beyond[q] = block, near(0, slice(members, deep))
    for q in range(cols):
        near = [c for c in (q - 1, q, q + 1) if 0 <= c < cols]
        gram = dot(turned[0, q], cat([upper(c) for c in near], 1), NN)
        for n, c in enumerate(near):
            k = 1 + c - q
            held[q, :, k * cells : (k + 1) * cells] = tapered(
                gram[:, n * cells : (n + 1) * cells], flipped[which[q, k]], on[q, k]
            )
    for c in range(cols):
        blocks, weights = [], []
        for q in (c - 1, c, c + 1):
            if q in beyond:
                block, weight = beyond[q]
            else:
                k = 1 + c - q
                block, weight = held[q, :, k * cells : (k + 1) * cells], w[0, q]
            blocks.append(block)
            weights.append(weight)
        back[c] = dot(cat(weights, 1), cat(blocks, 0), NN).astype(jnp.bfloat16)
    tail[...] = s[cols * members :]
    to_inside[...] = dot(s[cols * members :], jnp.where(even_column(), beyond[cols][0], beyond[-1][0]), NT)


def above(s, turned, w, inside, outside, live, index, flipped):
    _, cols, cells, members = turned.shape
    columns = w.shape[2]
    return pl.pallas_call(
        above_kernel,
        out_shape=(
            jax.ShapeDtypeStruct((cols, columns, cells), jnp.bfloat16),
            jax.ShapeDtypeStruct((cols, cells, 3 * cells), jnp.bfloat16),
            jax.ShapeDtypeStruct((columns, cells), jnp.float32),
            jax.ShapeDtypeStruct((columns, cells), jnp.bfloat16),
        ),
        in_specs=[VMEM] * 8,
        out_specs=(VMEM,) * 4,
        compiler_params=pltpu.CompilerParams(vmem_limit_bytes=GRANT),
        cost_estimate=pl.CostEstimate(
            flops=2 * 3 * cols * cells * cells * (members + columns),
            bytes_accessed=2 << 20,
            transcendentals=0,
        ),
        name="above",
    )(s, turned, w, inside, outside, live, index, flipped)


def columns_kernel(u, w, inside, outside, live, index, tapers, side):
    rows, cols, members, cells = u.shape
    deep = members + w.shape[2]
    last = cols - 1
    left, right = sides(inside, outside)
    on = [live[a] for a in range(rows)]
    which = [index[a] for a in range(rows)]
    total = {}

    def add(a, q, value):
        total[a, q] = total[a, q] + value if (a, q) in total else value

    for a in range(rows):
        near = [(5, a)] + ([(8, a + 1)] if a + 1 < rows else [])
        gram = dot(left(a, slice(0, members)), cat([u[p, 0] for _, p in near], 1), TN)
        blocks = cat(
            [
                tapered(gram[:, n * cells : (n + 1) * cells], tapers[which[p][0, 8 - k]], on[p][0, 8 - k])
                for n, (k, p) in enumerate(near)
            ],
            1,
        )
        both = dot(left(a, slice(members, deep)), blocks, NN)
        for n, (_, p) in enumerate(near):
            add(p, 0, both[:, n * cells : (n + 1) * cells])
        gram = dot(u[a, last], cat([right(p, slice(0, members)) for _, p in near], 1), TN)
        blocks = cat(
            [
                tapered(gram[:, n * cells : (n + 1) * cells], tapers[which[a][last, k]], on[a][last, k])
                for n, (k, _) in enumerate(near)
            ],
            1,
        )
        add(a, last, dot(cat([right(p, slice(members, deep)) for _, p in near], 1), blocks, NT))
        if a + 1 < rows:
            gram = dot(u[a, 0], left(a + 1, slice(0, members)), TN)
            block = tapered(gram, tapers[which[a][0, 6]], on[a][0, 6])
            add(a, 0, dot(left(a + 1, slice(members, deep)), block, NT))
            gram = dot(right(a, slice(0, members)), u[a + 1, last], TN)
            block = tapered(gram, tapers[which[a + 1][last, 2]], on[a + 1][last, 2])
            add(a + 1, last, dot(right(a, slice(members, deep)), block, NN))

    for a in range(rows):
        side[0, a] = total[a, 0]
        side[1, a] = total[a, last]


def columns(u, w, inside, outside, live, index, tapers):
    rows, _, members, cells = u.shape
    width = w.shape[2]
    return pl.pallas_call(
        columns_kernel,
        out_shape=jax.ShapeDtypeStruct((2, rows, width, cells), jnp.float32),
        in_specs=[VMEM] * 7,
        out_specs=VMEM,
        compiler_params=pltpu.CompilerParams(vmem_limit_bytes=GRANT),
        cost_estimate=pl.CostEstimate(
            flops=12 * rows * cells * cells * (members + width), bytes_accessed=2 << 20, transcendentals=0
        ),
        name="columns",
    )(u, w, inside, outside, live, index, tapers)


def outer_kernel(inc, side, held, tail, rest, u, live, index, tapers, out, top, low):
    rows, cols, members, cells = u.shape
    width = inc.shape[2]
    last = cols - 1
    even = even_column()
    on, which = live[0], index[0]
    start = (cols - 1) * width
    gram = dot(rest[start : start + members], jnp.where(even, u[0, 0], u[0, last]), TN)
    at = jnp.where(even, which[0, 0], which[last, 2])
    block = tapered(gram, tapers[at], jnp.where(even, on[0, 0], on[last, 2]))
    far = dot(rest[start + members :], block, NN)
    blank = jnp.zeros_like(far)
    parts = [rest[c * width : (c + 1) * width] for c in range(cols - 1)]
    tail = tail[...]
    weights = [jnp.where(even, parts[0], tail)]
    weights += [jnp.where(even, parts[c], parts[c - 1]) for c in range(1, last)]
    weights.append(jnp.where(even, tail, parts[last - 1]))
    for q in range(cols):
        near = [c for c in (q - 1, q, q + 1) if 0 <= c < cols]
        block = held[q, :, (1 + near[0] - q) * cells : (2 + near[-1] - q) * cells]
        value = inc[0, q] + dot(cat([weights[c] for c in near], 1), block, NT)
        if q in (0, last):
            value += side[q // last, 0]
            value += jnp.where(even, far, blank) if q == 0 else jnp.where(even, blank, far)
            top[q // last] = value
        out[0, q] = value
    for a in range(1, rows):
        for q in range(cols):
            value = inc[a, q] + side[q // last, a] if q in (0, last) else inc[a, q]
            out[a, q] = value
            if a == rows - 1:
                low[q] = value


def outer(inc, side, held, tail, rest, u, live, index, tapers):
    rows, cols, width, cells = inc.shape
    return pl.pallas_call(
        outer_kernel,
        out_shape=(
            jax.ShapeDtypeStruct(inc.shape, inc.dtype),
            jax.ShapeDtypeStruct((2, width, cells), inc.dtype),
            jax.ShapeDtypeStruct(inc.shape[1:], inc.dtype),
        ),
        in_specs=[VMEM] * 9,
        out_specs=(VMEM,) * 3,
        compiler_params=pltpu.CompilerParams(vmem_limit_bytes=GRANT),
        cost_estimate=pl.CostEstimate(flops=6 * cols * cells * cells * width, bytes_accessed=4 << 20, transcendentals=0),
        name="outer",
    )(inc, side, held, tail, rest, u, live, index, tapers)


def finish_kernel(inc, top, low, back, from_inside, out, end, total, sem):
    del inc
    rows, cols = out.shape[:2]
    half = cols // 2
    side = even_column().astype(jnp.int32)
    copies = []
    for n, part in enumerate((slice(0, half), slice(half, cols))):
        total[part] = low[part] + back[part].astype(jnp.float32)
        copies.append(pltpu.make_async_copy(total.at[part], out.at[rows - 1, part], sem.at[n]))
        copies[-1].start()
    end[...] = top[side] + from_inside[...]
    copies.append(pltpu.make_async_copy(end, out.at[0, side * (cols - 1)], sem.at[2]))
    copies[-1].start()
    for copy in copies:
        copy.wait()


def finish(inc, top, low, back, from_inside):
    return pl.pallas_call(
        finish_kernel,
        out_shape=jax.ShapeDtypeStruct(inc.shape, inc.dtype),
        in_specs=[ANY] + [VMEM] * 4,
        out_specs=ANY,
        scratch_shapes=[
            pltpu.VMEM(top.shape[1:], top.dtype),
            pltpu.VMEM(low.shape, low.dtype),
            pltpu.SemaphoreType.DMA((3,)),
        ],
        input_output_aliases={0: 0},
        compiler_params=pltpu.CompilerParams(vmem_limit_bytes=GRANT),
        cost_estimate=pl.CostEstimate(flops=low.size, bytes_accessed=10 * low.size, transcendentals=0),
        name="finish",
    )(inc, top, low, back, from_inside)


def forward(axis):
    return [(i, i + 1) for i in range(lax.axis_size(axis) - 1)]


def swaps(axis, start):
    pairs = [(i, i + 1) for i in range(start, lax.axis_size(axis) - 1, 2)]
    return pairs + [(b, a) for a, b in pairs]


def backward(axis):
    return [(i + 1, i) for i in range(lax.axis_size(axis) - 1)]


def pack_row_kernel(u, w, out, sem):
    rows, cols, members, cells = u.shape
    beside = (cols - 1) * even_column().astype(jnp.int32)
    deep = cols * members
    copies = [
        pltpu.make_async_copy(u.at[rows - 1].reshape(deep, cells), out.at[:deep], sem.at[0]),
        pltpu.make_async_copy(w.at[rows - 1, beside], out.at[deep:], sem.at[1]),
    ]
    for copy in copies:
        copy.start()
    for copy in copies:
        copy.wait()


def pack_row(u, w):
    _, cols, members, cells = u.shape
    shape = (cols * members + w.shape[2], cells)
    return pl.pallas_call(
        pack_row_kernel,
        out_shape=pltpu.VMEM(shape, u.dtype),
        in_specs=[HBM, HBM],
        out_specs=VMEM,
        scratch_shapes=[pltpu.SemaphoreType.DMA((2,))],
        cost_estimate=pl.CostEstimate(flops=0, bytes_accessed=4 * shape[0] * cells, transcendentals=0),
        name="pack_row",
    )(u, w)


def pack_rest_kernel(w, outside, out):
    rows, cols, width, _ = w.shape
    skip = 1 - even_column().astype(jnp.int32)
    for q in range(cols - 1):
        out[q * width : (q + 1) * width] = w[rows - 1, q + skip]
    start = (cols - 1) * width
    out[start:] = outside[rows - 1, : out.shape[0] - start]


def pack_rest(w, outside, members):
    _, cols, width, cells = w.shape
    return pl.pallas_call(
        pack_rest_kernel,
        out_shape=jax.ShapeDtypeStruct(((cols - 1) * width + members + width, cells), w.dtype),
        in_specs=[VMEM, VMEM],
        out_specs=VMEM,
        compiler_params=pltpu.CompilerParams(vmem_limit_bytes=GRANT),
        cost_estimate=pl.CostEstimate(flops=0, bytes_accessed=8 * cols * width * cells, transcendentals=0),
        name="pack_rest",
    )(w, outside)


def pack_columns_kernel(u, w, live, index, packed, inner_side, outer_side, sem):
    del packed
    rows, cols, members, cells = u.shape
    deep = members + w.shape[2]
    turn = (cols - 1) * even_column().astype(jnp.int32)
    copies = []
    for n, (out, b) in enumerate(((inner_side, turn), (outer_side, cols - 1 - turn))):
        copies.append(pltpu.make_async_copy(u.at[:, b], out.at[:, :members], sem.at[n, 0]))
        copies.append(pltpu.make_async_copy(w.at[:, b], out.at[:, members:deep], sem.at[n, 1]))
    for copy in copies:
        copy.start()
    for a in range(rows):
        lines = jnp.concatenate([live[a], index[a]], 0).astype(jnp.float32)
        blank = jnp.zeros((2 * cols, cells - live.shape[2]), jnp.float32)
        note = jnp.concatenate([lines, blank], 1).astype(jnp.bfloat16)
        inner_side[a, deep:] = note
        outer_side[a, deep:] = note
    for copy in copies:
        copy.wait()


def pack_columns(u, w, live, index, packed):
    rows, cols, members, cells = u.shape
    shape = (rows, members + w.shape[2] + 2 * cols, cells)
    return pl.pallas_call(
        pack_columns_kernel,
        out_shape=(jax.ShapeDtypeStruct(shape, u.dtype),) * 2,
        in_specs=[ANY, ANY, VMEM, VMEM, VMEM],
        out_specs=(VMEM, VMEM),
        scratch_shapes=[pltpu.SemaphoreType.DMA((2, 2))],
        compiler_params=pltpu.CompilerParams(vmem_limit_bytes=GRANT),
        cost_estimate=pl.CostEstimate(flops=0, bytes_accessed=8 * rows * shape[1] * cells, transcendentals=0),
        name="pack_columns",
    )(u, w, live, index, packed)


def body(u, w, live, index, tapers):
    packed = pack_row(u, w)
    s = lax.ppermute(packed, "row", forward("row"))
    inner_side, outer_side = pack_columns(u, w, live, index, packed)
    outside = lax.ppermute(outer_side, "col", swaps("col", 1))
    inside = lax.ppermute(inner_side, "col", swaps("col", 0))
    inc, turned, flipped = inner(u, w, live, index, tapers)
    inc, outside, inside = lax.optimization_barrier((inc, outside, inside))
    rest = lax.ppermute(pack_rest(w, outside, u.shape[2]), "row", forward("row"))
    back, held, to_inside, tail = above(s, turned, w, inside, outside, live, index, flipped)
    back = lax.ppermute(back, "row", backward("row"))
    from_inside = lax.ppermute(to_inside, "col", swaps("col", 0))
    side = columns(u, w, inside, outside, live, index, tapers)
    inc, top, low = outer(inc, side, held, tail, rest, u, live, index, tapers)
    return finish(inc, top, low, back, from_inside)


def solution(mesh):
    return jax.shard_map(
        body,
        mesh=mesh,
        in_specs=(
            P("row", "col", None, None),
            P("row", "col", None, None),
            P("row", "col", None),
            P("row", "col", None),
            P(),
        ),
        out_specs=P("row", "col", None, None),
        check_vma=False,
    )
```

```python
import jax
import jax.numpy as jnp
from jax import lax
from jax.experimental import pallas as pl
from jax.experimental.pallas import tpu as pltpu
from jax.sharding import PartitionSpec as P

MEMBERS = 256
GRANT = 16 << 20
SCALE = 1.0 / (MEMBERS - 1)
TN = (((0,), (0,)), ((), ()))
NT = (((1,), (1,)), ((), ()))
NN = (((1,), (0,)), ((), ()))
VMEM = pl.BlockSpec(memory_space=pltpu.VMEM)
ANY = pl.BlockSpec(memory_space=pl.ANY)
HBM = pl.BlockSpec(memory_space=pltpu.HBM)


def dot(a, b, dims):
    return lax.dot_general(a, b, dims, preferred_element_type=jnp.float32)


def cat(parts, axis):
    return parts[0] if len(parts) == 1 else jnp.concatenate(parts, axis=axis)


def tapered(gram, rho, live):
    factor = live.astype(jnp.float32) * SCALE
    return (rho.astype(jnp.float32) * gram * factor).astype(jnp.bfloat16)


def even_column():
    return lax.rem(lax.axis_index("col"), 2) == 0


def sides(inside, outside):
    even = even_column()
    return (
        lambda *at: jnp.where(even, outside[at], inside[at]),
        lambda *at: jnp.where(even, inside[at], outside[at]),
    )


def inner_kernel(u, w, live, index, tapers, out, turned, flipped, sym, held):
    rows, cols, _, cells = u.shape
    for n in range(tapers.shape[0]):
        t = tapers[n].astype(jnp.float32)
        sym[n] = 0.5 * (t + t.T)
        flipped[n] = t.T.astype(jnp.bfloat16)

    def ahead(a, b, last):
        near = [(4, a, b)]
        if b + 1 < cols:
            near.append((5, a, b + 1))
        if not last:
            for k in (6, 7, 8):
                if 0 <= b + k - 7 < cols:
                    near.append((k, a + 1, b + k - 7))
        return near

    for a in range(rows):
        last = a == rows - 1
        on, which = live[a], index[a]
        for b in range(cols):
            near = ahead(a, b, last)
            side_on = u[a, b].T
            turned[a, b] = side_on
            gram = dot(side_on, cat([u[p, q] for _, p, q in near], 1), NN)
            for n, (k, _, _) in enumerate(near):
                at = which[b, k]
                rho = sym[at] if k == 4 else tapers[at]
                held[a % 2, b, :, (k - 4) * cells : (k - 3) * cells] = tapered(
                    gram[:, n * cells : (n + 1) * cells], rho, on[b, k]
                )
        for b in range(cols):
            near = ahead(a, b, last)
            total = dot(
                cat([w[p, q] for _, p, q in near], 1),
                cat([held[a % 2, b, :, (k - 4) * cells : (k - 3) * cells] for k, _, _ in near], 1),
                NT,
            )
            behind = [(5, a, b - 1)] if b > 0 else []
            if a > 0:
                behind += [(k, a - 1, b - (k - 7)) for k in (6, 7, 8) if 0 <= b - (k - 7) < cols]
            if behind:
                total += dot(
                    cat([w[p, q] for _, p, q in behind], 1),
                    cat([held[p % 2, q, :, (k - 4) * cells : (k - 3) * cells] for k, p, q in behind], 0),
                    NN,
                )
            out[a, b] = total


def inner(u, w, live, index, tapers):
    rows, cols, members, cells = u.shape
    columns = w.shape[2]
    pairs = 5 * rows * cols
    return pl.pallas_call(
        inner_kernel,
        out_shape=(
            jax.ShapeDtypeStruct((rows, cols, columns, cells), jnp.float32),
            jax.ShapeDtypeStruct((rows, cols, cells, members), jnp.bfloat16),
            jax.ShapeDtypeStruct(tapers.shape, jnp.bfloat16),
        ),
        in_specs=[VMEM] * 5,
        out_specs=(VMEM,) * 3,
        scratch_shapes=[
            pltpu.VMEM(tapers.shape, jnp.float32),
            pltpu.VMEM((2, cols, cells, 5 * cells), jnp.bfloat16),
        ],
        compiler_params=pltpu.CompilerParams(vmem_limit_bytes=GRANT),
        cost_estimate=pl.CostEstimate(
            flops=2 * pairs * cells * cells * (members + 2 * columns),
            bytes_accessed=4 << 20,
            transcendentals=0,
        ),
        name="inner",
    )(u, w, live, index, tapers)


def above_kernel(s, turned, w, inside, outside, live, index, flipped, back, held, to_inside, tail):
    _, cols, cells, members = turned.shape
    deep = members + w.shape[2]
    last = cols - 1
    left, right = sides(inside, outside)
    on, which = live[0], index[0]

    def upper(c):
        return s[c * members : (c + 1) * members]

    beyond = {}
    for q, near, k, line in ((-1, left, 2, last), (cols, right, 0, 0)):
        note = near(0, slice(deep, None)).astype(jnp.int32)
        gram = dot(near(0, slice(0, members)), upper(min(max(q, 0), last)), TN)
        block = tapered(gram, flipped[note[cols + line, k]], note[line, k])
        beyond[q] = block, near(0, slice(members, deep))
    for q in range(cols):
        near = [c for c in (q - 1, q, q + 1) if 0 <= c < cols]
        gram = dot(turned[0, q], cat([upper(c) for c in near], 1), NN)
        for n, c in enumerate(near):
            k = 1 + c - q
            held[q, :, k * cells : (k + 1) * cells] = tapered(
                gram[:, n * cells : (n + 1) * cells], flipped[which[q, k]], on[q, k]
            )
    for c in range(cols):
        blocks, weights = [], []
        for q in (c - 1, c, c + 1):
            if q in beyond:
                block, weight = beyond[q]
            else:
                k = 1 + c - q
                block, weight = held[q, :, k * cells : (k + 1) * cells], w[0, q]
            blocks.append(block)
            weights.append(weight)
        back[c] = dot(cat(weights, 1), cat(blocks, 0), NN).astype(jnp.bfloat16)
    tail[...] = s[cols * members :]
    to_inside[...] = dot(s[cols * members :], jnp.where(even_column(), beyond[cols][0], beyond[-1][0]), NT)


def above(s, turned, w, inside, outside, live, index, flipped):
    _, cols, cells, members = turned.shape
    columns = w.shape[2]
    return pl.pallas_call(
        above_kernel,
        out_shape=(
            jax.ShapeDtypeStruct((cols, columns, cells), jnp.bfloat16),
            jax.ShapeDtypeStruct((cols, cells, 3 * cells), jnp.bfloat16),
            jax.ShapeDtypeStruct((columns, cells), jnp.float32),
            jax.ShapeDtypeStruct((columns, cells), jnp.bfloat16),
        ),
        in_specs=[VMEM] * 8,
        out_specs=(VMEM,) * 4,
        compiler_params=pltpu.CompilerParams(vmem_limit_bytes=GRANT),
        cost_estimate=pl.CostEstimate(
            flops=2 * 3 * cols * cells * cells * (members + columns),
            bytes_accessed=2 << 20,
            transcendentals=0,
        ),
        name="above",
    )(s, turned, w, inside, outside, live, index, flipped)


def columns_kernel(u, w, inside, outside, live, index, tapers, side):
    rows, cols, members, cells = u.shape
    deep = members + w.shape[2]
    last = cols - 1
    left, right = sides(inside, outside)
    on = [live[a] for a in range(rows)]
    which = [index[a] for a in range(rows)]
    total = {}

    def add(a, q, value):
        total[a, q] = total[a, q] + value if (a, q) in total else value

    for a in range(rows):
        near = [(5, a)] + ([(8, a + 1)] if a + 1 < rows else [])
        gram = dot(left(a, slice(0, members)), cat([u[p, 0] for _, p in near], 1), TN)
        blocks = cat(
            [
                tapered(gram[:, n * cells : (n + 1) * cells], tapers[which[p][0, 8 - k]], on[p][0, 8 - k])
                for n, (k, p) in enumerate(near)
            ],
            1,
        )
        both = dot(left(a, slice(members, deep)), blocks, NN)
        for n, (_, p) in enumerate(near):
            add(p, 0, both[:, n * cells : (n + 1) * cells])
        gram = dot(u[a, last], cat([right(p, slice(0, members)) for _, p in near], 1), TN)
        blocks = cat(
            [
                tapered(gram[:, n * cells : (n + 1) * cells], tapers[which[a][last, k]], on[a][last, k])
                for n, (k, _) in enumerate(near)
            ],
            1,
        )
        add(a, last, dot(cat([right(p, slice(members, deep)) for _, p in near], 1), blocks, NT))
        if a + 1 < rows:
            gram = dot(u[a, 0], left(a + 1, slice(0, members)), TN)
            block = tapered(gram, tapers[which[a][0, 6]], on[a][0, 6])
            add(a, 0, dot(left(a + 1, slice(members, deep)), block, NT))
            gram = dot(right(a, slice(0, members)), u[a + 1, last], TN)
            block = tapered(gram, tapers[which[a + 1][last, 2]], on[a + 1][last, 2])
            add(a + 1, last, dot(right(a, slice(members, deep)), block, NN))

    for a in range(rows):
        side[0, a] = total[a, 0]
        side[1, a] = total[a, last]


def columns(u, w, inside, outside, live, index, tapers):
    rows, _, members, cells = u.shape
    width = w.shape[2]
    return pl.pallas_call(
        columns_kernel,
        out_shape=jax.ShapeDtypeStruct((2, rows, width, cells), jnp.float32),
        in_specs=[VMEM] * 7,
        out_specs=VMEM,
        compiler_params=pltpu.CompilerParams(vmem_limit_bytes=GRANT),
        cost_estimate=pl.CostEstimate(
            flops=12 * rows * cells * cells * (members + width), bytes_accessed=2 << 20, transcendentals=0
        ),
        name="columns",
    )(u, w, inside, outside, live, index, tapers)


def outer_kernel(inc, side, held, tail, rest, u, live, index, tapers, out, top, low):
    rows, cols, members, cells = u.shape
    width = inc.shape[2]
    last = cols - 1
    even = even_column()
    on, which = live[0], index[0]
    start = (cols - 1) * width
    gram = dot(rest[start : start + members], jnp.where(even, u[0, 0], u[0, last]), TN)
    at = jnp.where(even, which[0, 0], which[last, 2])
    block = tapered(gram, tapers[at], jnp.where(even, on[0, 0], on[last, 2]))
    far = dot(rest[start + members :], block, NN)
    blank = jnp.zeros_like(far)
    parts = [rest[c * width : (c + 1) * width] for c in range(cols - 1)]
    tail = tail[...]
    weights = [jnp.where(even, parts[0], tail)]
    weights += [jnp.where(even, parts[c], parts[c - 1]) for c in range(1, last)]
    weights.append(jnp.where(even, tail, parts[last - 1]))
    for q in range(cols):
        near = [c for c in (q - 1, q, q + 1) if 0 <= c < cols]
        block = held[q, :, (1 + near[0] - q) * cells : (2 + near[-1] - q) * cells]
        value = inc[0, q] + dot(cat([weights[c] for c in near], 1), block, NT)
        if q in (0, last):
            value += side[q // last, 0]
            value += jnp.where(even, far, blank) if q == 0 else jnp.where(even, blank, far)
            top[q // last] = value
        out[0, q] = value
    for a in range(1, rows):
        for q in range(cols):
            value = inc[a, q] + side[q // last, a] if q in (0, last) else inc[a, q]
            out[a, q] = value
            if a == rows - 1:
                low[q] = value


def outer(inc, side, held, tail, rest, u, live, index, tapers):
    rows, cols, width, cells = inc.shape
    return pl.pallas_call(
        outer_kernel,
        out_shape=(
            jax.ShapeDtypeStruct(inc.shape, inc.dtype),
            jax.ShapeDtypeStruct((2, width, cells), inc.dtype),
            jax.ShapeDtypeStruct(inc.shape[1:], inc.dtype),
        ),
        in_specs=[VMEM] * 9,
        out_specs=(VMEM,) * 3,
        compiler_params=pltpu.CompilerParams(vmem_limit_bytes=GRANT),
        cost_estimate=pl.CostEstimate(flops=6 * cols * cells * cells * width, bytes_accessed=4 << 20, transcendentals=0),
        name="outer",
    )(inc, side, held, tail, rest, u, live, index, tapers)


def finish_kernel(inc, top, low, back, from_inside, out, end, total, sem):
    del inc
    rows, cols = out.shape[:2]
    half = cols // 2
    side = even_column().astype(jnp.int32)
    copies = []
    for n, part in enumerate((slice(0, half), slice(half, cols))):
        total[part] = low[part] + back[part].astype(jnp.float32)
        copies.append(pltpu.make_async_copy(total.at[part], out.at[rows - 1, part], sem.at[n]))
        copies[-1].start()
    end[...] = top[side] + from_inside[...]
    copies.append(pltpu.make_async_copy(end, out.at[0, side * (cols - 1)], sem.at[2]))
    copies[-1].start()
    for copy in copies:
        copy.wait()


def finish(inc, top, low, back, from_inside):
    return pl.pallas_call(
        finish_kernel,
        out_shape=jax.ShapeDtypeStruct(inc.shape, inc.dtype),
        in_specs=[ANY] + [VMEM] * 4,
        out_specs=ANY,
        scratch_shapes=[
            pltpu.VMEM(top.shape[1:], top.dtype),
            pltpu.VMEM(low.shape, low.dtype),
            pltpu.SemaphoreType.DMA((3,)),
        ],
        input_output_aliases={0: 0},
        compiler_params=pltpu.CompilerParams(vmem_limit_bytes=GRANT),
        cost_estimate=pl.CostEstimate(flops=low.size, bytes_accessed=10 * low.size, transcendentals=0),
        name="finish",
    )(inc, top, low, back, from_inside)


def forward(axis):
    return [(i, i + 1) for i in range(lax.axis_size(axis) - 1)]


def swaps(axis, start):
    pairs = [(i, i + 1) for i in range(start, lax.axis_size(axis) - 1, 2)]
    return pairs + [(b, a) for a, b in pairs]


def backward(axis):
    return [(i + 1, i) for i in range(lax.axis_size(axis) - 1)]


def pack_row_kernel(u, w, out, sem):
    rows, cols, members, cells = u.shape
    beside = (cols - 1) * even_column().astype(jnp.int32)
    deep = cols * members
    copies = [
        pltpu.make_async_copy(u.at[rows - 1].reshape(deep, cells), out.at[:deep], sem.at[0]),
        pltpu.make_async_copy(w.at[rows - 1, beside], out.at[deep:], sem.at[1]),
    ]
    for copy in copies:
        copy.start()
    for copy in copies:
        copy.wait()


def pack_row(u, w):
    _, cols, members, cells = u.shape
    shape = (cols * members + w.shape[2], cells)
    return pl.pallas_call(
        pack_row_kernel,
        out_shape=pltpu.VMEM(shape, u.dtype),
        in_specs=[HBM, HBM],
        out_specs=VMEM,
        scratch_shapes=[pltpu.SemaphoreType.DMA((2,))],
        cost_estimate=pl.CostEstimate(flops=0, bytes_accessed=4 * shape[0] * cells, transcendentals=0),
        name="pack_row",
    )(u, w)


def pack_rest_kernel(w, outside, out):
    rows, cols, width, _ = w.shape
    skip = 1 - even_column().astype(jnp.int32)
    for q in range(cols - 1):
        out[q * width : (q + 1) * width] = w[rows - 1, q + skip]
    start = (cols - 1) * width
    out[start:] = outside[rows - 1, : out.shape[0] - start]


def pack_rest(w, outside, members):
    _, cols, width, cells = w.shape
    return pl.pallas_call(
        pack_rest_kernel,
        out_shape=jax.ShapeDtypeStruct(((cols - 1) * width + members + width, cells), w.dtype),
        in_specs=[VMEM, VMEM],
        out_specs=VMEM,
        compiler_params=pltpu.CompilerParams(vmem_limit_bytes=GRANT),
        cost_estimate=pl.CostEstimate(flops=0, bytes_accessed=8 * cols * width * cells, transcendentals=0),
        name="pack_rest",
    )(w, outside)


def pack_columns_kernel(u, w, live, index, packed, inner_side, outer_side, sem):
    del packed
    rows, cols, members, cells = u.shape
    deep = members + w.shape[2]
    turn = (cols - 1) * even_column().astype(jnp.int32)
    copies = []
    for n, (out, b) in enumerate(((inner_side, turn), (outer_side, cols - 1 - turn))):
        copies.append(pltpu.make_async_copy(u.at[:, b], out.at[:, :members], sem.at[n, 0]))
        copies.append(pltpu.make_async_copy(w.at[:, b], out.at[:, members:deep], sem.at[n, 1]))
    for copy in copies:
        copy.start()
    for a in range(rows):
        lines = jnp.concatenate([live[a], index[a]], 0).astype(jnp.float32)
        blank = jnp.zeros((2 * cols, cells - live.shape[2]), jnp.float32)
        note = jnp.concatenate([lines, blank], 1).astype(jnp.bfloat16)
        inner_side[a, deep:] = note
        outer_side[a, deep:] = note
    for copy in copies:
        copy.wait()


def pack_columns(u, w, live, index, packed):
    rows, cols, members, cells = u.shape
    shape = (rows, members + w.shape[2] + 2 * cols, cells)
    return pl.pallas_call(
        pack_columns_kernel,
        out_shape=(jax.ShapeDtypeStruct(shape, u.dtype),) * 2,
        in_specs=[ANY, ANY, VMEM, VMEM, VMEM],
        out_specs=(VMEM, VMEM),
        scratch_shapes=[pltpu.SemaphoreType.DMA((2, 2))],
        compiler_params=pltpu.CompilerParams(vmem_limit_bytes=GRANT),
        cost_estimate=pl.CostEstimate(flops=0, bytes_accessed=8 * rows * shape[1] * cells, transcendentals=0),
        name="pack_columns",
    )(u, w, live, index, packed)


def body(u, w, live, index, tapers):
    packed = pack_row(u, w)
    s = lax.ppermute(packed, "row", forward("row"))
    inner_side, outer_side = pack_columns(u, w, live, index, packed)
    outside = lax.ppermute(outer_side, "col", swaps("col", 1))
    inside = lax.ppermute(inner_side, "col", swaps("col", 0))
    inc, turned, flipped = inner(u, w, live, index, tapers)
    inc, outside, inside = lax.optimization_barrier((inc, outside, inside))
    rest = lax.ppermute(pack_rest(w, outside, u.shape[2]), "row", forward("row"))
    back, held, to_inside, tail = above(s, turned, w, inside, outside, live, index, flipped)
    back = lax.ppermute(back, "row", backward("row"))
    from_inside = lax.ppermute(to_inside, "col", swaps("col", 0))
    side = columns(u, w, inside, outside, live, index, tapers)
    inc, top, low = outer(inc, side, held, tail, rest, u, live, index, tapers)
    return finish(inc, top, low, back, from_inside)


def solution(mesh):
    return jax.shard_map(
        body,
        mesh=mesh,
        in_specs=(
            P("row", "col", None, None),
            P("row", "col", None, None),
            P("row", "col", None),
            P("row", "col", None),
            P(),
        ),
        out_specs=P("row", "col", None, None),
        check_vma=False,
    )
```

```python
import functools

import jax
import jax.numpy as jnp
from jax import lax
from jax.experimental import pallas as pl
from jax.experimental.pallas import tpu as pltpu
from jax.sharding import PartitionSpec as P

MEMBERS = 256
GRANT = 16 << 20
SCALE = 1.0 / (MEMBERS - 1)
TN = (((0,), (0,)), ((), ()))
NT = (((1,), (1,)), ((), ()))
NN = (((1,), (0,)), ((), ()))
VMEM = pl.BlockSpec(memory_space=pltpu.VMEM)
ANY = pl.BlockSpec(memory_space=pl.ANY)
HBM = pl.BlockSpec(memory_space=pltpu.HBM)


def dot(a, b, dims):
    return lax.dot_general(a, b, dims, preferred_element_type=jnp.float32)


def cat(parts, axis):
    return parts[0] if len(parts) == 1 else jnp.concatenate(parts, axis=axis)


def tapered(gram, rho, live):
    factor = live.astype(jnp.float32) * SCALE
    return (rho.astype(jnp.float32) * gram * factor).astype(jnp.bfloat16)


def even_column():
    return lax.rem(lax.axis_index("col"), 2) == 0


def sides(inside, outside):
    even = even_column()
    return (
        lambda *at: jnp.where(even, outside[at], inside[at]),
        lambda *at: jnp.where(even, inside[at], outside[at]),
    )


def inner_kernel(u, w, live, index, tapers, out, turned, flipped, sym, held):
    rows, cols, _, cells = u.shape
    for n in range(tapers.shape[0]):
        t = tapers[n].astype(jnp.float32)
        sym[n] = 0.5 * (t + t.T)
        flipped[n] = t.T.astype(jnp.bfloat16)

    def ahead(a, b, last):
        near = [(4, a, b)]
        if b + 1 < cols:
            near.append((5, a, b + 1))
        if not last:
            for k in (6, 7, 8):
                if 0 <= b + k - 7 < cols:
                    near.append((k, a + 1, b + k - 7))
        return near

    for a in range(rows):
        last = a == rows - 1
        on, which = live[a], index[a]
        for b in range(cols):
            near = ahead(a, b, last)
            side_on = u[a, b].T
            turned[a, b] = side_on
            gram = dot(side_on, cat([u[p, q] for _, p, q in near], 1), NN)
            for n, (k, _, _) in enumerate(near):
                at = which[b, k]
                rho = sym[at] if k == 4 else tapers[at]
                held[a % 2, b, :, (k - 4) * cells : (k - 3) * cells] = tapered(
                    gram[:, n * cells : (n + 1) * cells], rho, on[b, k]
                )
        for b in range(cols):
            near = ahead(a, b, last)
            total = dot(
                cat([w[p, q] for _, p, q in near], 1),
                cat([held[a % 2, b, :, (k - 4) * cells : (k - 3) * cells] for k, _, _ in near], 1),
                NT,
            )
            behind = [(5, a, b - 1)] if b > 0 else []
            if a > 0:
                behind += [(k, a - 1, b - (k - 7)) for k in (6, 7, 8) if 0 <= b - (k - 7) < cols]
            if behind:
                total += dot(
                    cat([w[p, q] for _, p, q in behind], 1),
                    cat([held[p % 2, q, :, (k - 4) * cells : (k - 3) * cells] for k, p, q in behind], 0),
                    NN,
                )
            out[a, b] = total


def inner(u, w, live, index, tapers):
    rows, cols, members, cells = u.shape
    columns = w.shape[2]
    pairs = 5 * rows * cols
    return pl.pallas_call(
        inner_kernel,
        out_shape=(
            jax.ShapeDtypeStruct((rows, cols, columns, cells), jnp.float32),
            jax.ShapeDtypeStruct((rows, cols, cells, members), jnp.bfloat16),
            jax.ShapeDtypeStruct(tapers.shape, jnp.bfloat16),
        ),
        in_specs=[VMEM] * 5,
        out_specs=(VMEM,) * 3,
        scratch_shapes=[
            pltpu.VMEM(tapers.shape, jnp.float32),
            pltpu.VMEM((2, cols, cells, 5 * cells), jnp.bfloat16),
        ],
        compiler_params=pltpu.CompilerParams(vmem_limit_bytes=GRANT),
        cost_estimate=pl.CostEstimate(
            flops=2 * pairs * cells * cells * (members + 2 * columns),
            bytes_accessed=4 << 20,
            transcendentals=0,
        ),
        name="inner",
    )(u, w, live, index, tapers)


def above_kernel(s, turned, w, inside, outside, live, index, flipped, back, held, to_inside, tail):
    _, cols, cells, members = turned.shape
    deep = members + w.shape[2]
    last = cols - 1
    left, right = sides(inside, outside)
    on, which = live[0], index[0]

    def upper(c):
        return s[c * members : (c + 1) * members]

    beyond = {}
    for q, near, k, line in ((-1, left, 2, last), (cols, right, 0, 0)):
        note = near(0, slice(deep, None)).astype(jnp.int32)
        gram = dot(near(0, slice(0, members)), upper(min(max(q, 0), last)), TN)
        block = tapered(gram, flipped[note[cols + line, k]], note[line, k])
        beyond[q] = block, near(0, slice(members, deep))
    for q in range(cols):
        near = [c for c in (q - 1, q, q + 1) if 0 <= c < cols]
        gram = dot(turned[0, q], cat([upper(c) for c in near], 1), NN)
        for n, c in enumerate(near):
            k = 1 + c - q
            held[q, :, k * cells : (k + 1) * cells] = tapered(
                gram[:, n * cells : (n + 1) * cells], flipped[which[q, k]], on[q, k]
            )
    for c in range(cols):
        blocks, weights = [], []
        for q in (c - 1, c, c + 1):
            if q in beyond:
                block, weight = beyond[q]
            else:
                k = 1 + c - q
                block, weight = held[q, :, k * cells : (k + 1) * cells], w[0, q]
            blocks.append(block)
            weights.append(weight)
        back[c] = dot(cat(weights, 1), cat(blocks, 0), NN).astype(jnp.bfloat16)
    tail[...] = s[cols * members :]
    to_inside[...] = dot(s[cols * members :], jnp.where(even_column(), beyond[cols][0], beyond[-1][0]), NT)


def above(s, turned, w, inside, outside, live, index, flipped):
    _, cols, cells, members = turned.shape
    columns = w.shape[2]
    return pl.pallas_call(
        above_kernel,
        out_shape=(
            jax.ShapeDtypeStruct((cols, columns, cells), jnp.bfloat16),
            jax.ShapeDtypeStruct((cols, cells, 3 * cells), jnp.bfloat16),
            jax.ShapeDtypeStruct((columns, cells), jnp.float32),
            jax.ShapeDtypeStruct((columns, cells), jnp.bfloat16),
        ),
        in_specs=[VMEM] * 8,
        out_specs=(VMEM,) * 4,
        compiler_params=pltpu.CompilerParams(vmem_limit_bytes=GRANT),
        cost_estimate=pl.CostEstimate(
            flops=2 * 3 * cols * cells * cells * (members + columns),
            bytes_accessed=2 << 20,
            transcendentals=0,
        ),
        name="above",
    )(s, turned, w, inside, outside, live, index, flipped)


def column_kernel(outward, near, turned, w, live, index, tapers, flipped, side):
    rows, cols, cells, members = turned.shape
    deep = members + w.shape[2]
    last = cols - 1
    on_left = even_column() if outward else jnp.logical_not(even_column())
    b = jnp.where(on_left, 0, last)
    for a in range(rows):
        on, which = live[a], index[a]
        around = [q for q in (a - 1, a, a + 1) if 0 <= q < rows]
        gram = dot(turned[a, b], cat([near[q, :members] for q in around], 1), NN)
        blocks = []
        for n, q in enumerate(around):
            k = 3 * (q - a + 1)
            at = jnp.where(on_left, which[0, k], which[last, k + 2])
            if q < a:
                rho = flipped[at]
            elif q > a:
                rho = tapers[at]
            else:
                rho = jnp.where(on_left, flipped[at], tapers[at])
            lively = jnp.where(on_left, on[0, k], on[last, k + 2])
            blocks.append(tapered(gram[:, n * cells : (n + 1) * cells], rho, lively))
        side[a] = dot(cat([near[q, members:deep] for q in around], 1), cat(blocks, 1), NT)


def column(near, turned, w, live, index, tapers, flipped, outward):
    rows, _, cells, members = turned.shape
    width = w.shape[2]
    return pl.pallas_call(
        functools.partial(column_kernel, outward),
        out_shape=jax.ShapeDtypeStruct((rows, width, cells), jnp.float32),
        in_specs=[VMEM] * 7,
        out_specs=VMEM,
        compiler_params=pltpu.CompilerParams(vmem_limit_bytes=GRANT),
        cost_estimate=pl.CostEstimate(
            flops=6 * rows * cells * cells * (members + width), bytes_accessed=2 << 20, transcendentals=0
        ),
        name="column",
    )(near, turned, w, live, index, tapers, flipped)


def outer_kernel(inc, near_side, far_side, held, tail, rest, plain, u, live, index, tapers, out, top, low):
    rows, cols, members, cells = u.shape
    width = inc.shape[2]
    last = cols - 1
    even = even_column()
    on, which = live[0], index[0]
    start = (cols - 1) * width
    gram = dot(rest[start : start + members], jnp.where(even, u[0, 0], u[0, last]), TN)
    at = jnp.where(even, which[0, 0], which[last, 2])
    block = tapered(gram, tapers[at], jnp.where(even, on[0, 0], on[last, 2]))
    far = dot(rest[start + members :], block, NN)
    blank = jnp.zeros_like(far)

    def side(q, a):
        near, other = near_side[a], far_side[a]
        return jnp.where(even, other, near) if q == 0 else jnp.where(even, near, other)

    parts = [rest[c * width : (c + 1) * width] for c in range(cols - 1)]
    tail = tail[...]
    weights = [jnp.where(even, parts[0], tail)]
    weights += [jnp.where(even, parts[c], parts[c - 1]) for c in range(1, last)]
    weights.append(jnp.where(even, tail, parts[last - 1]))
    place = lax.axis_index("col")
    alone = jnp.logical_or(place == 0, place == lax.axis_size("col") - 1)
    weights = [jnp.where(alone, plain[c], weight) for c, weight in enumerate(weights)]
    for q in range(cols):
        near = [c for c in (q - 1, q, q + 1) if 0 <= c < cols]
        block = held[q, :, (1 + near[0] - q) * cells : (2 + near[-1] - q) * cells]
        value = inc[0, q] + dot(cat([weights[c] for c in near], 1), block, NT)
        if q in (0, last):
            value += side(q, 0)
            value += jnp.where(even, far, blank) if q == 0 else jnp.where(even, blank, far)
            top[q // last] = value
        out[0, q] = value
    for a in range(1, rows):
        for q in range(cols):
            value = inc[a, q] + side(q, a) if q in (0, last) else inc[a, q]
            out[a, q] = value
            if a == rows - 1:
                low[q] = value


def outer(inc, near_side, far_side, held, tail, rest, plain, u, live, index, tapers):
    rows, cols, width, cells = inc.shape
    return pl.pallas_call(
        outer_kernel,
        out_shape=(
            jax.ShapeDtypeStruct(inc.shape, inc.dtype),
            jax.ShapeDtypeStruct((2, width, cells), inc.dtype),
            jax.ShapeDtypeStruct(inc.shape[1:], inc.dtype),
        ),
        in_specs=[VMEM] * 11,
        out_specs=(VMEM,) * 3,
        compiler_params=pltpu.CompilerParams(vmem_limit_bytes=GRANT),
        cost_estimate=pl.CostEstimate(flops=6 * cols * cells * cells * width, bytes_accessed=4 << 20, transcendentals=0),
        name="outer",
    )(inc, near_side, far_side, held, tail, rest, plain, u, live, index, tapers)


def finish_kernel(inc, top, low, back, from_inside, out, end, total, sem):
    del inc
    rows, cols = out.shape[:2]
    half = cols // 2
    side = even_column().astype(jnp.int32)
    copies = []
    for n, part in enumerate((slice(0, half), slice(half, cols))):
        total[part] = low[part] + back[part].astype(jnp.float32)
        copies.append(pltpu.make_async_copy(total.at[part], out.at[rows - 1, part], sem.at[n]))
        copies[-1].start()
    end[...] = top[side] + from_inside[...]
    copies.append(pltpu.make_async_copy(end, out.at[0, side * (cols - 1)], sem.at[2]))
    copies[-1].start()
    for copy in copies:
        copy.wait()


def finish(inc, top, low, back, from_inside):
    return pl.pallas_call(
        finish_kernel,
        out_shape=jax.ShapeDtypeStruct(inc.shape, inc.dtype),
        in_specs=[ANY] + [VMEM] * 4,
        out_specs=ANY,
        scratch_shapes=[
            pltpu.VMEM(top.shape[1:], top.dtype),
            pltpu.VMEM(low.shape, low.dtype),
            pltpu.SemaphoreType.DMA((3,)),
        ],
        input_output_aliases={0: 0},
        compiler_params=pltpu.CompilerParams(vmem_limit_bytes=GRANT),
        cost_estimate=pl.CostEstimate(flops=low.size, bytes_accessed=10 * low.size, transcendentals=0),
        name="finish",
    )(inc, top, low, back, from_inside)


def forward(axis):
    return [(i, i + 1) for i in range(lax.axis_size(axis) - 1)]


def swaps(axis, start):
    pairs = [(i, i + 1) for i in range(start, lax.axis_size(axis) - 1, 2)]
    return pairs + [(b, a) for a, b in pairs]


def backward(axis):
    return [(i + 1, i) for i in range(lax.axis_size(axis) - 1)]


def pack_row_kernel(u, w, out, sem):
    rows, cols, members, cells = u.shape
    beside = (cols - 1) * even_column().astype(jnp.int32)
    deep = cols * members
    copies = [
        pltpu.make_async_copy(u.at[rows - 1].reshape(deep, cells), out.at[:deep], sem.at[0]),
        pltpu.make_async_copy(w.at[rows - 1, beside], out.at[deep:], sem.at[1]),
    ]
    for copy in copies:
        copy.start()
    for copy in copies:
        copy.wait()


def pack_row(u, w):
    _, cols, members, cells = u.shape
    shape = (cols * members + w.shape[2], cells)
    return pl.pallas_call(
        pack_row_kernel,
        out_shape=pltpu.VMEM(shape, u.dtype),
        in_specs=[HBM, HBM],
        out_specs=VMEM,
        scratch_shapes=[pltpu.SemaphoreType.DMA((2,))],
        cost_estimate=pl.CostEstimate(flops=0, bytes_accessed=4 * shape[0] * cells, transcendentals=0),
        name="pack_row",
    )(u, w)


def pack_rest_kernel(w, outside, out, plain):
    rows, cols, width, _ = w.shape
    skip = 1 - even_column().astype(jnp.int32)
    for q in range(cols - 1):
        out[q * width : (q + 1) * width] = w[rows - 1, q + skip]
    start = (cols - 1) * width
    out[start:] = outside[rows - 1, : out.shape[0] - start]
    plain[...] = w[rows - 1]


def pack_rest(w, outside, members):
    _, cols, width, cells = w.shape
    return pl.pallas_call(
        pack_rest_kernel,
        out_shape=(
            jax.ShapeDtypeStruct(((cols - 1) * width + members + width, cells), w.dtype),
            jax.ShapeDtypeStruct((cols, width, cells), w.dtype),
        ),
        in_specs=[VMEM, VMEM],
        out_specs=(VMEM, VMEM),
        compiler_params=pltpu.CompilerParams(vmem_limit_bytes=GRANT),
        cost_estimate=pl.CostEstimate(flops=0, bytes_accessed=8 * cols * width * cells, transcendentals=0),
        name="pack_rest",
    )(w, outside)


def pack_columns_kernel(u, w, live, index, packed, inner_side, outer_side, sem):
    del packed
    rows, cols, members, cells = u.shape
    deep = members + w.shape[2]
    turn = (cols - 1) * even_column().astype(jnp.int32)
    copies = []
    for n, (out, b) in enumerate(((inner_side, turn), (outer_side, cols - 1 - turn))):
        copies.append(pltpu.make_async_copy(u.at[:, b], out.at[:, :members], sem.at[n, 0]))
        copies.append(pltpu.make_async_copy(w.at[:, b], out.at[:, members:deep], sem.at[n, 1]))
    for copy in copies:
        copy.start()
    for a in range(rows):
        lines = jnp.concatenate([live[a], index[a]], 0).astype(jnp.float32)
        blank = jnp.zeros((2 * cols, cells - live.shape[2]), jnp.float32)
        note = jnp.concatenate([lines, blank], 1).astype(jnp.bfloat16)
        inner_side[a, deep:] = note
        outer_side[a, deep:] = note
    for copy in copies:
        copy.wait()


def pack_columns(u, w, live, index, packed):
    rows, cols, members, cells = u.shape
    shape = (rows, members + w.shape[2] + 2 * cols, cells)
    return pl.pallas_call(
        pack_columns_kernel,
        out_shape=(jax.ShapeDtypeStruct(shape, u.dtype),) * 2,
        in_specs=[ANY, ANY, VMEM, VMEM, VMEM],
        out_specs=(VMEM, VMEM),
        scratch_shapes=[pltpu.SemaphoreType.DMA((2, 2))],
        compiler_params=pltpu.CompilerParams(vmem_limit_bytes=GRANT),
        cost_estimate=pl.CostEstimate(flops=0, bytes_accessed=8 * rows * shape[1] * cells, transcendentals=0),
        name="pack_columns",
    )(u, w, live, index, packed)


def down(row, col, chosen):
    wide = lax.axis_size(col)
    return [(r * wide + c, (r + 1) * wide + c) for r in range(lax.axis_size(row) - 1) for c in chosen]


def body(u, w, live, index, tapers):
    wide = lax.axis_size("col")
    packed = pack_row(u, w)
    s = lax.ppermute(packed, "row", forward("row"))
    inner_side, outer_side = pack_columns(u, w, live, index, packed)
    outside = lax.ppermute(outer_side, "col", swaps("col", 1))
    inside = lax.ppermute(inner_side, "col", swaps("col", 0))
    inc, turned, flipped = inner(u, w, live, index, tapers)
    inc, outside, inside = lax.optimization_barrier((inc, outside, inside))
    rest, plain = pack_rest(w, outside, u.shape[2])
    rest = lax.ppermute(rest, ("row", "col"), down("row", "col", range(1, wide - 1)))
    plain = lax.ppermute(plain, ("row", "col"), down("row", "col", sorted({0, wide - 1})))
    back, held, to_inside, tail = above(s, turned, w, inside, outside, live, index, flipped)
    back = lax.ppermute(back, "row", backward("row"))
    from_inside = lax.ppermute(to_inside, "col", swaps("col", 0))
    near_side = column(inside, turned, w, live, index, tapers, flipped, False)
    far_side = column(outside, turned, w, live, index, tapers, flipped, True)
    inc, top, low = outer(inc, near_side, far_side, held, tail, rest, plain, u, live, index, tapers)
    return finish(inc, top, low, back, from_inside)


def solution(mesh):
    return jax.shard_map(
        body,
        mesh=mesh,
        in_specs=(
            P("row", "col", None, None),
            P("row", "col", None, None),
            P("row", "col", None),
            P("row", "col", None),
            P(),
        ),
        out_specs=P("row", "col", None, None),
        check_vma=False,
    )
```

```python
import functools

import jax
import jax.numpy as jnp
from jax import lax
from jax.experimental import pallas as pl
from jax.experimental.pallas import tpu as pltpu
from jax.sharding import PartitionSpec as P

MEMBERS = 256
GRANT = 16 << 20
SCALE = 1.0 / (MEMBERS - 1)
TN = (((0,), (0,)), ((), ()))
NT = (((1,), (1,)), ((), ()))
NN = (((1,), (0,)), ((), ()))
VMEM = pl.BlockSpec(memory_space=pltpu.VMEM)
ANY = pl.BlockSpec(memory_space=pl.ANY)
HBM = pl.BlockSpec(memory_space=pltpu.HBM)


def dot(a, b, dims):
    return lax.dot_general(a, b, dims, preferred_element_type=jnp.float32)


def cat(parts, axis):
    return parts[0] if len(parts) == 1 else jnp.concatenate(parts, axis=axis)


def tapered(gram, rho, live):
    factor = live.astype(jnp.float32) * SCALE
    return (rho.astype(jnp.float32) * gram * factor).astype(jnp.bfloat16)


def even_column():
    return lax.rem(lax.axis_index("col"), 2) == 0


def sides(inside, outside):
    even = even_column()
    return (
        lambda *at: jnp.where(even, outside[at], inside[at]),
        lambda *at: jnp.where(even, inside[at], outside[at]),
    )


def inner_kernel(u, w, live, index, tapers, out, turned, flipped, sym, held):
    rows, cols, _, cells = u.shape
    for n in range(tapers.shape[0]):
        t = tapers[n].astype(jnp.float32)
        sym[n] = 0.5 * (t + t.T)
        flipped[n] = t.T.astype(jnp.bfloat16)

    def ahead(a, b, last):
        near = [(4, a, b)]
        if b + 1 < cols:
            near.append((5, a, b + 1))
        if not last:
            for k in (6, 7, 8):
                if 0 <= b + k - 7 < cols:
                    near.append((k, a + 1, b + k - 7))
        return near

    for a in range(rows):
        last = a == rows - 1
        on, which = live[a], index[a]
        for b in range(cols):
            near = ahead(a, b, last)
            side_on = u[a, b].T
            turned[a, b] = side_on
            gram = dot(side_on, cat([u[p, q] for _, p, q in near], 1), NN)
            for n, (k, _, _) in enumerate(near):
                at = which[b, k]
                rho = sym[at] if k == 4 else tapers[at]
                held[a % 2, b, :, (k - 4) * cells : (k - 3) * cells] = tapered(
                    gram[:, n * cells : (n + 1) * cells], rho, on[b, k]
                )
        for b in range(cols):
            near = ahead(a, b, last)
            total = dot(
                cat([w[p, q] for _, p, q in near], 1),
                cat([held[a % 2, b, :, (k - 4) * cells : (k - 3) * cells] for k, _, _ in near], 1),
                NT,
            )
            behind = [(5, a, b - 1)] if b > 0 else []
            if a > 0:
                behind += [(k, a - 1, b - (k - 7)) for k in (6, 7, 8) if 0 <= b - (k - 7) < cols]
            if behind:
                total += dot(
                    cat([w[p, q] for _, p, q in behind], 1),
                    cat([held[p % 2, q, :, (k - 4) * cells : (k - 3) * cells] for k, p, q in behind], 0),
                    NN,
                )
            out[a, b] = total


def inner(u, w, live, index, tapers):
    rows, cols, members, cells = u.shape
    columns = w.shape[2]
    pairs = 5 * rows * cols
    return pl.pallas_call(
        inner_kernel,
        out_shape=(
            jax.ShapeDtypeStruct((rows, cols, columns, cells), jnp.float32),
            jax.ShapeDtypeStruct((rows, cols, cells, members), jnp.bfloat16),
            jax.ShapeDtypeStruct(tapers.shape, jnp.bfloat16),
        ),
        in_specs=[VMEM] * 5,
        out_specs=(VMEM,) * 3,
        scratch_shapes=[
            pltpu.VMEM(tapers.shape, jnp.float32),
            pltpu.VMEM((2, cols, cells, 5 * cells), jnp.bfloat16),
        ],
        compiler_params=pltpu.CompilerParams(vmem_limit_bytes=GRANT),
        cost_estimate=pl.CostEstimate(
            flops=2 * pairs * cells * cells * (members + 2 * columns),
            bytes_accessed=4 << 20,
            transcendentals=0,
        ),
        name="inner",
    )(u, w, live, index, tapers)


def above_kernel(s, turned, w, inside, outside, live, index, flipped, back, held, to_inside, tail):
    _, cols, cells, members = turned.shape
    deep = members + w.shape[2]
    last = cols - 1
    left, right = sides(inside, outside)
    on, which = live[0], index[0]

    def upper(c):
        return s[c * members : (c + 1) * members]

    beyond = {}
    for q, near, k, line in ((-1, left, 2, last), (cols, right, 0, 0)):
        note = near(0, slice(deep, None)).astype(jnp.int32)
        gram = dot(near(0, slice(0, members)), upper(min(max(q, 0), last)), TN)
        block = tapered(gram, flipped[note[cols + line, k]], note[line, k])
        beyond[q] = block, near(0, slice(members, deep))
    for q in range(cols):
        near = [c for c in (q - 1, q, q + 1) if 0 <= c < cols]
        gram = dot(turned[0, q], cat([upper(c) for c in near], 1), NN)
        for n, c in enumerate(near):
            k = 1 + c - q
            held[q, :, k * cells : (k + 1) * cells] = tapered(
                gram[:, n * cells : (n + 1) * cells], flipped[which[q, k]], on[q, k]
            )
    for c in range(cols):
        blocks, weights = [], []
        for q in (c - 1, c, c + 1):
            if q in beyond:
                block, weight = beyond[q]
            else:
                k = 1 + c - q
                block, weight = held[q, :, k * cells : (k + 1) * cells], w[0, q]
            blocks.append(block)
            weights.append(weight)
        back[c] = dot(cat(weights, 1), cat(blocks, 0), NN).astype(jnp.bfloat16)
    tail[...] = s[cols * members :]
    to_inside[...] = dot(s[cols * members :], jnp.where(even_column(), beyond[cols][0], beyond[-1][0]), NT)


def above(s, turned, w, inside, outside, live, index, flipped):
    _, cols, cells, members = turned.shape
    columns = w.shape[2]
    return pl.pallas_call(
        above_kernel,
        out_shape=(
            jax.ShapeDtypeStruct((cols, columns, cells), jnp.bfloat16),
            jax.ShapeDtypeStruct((cols, cells, 3 * cells), jnp.bfloat16),
            jax.ShapeDtypeStruct((columns, cells), jnp.float32),
            jax.ShapeDtypeStruct((columns, cells), jnp.bfloat16),
        ),
        in_specs=[VMEM] * 8,
        out_specs=(VMEM,) * 4,
        compiler_params=pltpu.CompilerParams(vmem_limit_bytes=GRANT),
        cost_estimate=pl.CostEstimate(
            flops=2 * 3 * cols * cells * cells * (members + columns),
            bytes_accessed=2 << 20,
            transcendentals=0,
        ),
        name="above",
    )(s, turned, w, inside, outside, live, index, flipped)


def column_kernel(outward, near, turned, w, live, index, tapers, flipped, side):
    rows, cols, cells, members = turned.shape
    deep = members + w.shape[2]
    last = cols - 1
    on_left = even_column() if outward else jnp.logical_not(even_column())
    b = jnp.where(on_left, 0, last)
    for a in range(rows):
        on, which = live[a], index[a]
        around = [q for q in (a - 1, a, a + 1) if 0 <= q < rows]
        gram = dot(turned[a, b], cat([near[q, :members] for q in around], 1), NN)
        blocks = []
        for n, q in enumerate(around):
            k = 3 * (q - a + 1)
            at = jnp.where(on_left, which[0, k], which[last, k + 2])
            if q < a:
                rho = flipped[at]
            elif q > a:
                rho = tapers[at]
            else:
                rho = jnp.where(on_left, flipped[at], tapers[at])
            lively = jnp.where(on_left, on[0, k], on[last, k + 2])
            blocks.append(tapered(gram[:, n * cells : (n + 1) * cells], rho, lively))
        side[a] = dot(cat([near[q, members:deep] for q in around], 1), cat(blocks, 1), NT)


def column(near, turned, w, live, index, tapers, flipped, outward):
    rows, _, cells, members = turned.shape
    width = w.shape[2]
    return pl.pallas_call(
        functools.partial(column_kernel, outward),
        out_shape=jax.ShapeDtypeStruct((rows, width, cells), jnp.float32),
        in_specs=[VMEM] * 7,
        out_specs=VMEM,
        compiler_params=pltpu.CompilerParams(vmem_limit_bytes=GRANT),
        cost_estimate=pl.CostEstimate(
            flops=6 * rows * cells * cells * (members + width), bytes_accessed=2 << 20, transcendentals=0
        ),
        name="column",
    )(near, turned, w, live, index, tapers, flipped)


def outer_kernel(inc, near_side, far_side, held, tail, rest, u, live, index, tapers, out, top, low):
    rows, cols, members, cells = u.shape
    width = inc.shape[2]
    last = cols - 1
    even = even_column()
    on, which = live[0], index[0]
    start = (cols - 1) * width
    gram = dot(rest[start : start + members], jnp.where(even, u[0, 0], u[0, last]), TN)
    at = jnp.where(even, which[0, 0], which[last, 2])
    block = tapered(gram, tapers[at], jnp.where(even, on[0, 0], on[last, 2]))
    far = dot(rest[start + members :], block, NN)
    blank = jnp.zeros_like(far)

    def side(q, a):
        near, other = near_side[a], far_side[a]
        return jnp.where(even, other, near) if q == 0 else jnp.where(even, near, other)

    parts = [rest[c * width : (c + 1) * width] for c in range(cols - 1)]
    tail = tail[...]
    weights = [jnp.where(even, parts[0], tail)]
    weights += [jnp.where(even, parts[c], parts[c - 1]) for c in range(1, last)]
    weights.append(jnp.where(even, tail, parts[last - 1]))
    for q in range(cols):
        near = [c for c in (q - 1, q, q + 1) if 0 <= c < cols]
        block = held[q, :, (1 + near[0] - q) * cells : (2 + near[-1] - q) * cells]
        value = inc[0, q] + dot(cat([weights[c] for c in near], 1), block, NT)
        if q in (0, last):
            value += side(q, 0)
            value += jnp.where(even, far, blank) if q == 0 else jnp.where(even, blank, far)
            top[q // last] = value
        out[0, q] = value
    for a in range(1, rows):
        for q in range(cols):
            value = inc[a, q] + side(q, a) if q in (0, last) else inc[a, q]
            out[a, q] = value
            if a == rows - 1:
                low[q] = value


def outer(inc, near_side, far_side, held, tail, rest, u, live, index, tapers):
    rows, cols, width, cells = inc.shape
    return pl.pallas_call(
        outer_kernel,
        out_shape=(
            jax.ShapeDtypeStruct(inc.shape, inc.dtype),
            jax.ShapeDtypeStruct((2, width, cells), inc.dtype),
            jax.ShapeDtypeStruct(inc.shape[1:], inc.dtype),
        ),
        in_specs=[VMEM] * 10,
        out_specs=(VMEM,) * 3,
        compiler_params=pltpu.CompilerParams(vmem_limit_bytes=GRANT),
        cost_estimate=pl.CostEstimate(flops=6 * cols * cells * cells * width, bytes_accessed=4 << 20, transcendentals=0),
        name="outer",
    )(inc, near_side, far_side, held, tail, rest, u, live, index, tapers)


def finish_kernel(inc, top, low, back, from_inside, out, end, total, sem):
    del inc
    rows, cols = out.shape[:2]
    half = cols // 2
    side = even_column().astype(jnp.int32)
    copies = []
    for n, part in enumerate((slice(0, half), slice(half, cols))):
        total[part] = low[part] + back[part].astype(jnp.float32)
        copies.append(pltpu.make_async_copy(total.at[part], out.at[rows - 1, part], sem.at[n]))
        copies[-1].start()
    end[...] = top[side] + from_inside[...]
    copies.append(pltpu.make_async_copy(end, out.at[0, side * (cols - 1)], sem.at[2]))
    copies[-1].start()
    for copy in copies:
        copy.wait()


def finish(inc, top, low, back, from_inside):
    return pl.pallas_call(
        finish_kernel,
        out_shape=jax.ShapeDtypeStruct(inc.shape, inc.dtype),
        in_specs=[ANY] + [VMEM] * 4,
        out_specs=ANY,
        scratch_shapes=[
            pltpu.VMEM(top.shape[1:], top.dtype),
            pltpu.VMEM(low.shape, low.dtype),
            pltpu.SemaphoreType.DMA((3,)),
        ],
        input_output_aliases={0: 0},
        compiler_params=pltpu.CompilerParams(vmem_limit_bytes=GRANT),
        cost_estimate=pl.CostEstimate(flops=low.size, bytes_accessed=10 * low.size, transcendentals=0),
        name="finish",
    )(inc, top, low, back, from_inside)


def forward(axis):
    return [(i, i + 1) for i in range(lax.axis_size(axis) - 1)]


def swaps(axis, start):
    pairs = [(i, i + 1) for i in range(start, lax.axis_size(axis) - 1, 2)]
    return pairs + [(b, a) for a, b in pairs]


def backward(axis):
    return [(i + 1, i) for i in range(lax.axis_size(axis) - 1)]


def pack_row_kernel(u, w, out, sem):
    rows, cols, members, cells = u.shape
    beside = (cols - 1) * even_column().astype(jnp.int32)
    deep = cols * members
    copies = [
        pltpu.make_async_copy(u.at[rows - 1].reshape(deep, cells), out.at[:deep], sem.at[0]),
        pltpu.make_async_copy(w.at[rows - 1, beside], out.at[deep:], sem.at[1]),
    ]
    for copy in copies:
        copy.start()
    for copy in copies:
        copy.wait()


def pack_row(u, w):
    _, cols, members, cells = u.shape
    shape = (cols * members + w.shape[2], cells)
    return pl.pallas_call(
        pack_row_kernel,
        out_shape=pltpu.VMEM(shape, u.dtype),
        in_specs=[HBM, HBM],
        out_specs=VMEM,
        scratch_shapes=[pltpu.SemaphoreType.DMA((2,))],
        cost_estimate=pl.CostEstimate(flops=0, bytes_accessed=4 * shape[0] * cells, transcendentals=0),
        name="pack_row",
    )(u, w)


def pack_rest_kernel(w, outside, out):
    rows, cols, width, _ = w.shape
    skip = 1 - even_column().astype(jnp.int32)
    for q in range(cols - 1):
        out[q * width : (q + 1) * width] = w[rows - 1, q + skip]
    start = (cols - 1) * width
    out[start:] = outside[rows - 1, : out.shape[0] - start]


def pack_rest(w, outside, members):
    _, cols, width, cells = w.shape
    return pl.pallas_call(
        pack_rest_kernel,
        out_shape=jax.ShapeDtypeStruct(((cols - 1) * width + members + width, cells), w.dtype),
        in_specs=[VMEM, VMEM],
        out_specs=VMEM,
        compiler_params=pltpu.CompilerParams(vmem_limit_bytes=GRANT),
        cost_estimate=pl.CostEstimate(flops=0, bytes_accessed=8 * cols * width * cells, transcendentals=0),
        name="pack_rest",
    )(w, outside)


def pack_columns_kernel(u, w, live, index, packed, inner_side, outer_side, sem):
    del packed
    rows, cols, members, cells = u.shape
    deep = members + w.shape[2]
    turn = (cols - 1) * even_column().astype(jnp.int32)
    copies = []
    for n, (out, b) in enumerate(((inner_side, turn), (outer_side, cols - 1 - turn))):
        copies.append(pltpu.make_async_copy(u.at[:, b], out.at[:, :members], sem.at[n, 0]))
        copies.append(pltpu.make_async_copy(w.at[:, b], out.at[:, members:deep], sem.at[n, 1]))
    for copy in copies:
        copy.start()
    for a in range(rows):
        lines = jnp.concatenate([live[a], index[a]], 0).astype(jnp.float32)
        blank = jnp.zeros((2 * cols, cells - live.shape[2]), jnp.float32)
        note = jnp.concatenate([lines, blank], 1).astype(jnp.bfloat16)
        inner_side[a, deep:] = note
        outer_side[a, deep:] = note
    for copy in copies:
        copy.wait()


def pack_columns(u, w, live, index, packed):
    rows, cols, members, cells = u.shape
    shape = (rows, members + w.shape[2] + 2 * cols, cells)
    return pl.pallas_call(
        pack_columns_kernel,
        out_shape=(jax.ShapeDtypeStruct(shape, u.dtype),) * 2,
        in_specs=[ANY, ANY, VMEM, VMEM, VMEM],
        out_specs=(VMEM, VMEM),
        scratch_shapes=[pltpu.SemaphoreType.DMA((2, 2))],
        compiler_params=pltpu.CompilerParams(vmem_limit_bytes=GRANT),
        cost_estimate=pl.CostEstimate(flops=0, bytes_accessed=8 * rows * shape[1] * cells, transcendentals=0),
        name="pack_columns",
    )(u, w, live, index, packed)


def body(u, w, live, index, tapers):
    packed = pack_row(u, w)
    s = lax.ppermute(packed, "row", forward("row"))
    inner_side, outer_side = pack_columns(u, w, live, index, packed)
    outside = lax.ppermute(outer_side, "col", swaps("col", 1))
    inside = lax.ppermute(inner_side, "col", swaps("col", 0))
    inc, turned, flipped = inner(u, w, live, index, tapers)
    inc, outside, inside = lax.optimization_barrier((inc, outside, inside))
    near_side = column(inside, turned, w, live, index, tapers, flipped, False)
    near_side, outside = lax.optimization_barrier((near_side, outside))
    rest = lax.ppermute(pack_rest(w, outside, u.shape[2]), "row", forward("row"))
    back, held, to_inside, tail = above(s, turned, w, inside, outside, live, index, flipped)
    back = lax.ppermute(back, "row", backward("row"))
    from_inside = lax.ppermute(to_inside, "col", swaps("col", 0))
    far_side = column(outside, turned, w, live, index, tapers, flipped, True)
    inc, top, low = outer(inc, near_side, far_side, held, tail, rest, u, live, index, tapers)
    return finish(inc, top, low, back, from_inside)


def solution(mesh):
    return jax.shard_map(
        body,
        mesh=mesh,
        in_specs=(
            P("row", "col", None, None),
            P("row", "col", None, None),
            P("row", "col", None),
            P("row", "col", None),
            P(),
        ),
        out_specs=P("row", "col", None, None),
        check_vma=False,
    )
```

```python
import functools

import jax
import jax.numpy as jnp
from jax import lax
from jax.experimental import pallas as pl
from jax.experimental.pallas import tpu as pltpu
from jax.sharding import PartitionSpec as P

MEMBERS = 256
GRANT = 16 << 20
SCALE = 1.0 / (MEMBERS - 1)
TN = (((0,), (0,)), ((), ()))
NT = (((1,), (1,)), ((), ()))
NN = (((1,), (0,)), ((), ()))
VMEM = pl.BlockSpec(memory_space=pltpu.VMEM)
ANY = pl.BlockSpec(memory_space=pl.ANY)
HBM = pl.BlockSpec(memory_space=pltpu.HBM)


def dot(a, b, dims):
    return lax.dot_general(a, b, dims, preferred_element_type=jnp.float32)


def cat(parts, axis):
    return parts[0] if len(parts) == 1 else jnp.concatenate(parts, axis=axis)


def tapered(gram, rho, live):
    factor = live.astype(jnp.float32) * SCALE
    return (rho.astype(jnp.float32) * gram * factor).astype(jnp.bfloat16)


def even_column():
    return lax.rem(lax.axis_index("col"), 2) == 0


def sides(inside, outside):
    even = even_column()
    return (
        lambda *at: jnp.where(even, outside[at], inside[at]),
        lambda *at: jnp.where(even, inside[at], outside[at]),
    )


def inner_kernel(u, w, live, index, tapers, out, turned, flipped, sym, held):
    rows, cols, _, cells = u.shape
    for n in range(tapers.shape[0]):
        t = tapers[n].astype(jnp.float32)
        sym[n] = 0.5 * (t + t.T)
        flipped[n] = t.T.astype(jnp.bfloat16)

    def ahead(a, b, last):
        near = [(4, a, b)]
        if b + 1 < cols:
            near.append((5, a, b + 1))
        if not last:
            for k in (6, 7, 8):
                if 0 <= b + k - 7 < cols:
                    near.append((k, a + 1, b + k - 7))
        return near

    for a in range(rows):
        last = a == rows - 1
        on, which = live[a], index[a]
        for b in range(cols):
            near = ahead(a, b, last)
            side_on = u[a, b].T
            turned[a, b] = side_on
            gram = dot(side_on, cat([u[p, q] for _, p, q in near], 1), NN)
            for n, (k, _, _) in enumerate(near):
                at = which[b, k]
                rho = sym[at] if k == 4 else tapers[at]
                held[a % 2, b, :, (k - 4) * cells : (k - 3) * cells] = tapered(
                    gram[:, n * cells : (n + 1) * cells], rho, on[b, k]
                )
        for b in range(cols):
            near = ahead(a, b, last)
            total = dot(
                cat([w[p, q] for _, p, q in near], 1),
                cat([held[a % 2, b, :, (k - 4) * cells : (k - 3) * cells] for k, _, _ in near], 1),
                NT,
            )
            behind = [(5, a, b - 1)] if b > 0 else []
            if a > 0:
                behind += [(k, a - 1, b - (k - 7)) for k in (6, 7, 8) if 0 <= b - (k - 7) < cols]
            if behind:
                total += dot(
                    cat([w[p, q] for _, p, q in behind], 1),
                    cat([held[p % 2, q, :, (k - 4) * cells : (k - 3) * cells] for k, p, q in behind], 0),
                    NN,
                )
            out[a, b] = total


def inner(u, w, live, index, tapers):
    rows, cols, members, cells = u.shape
    columns = w.shape[2]
    pairs = 5 * rows * cols
    return pl.pallas_call(
        inner_kernel,
        out_shape=(
            jax.ShapeDtypeStruct((rows, cols, columns, cells), jnp.float32),
            jax.ShapeDtypeStruct((rows, cols, cells, members), jnp.bfloat16),
            jax.ShapeDtypeStruct(tapers.shape, jnp.bfloat16),
        ),
        in_specs=[VMEM] * 5,
        out_specs=(VMEM,) * 3,
        scratch_shapes=[
            pltpu.VMEM(tapers.shape, jnp.float32),
            pltpu.VMEM((2, cols, cells, 5 * cells), jnp.bfloat16),
        ],
        compiler_params=pltpu.CompilerParams(vmem_limit_bytes=GRANT),
        cost_estimate=pl.CostEstimate(
            flops=2 * pairs * cells * cells * (members + 2 * columns),
            bytes_accessed=4 << 20,
            transcendentals=0,
        ),
        name="inner",
    )(u, w, live, index, tapers)


def above_kernel(s, turned, w, inside, outside, live, index, flipped, back, held, to_inside, tail):
    _, cols, cells, members = turned.shape
    deep = members + w.shape[2]
    last = cols - 1
    left, right = sides(inside, outside)
    on, which = live[0], index[0]

    def upper(c):
        return s[c * members : (c + 1) * members]

    beyond = {}
    for q, near, k, line in ((-1, left, 2, last), (cols, right, 0, 0)):
        note = near(0, slice(deep, None)).astype(jnp.int32)
        gram = dot(near(0, slice(0, members)), upper(min(max(q, 0), last)), TN)
        block = tapered(gram, flipped[note[cols + line, k]], note[line, k])
        beyond[q] = block, near(0, slice(members, deep))
    for q in range(cols):
        near = [c for c in (q - 1, q, q + 1) if 0 <= c < cols]
        gram = dot(turned[0, q], cat([upper(c) for c in near], 1), NN)
        for n, c in enumerate(near):
            k = 1 + c - q
            held[q, :, k * cells : (k + 1) * cells] = tapered(
                gram[:, n * cells : (n + 1) * cells], flipped[which[q, k]], on[q, k]
            )
    for c in range(cols):
        blocks, weights = [], []
        for q in (c - 1, c, c + 1):
            if q in beyond:
                block, weight = beyond[q]
            else:
                k = 1 + c - q
                block, weight = held[q, :, k * cells : (k + 1) * cells], w[0, q]
            blocks.append(block)
            weights.append(weight)
        back[c] = dot(cat(weights, 1), cat(blocks, 0), NN).astype(jnp.bfloat16)
    tail[...] = s[cols * members :]
    to_inside[...] = dot(s[cols * members :], jnp.where(even_column(), beyond[cols][0], beyond[-1][0]), NT)


def above(s, turned, w, inside, outside, live, index, flipped):
    _, cols, cells, members = turned.shape
    columns = w.shape[2]
    return pl.pallas_call(
        above_kernel,
        out_shape=(
            jax.ShapeDtypeStruct((cols, columns, cells), jnp.bfloat16),
            jax.ShapeDtypeStruct((cols, cells, 3 * cells), jnp.bfloat16),
            jax.ShapeDtypeStruct((columns, cells), jnp.float32),
            jax.ShapeDtypeStruct((columns, cells), jnp.bfloat16),
        ),
        in_specs=[VMEM] * 8,
        out_specs=(VMEM,) * 4,
        compiler_params=pltpu.CompilerParams(vmem_limit_bytes=GRANT),
        cost_estimate=pl.CostEstimate(
            flops=2 * 3 * cols * cells * cells * (members + columns),
            bytes_accessed=2 << 20,
            transcendentals=0,
        ),
        name="above",
    )(s, turned, w, inside, outside, live, index, flipped)


def column_part(outward, near, turned, w, live, index, tapers, flipped, side):
    rows, cols, cells, members = turned.shape
    deep = members + w.shape[2]
    last = cols - 1
    on_left = even_column() if outward else jnp.logical_not(even_column())
    b = jnp.where(on_left, 0, last)
    for a in range(rows):
        on, which = live[a], index[a]
        around = [q for q in (a - 1, a, a + 1) if 0 <= q < rows]
        gram = dot(turned[a, b], cat([near[q, :members] for q in around], 1), NN)
        blocks = []
        for n, q in enumerate(around):
            k = 3 * (q - a + 1)
            at = jnp.where(on_left, which[0, k], which[last, k + 2])
            if q < a:
                rho = flipped[at]
            elif q > a:
                rho = tapers[at]
            else:
                rho = jnp.where(on_left, flipped[at], tapers[at])
            lively = jnp.where(on_left, on[0, k], on[last, k + 2])
            blocks.append(tapered(gram[:, n * cells : (n + 1) * cells], rho, lively))
        side[a] = dot(cat([near[q, members:deep] for q in around], 1), cat(blocks, 1), NT)


def column_kernel(outward, alone, near, turned, w, live, index, tapers, flipped, side):
    place = lax.axis_index("col")
    here = jnp.logical_or(place == 0, place == lax.axis_size("col") - 1)
    here = here if alone else jnp.logical_not(here)

    @pl.when(here)
    def _():
        column_part(outward, near, turned, w, live, index, tapers, flipped, side)

    @pl.when(jnp.logical_not(here))
    def _():
        side[...] = jnp.zeros_like(side)


def column(near, turned, w, live, index, tapers, flipped, outward, alone):
    rows, _, cells, members = turned.shape
    width = w.shape[2]
    return pl.pallas_call(
        functools.partial(column_kernel, outward, alone),
        out_shape=jax.ShapeDtypeStruct((rows, width, cells), jnp.float32),
        in_specs=[VMEM] * 7,
        out_specs=VMEM,
        compiler_params=pltpu.CompilerParams(vmem_limit_bytes=GRANT),
        cost_estimate=pl.CostEstimate(
            flops=6 * rows * cells * cells * (members + width), bytes_accessed=2 << 20, transcendentals=0
        ),
        name="column",
    )(near, turned, w, live, index, tapers, flipped)


def outer_kernel(inc, near_side, more_side, far_side, held, tail, rest, u, live, index, tapers, out, top, low):
    rows, cols, members, cells = u.shape
    width = inc.shape[2]
    last = cols - 1
    even = even_column()
    on, which = live[0], index[0]
    start = (cols - 1) * width
    gram = dot(rest[start : start + members], jnp.where(even, u[0, 0], u[0, last]), TN)
    at = jnp.where(even, which[0, 0], which[last, 2])
    block = tapered(gram, tapers[at], jnp.where(even, on[0, 0], on[last, 2]))
    far = dot(rest[start + members :], block, NN)
    blank = jnp.zeros_like(far)

    def side(q, a):
        near, other = near_side[a] + more_side[a], far_side[a]
        return jnp.where(even, other, near) if q == 0 else jnp.where(even, near, other)

    parts = [rest[c * width : (c + 1) * width] for c in range(cols - 1)]
    tail = tail[...]
    weights = [jnp.where(even, parts[0], tail)]
    weights += [jnp.where(even, parts[c], parts[c - 1]) for c in range(1, last)]
    weights.append(jnp.where(even, tail, parts[last - 1]))
    for q in range(cols):
        near = [c for c in (q - 1, q, q + 1) if 0 <= c < cols]
        block = held[q, :, (1 + near[0] - q) * cells : (2 + near[-1] - q) * cells]
        value = inc[0, q] + dot(cat([weights[c] for c in near], 1), block, NT)
        if q in (0, last):
            value += side(q, 0)
            value += jnp.where(even, far, blank) if q == 0 else jnp.where(even, blank, far)
            top[q // last] = value
        out[0, q] = value
    for a in range(1, rows):
        for q in range(cols):
            value = inc[a, q] + side(q, a) if q in (0, last) else inc[a, q]
            out[a, q] = value
            if a == rows - 1:
                low[q] = value


def outer(inc, near_side, more_side, far_side, held, tail, rest, u, live, index, tapers):
    rows, cols, width, cells = inc.shape
    return pl.pallas_call(
        outer_kernel,
        out_shape=(
            jax.ShapeDtypeStruct(inc.shape, inc.dtype),
            jax.ShapeDtypeStruct((2, width, cells), inc.dtype),
            jax.ShapeDtypeStruct(inc.shape[1:], inc.dtype),
        ),
        in_specs=[VMEM] * 11,
        out_specs=(VMEM,) * 3,
        compiler_params=pltpu.CompilerParams(vmem_limit_bytes=GRANT),
        cost_estimate=pl.CostEstimate(flops=6 * cols * cells * cells * width, bytes_accessed=4 << 20, transcendentals=0),
        name="outer",
    )(inc, near_side, more_side, far_side, held, tail, rest, u, live, index, tapers)


def finish_kernel(inc, top, low, back, from_inside, out, end, total, sem):
    del inc
    rows, cols = out.shape[:2]
    half = cols // 2
    side = even_column().astype(jnp.int32)
    copies = []
    for n, part in enumerate((slice(0, half), slice(half, cols))):
        total[part] = low[part] + back[part].astype(jnp.float32)
        copies.append(pltpu.make_async_copy(total.at[part], out.at[rows - 1, part], sem.at[n]))
        copies[-1].start()
    end[...] = top[side] + from_inside[...]
    copies.append(pltpu.make_async_copy(end, out.at[0, side * (cols - 1)], sem.at[2]))
    copies[-1].start()
    for copy in copies:
        copy.wait()


def finish(inc, top, low, back, from_inside):
    return pl.pallas_call(
        finish_kernel,
        out_shape=jax.ShapeDtypeStruct(inc.shape, inc.dtype),
        in_specs=[ANY] + [VMEM] * 4,
        out_specs=ANY,
        scratch_shapes=[
            pltpu.VMEM(top.shape[1:], top.dtype),
            pltpu.VMEM(low.shape, low.dtype),
            pltpu.SemaphoreType.DMA((3,)),
        ],
        input_output_aliases={0: 0},
        compiler_params=pltpu.CompilerParams(vmem_limit_bytes=GRANT),
        cost_estimate=pl.CostEstimate(flops=low.size, bytes_accessed=10 * low.size, transcendentals=0),
        name="finish",
    )(inc, top, low, back, from_inside)


def forward(axis):
    return [(i, i + 1) for i in range(lax.axis_size(axis) - 1)]


def swaps(axis, start):
    pairs = [(i, i + 1) for i in range(start, lax.axis_size(axis) - 1, 2)]
    return pairs + [(b, a) for a, b in pairs]


def backward(axis):
    return [(i + 1, i) for i in range(lax.axis_size(axis) - 1)]


def pack_row_kernel(u, w, out, sem):
    rows, cols, members, cells = u.shape
    beside = (cols - 1) * even_column().astype(jnp.int32)
    deep = cols * members
    copies = [
        pltpu.make_async_copy(u.at[rows - 1].reshape(deep, cells), out.at[:deep], sem.at[0]),
        pltpu.make_async_copy(w.at[rows - 1, beside], out.at[deep:], sem.at[1]),
    ]
    for copy in copies:
        copy.start()
    for copy in copies:
        copy.wait()


def pack_row(u, w):
    _, cols, members, cells = u.shape
    shape = (cols * members + w.shape[2], cells)
    return pl.pallas_call(
        pack_row_kernel,
        out_shape=pltpu.VMEM(shape, u.dtype),
        in_specs=[HBM, HBM],
        out_specs=VMEM,
        scratch_shapes=[pltpu.SemaphoreType.DMA((2,))],
        cost_estimate=pl.CostEstimate(flops=0, bytes_accessed=4 * shape[0] * cells, transcendentals=0),
        name="pack_row",
    )(u, w)


def pack_rest_kernel(w, outside, out):
    rows, cols, width, _ = w.shape
    skip = 1 - even_column().astype(jnp.int32)
    for q in range(cols - 1):
        out[q * width : (q + 1) * width] = w[rows - 1, q + skip]
    start = (cols - 1) * width
    out[start:] = outside[rows - 1, : out.shape[0] - start]


def pack_rest(w, outside, members):
    _, cols, width, cells = w.shape
    return pl.pallas_call(
        pack_rest_kernel,
        out_shape=jax.ShapeDtypeStruct(((cols - 1) * width + members + width, cells), w.dtype),
        in_specs=[VMEM, VMEM],
        out_specs=VMEM,
        compiler_params=pltpu.CompilerParams(vmem_limit_bytes=GRANT),
        cost_estimate=pl.CostEstimate(flops=0, bytes_accessed=8 * cols * width * cells, transcendentals=0),
        name="pack_rest",
    )(w, outside)


def pack_columns_kernel(u, w, live, index, packed, inner_side, outer_side, sem):
    del packed
    rows, cols, members, cells = u.shape
    deep = members + w.shape[2]
    turn = (cols - 1) * even_column().astype(jnp.int32)
    copies = []
    for n, (out, b) in enumerate(((inner_side, turn), (outer_side, cols - 1 - turn))):
        copies.append(pltpu.make_async_copy(u.at[:, b], out.at[:, :members], sem.at[n, 0]))
        copies.append(pltpu.make_async_copy(w.at[:, b], out.at[:, members:deep], sem.at[n, 1]))
    for copy in copies:
        copy.start()
    for a in range(rows):
        lines = jnp.concatenate([live[a], index[a]], 0).astype(jnp.float32)
        blank = jnp.zeros((2 * cols, cells - live.shape[2]), jnp.float32)
        note = jnp.concatenate([lines, blank], 1).astype(jnp.bfloat16)
        inner_side[a, deep:] = note
        outer_side[a, deep:] = note
    for copy in copies:
        copy.wait()


def pack_columns(u, w, live, index, packed):
    rows, cols, members, cells = u.shape
    shape = (rows, members + w.shape[2] + 2 * cols, cells)
    return pl.pallas_call(
        pack_columns_kernel,
        out_shape=(jax.ShapeDtypeStruct(shape, u.dtype),) * 2,
        in_specs=[ANY, ANY, VMEM, VMEM, VMEM],
        out_specs=(VMEM, VMEM),
        scratch_shapes=[pltpu.SemaphoreType.DMA((2, 2))],
        compiler_params=pltpu.CompilerParams(vmem_limit_bytes=GRANT),
        cost_estimate=pl.CostEstimate(flops=0, bytes_accessed=8 * rows * shape[1] * cells, transcendentals=0),
        name="pack_columns",
    )(u, w, live, index, packed)


def body(u, w, live, index, tapers):
    packed = pack_row(u, w)
    s = lax.ppermute(packed, "row", forward("row"))
    inner_side, outer_side = pack_columns(u, w, live, index, packed)
    outside = lax.ppermute(outer_side, "col", swaps("col", 1))
    inside = lax.ppermute(inner_side, "col", swaps("col", 0))
    inc, turned, flipped = inner(u, w, live, index, tapers)
    inc, outside, inside = lax.optimization_barrier((inc, outside, inside))
    near_side = column(inside, turned, w, live, index, tapers, flipped, False, True)
    near_side, outside = lax.optimization_barrier((near_side, outside))
    rest = lax.ppermute(pack_rest(w, outside, u.shape[2]), "row", forward("row"))
    back, held, to_inside, tail = above(s, turned, w, inside, outside, live, index, flipped)
    back = lax.ppermute(back, "row", backward("row"))
    from_inside = lax.ppermute(to_inside, "col", swaps("col", 0))
    more_side = column(inside, turned, w, live, index, tapers, flipped, False, False)
    far_side = column(outside, turned, w, live, index, tapers, flipped, True, False)
    inc, top, low = outer(inc, near_side, more_side, far_side, held, tail, rest, u, live, index, tapers)
    return finish(inc, top, low, back, from_inside)


def solution(mesh):
    return jax.shard_map(
        body,
        mesh=mesh,
        in_specs=(
            P("row", "col", None, None),
            P("row", "col", None, None),
            P("row", "col", None),
            P("row", "col", None),
            P(),
        ),
        out_specs=P("row", "col", None, None),
        check_vma=False,
    )
```

```python
import functools

import jax
import jax.numpy as jnp
from jax import lax
from jax.experimental import pallas as pl
from jax.experimental.pallas import tpu as pltpu
from jax.sharding import PartitionSpec as P

MEMBERS = 256
GRANT = 16 << 20
SCALE = 1.0 / (MEMBERS - 1)
TN = (((0,), (0,)), ((), ()))
NT = (((1,), (1,)), ((), ()))
NN = (((1,), (0,)), ((), ()))
VMEM = pl.BlockSpec(memory_space=pltpu.VMEM)
ANY = pl.BlockSpec(memory_space=pl.ANY)
HBM = pl.BlockSpec(memory_space=pltpu.HBM)


def dot(a, b, dims):
    return lax.dot_general(a, b, dims, preferred_element_type=jnp.float32)


def cat(parts, axis):
    return parts[0] if len(parts) == 1 else jnp.concatenate(parts, axis=axis)


def tapered(gram, rho, live):
    factor = live.astype(jnp.float32) * SCALE
    return (rho.astype(jnp.float32) * gram * factor).astype(jnp.bfloat16)


def even_column():
    return lax.rem(lax.axis_index("col"), 2) == 0


def sides(inside, outside):
    even = even_column()
    return (
        lambda *at: jnp.where(even, outside[at], inside[at]),
        lambda *at: jnp.where(even, inside[at], outside[at]),
    )


def inner_kernel(u, w, live, index, tapers, out, turned, flipped, sym, held):
    rows, cols, _, cells = u.shape
    for n in range(tapers.shape[0]):
        t = tapers[n].astype(jnp.float32)
        sym[n] = 0.5 * (t + t.T)
        flipped[n] = t.T.astype(jnp.bfloat16)

    def ahead(a, b, last):
        near = [(4, a, b)]
        if b + 1 < cols:
            near.append((5, a, b + 1))
        if not last:
            for k in (6, 7, 8):
                if 0 <= b + k - 7 < cols:
                    near.append((k, a + 1, b + k - 7))
        return near

    for a in range(rows):
        last = a == rows - 1
        on, which = live[a], index[a]
        for b in range(cols):
            near = ahead(a, b, last)
            side_on = u[a, b].T
            turned[a, b] = side_on
            gram = dot(side_on, cat([u[p, q] for _, p, q in near], 1), NN)
            for n, (k, _, _) in enumerate(near):
                at = which[b, k]
                rho = sym[at] if k == 4 else tapers[at]
                held[a % 2, b, :, (k - 4) * cells : (k - 3) * cells] = tapered(
                    gram[:, n * cells : (n + 1) * cells], rho, on[b, k]
                )
        for b in range(cols):
            near = ahead(a, b, last)
            total = dot(
                cat([w[p, q] for _, p, q in near], 1),
                cat([held[a % 2, b, :, (k - 4) * cells : (k - 3) * cells] for k, _, _ in near], 1),
                NT,
            )
            behind = [(5, a, b - 1)] if b > 0 else []
            if a > 0:
                behind += [(k, a - 1, b - (k - 7)) for k in (6, 7, 8) if 0 <= b - (k - 7) < cols]
            if behind:
                total += dot(
                    cat([w[p, q] for _, p, q in behind], 1),
                    cat([held[p % 2, q, :, (k - 4) * cells : (k - 3) * cells] for k, p, q in behind], 0),
                    NN,
                )
            out[a, b] = total


def inner(u, w, live, index, tapers):
    rows, cols, members, cells = u.shape
    columns = w.shape[2]
    pairs = 5 * rows * cols
    return pl.pallas_call(
        inner_kernel,
        out_shape=(
            jax.ShapeDtypeStruct((rows, cols, columns, cells), jnp.float32),
            jax.ShapeDtypeStruct((rows, cols, cells, members), jnp.bfloat16),
            jax.ShapeDtypeStruct(tapers.shape, jnp.bfloat16),
        ),
        in_specs=[VMEM] * 5,
        out_specs=(VMEM,) * 3,
        scratch_shapes=[
            pltpu.VMEM(tapers.shape, jnp.float32),
            pltpu.VMEM((2, cols, cells, 5 * cells), jnp.bfloat16),
        ],
        compiler_params=pltpu.CompilerParams(vmem_limit_bytes=GRANT),
        cost_estimate=pl.CostEstimate(
            flops=2 * pairs * cells * cells * (members + 2 * columns),
            bytes_accessed=4 << 20,
            transcendentals=0,
        ),
        name="inner",
    )(u, w, live, index, tapers)


def above_kernel(s, turned, w, inside, outside, live, index, flipped, back, held, to_inside, tail):
    _, cols, cells, members = turned.shape
    deep = members + w.shape[2]
    last = cols - 1
    left, right = sides(inside, outside)
    on, which = live[0], index[0]

    def upper(c):
        return s[c * members : (c + 1) * members]

    beyond = {}
    for q, near, k, line in ((-1, left, 2, last), (cols, right, 0, 0)):
        note = near(0, slice(deep, None)).astype(jnp.int32)
        gram = dot(near(0, slice(0, members)), upper(min(max(q, 0), last)), TN)
        block = tapered(gram, flipped[note[cols + line, k]], note[line, k])
        beyond[q] = block, near(0, slice(members, deep))
    for q in range(cols):
        near = [c for c in (q - 1, q, q + 1) if 0 <= c < cols]
        gram = dot(turned[0, q], cat([upper(c) for c in near], 1), NN)
        for n, c in enumerate(near):
            k = 1 + c - q
            held[q, :, k * cells : (k + 1) * cells] = tapered(
                gram[:, n * cells : (n + 1) * cells], flipped[which[q, k]], on[q, k]
            )
    for c in range(cols):
        blocks, weights = [], []
        for q in (c - 1, c, c + 1):
            if q in beyond:
                block, weight = beyond[q]
            else:
                k = 1 + c - q
                block, weight = held[q, :, k * cells : (k + 1) * cells], w[0, q]
            blocks.append(block)
            weights.append(weight)
        back[c] = dot(cat(weights, 1), cat(blocks, 0), NN).astype(jnp.bfloat16)
    tail[...] = s[cols * members :]
    to_inside[...] = dot(s[cols * members :], jnp.where(even_column(), beyond[cols][0], beyond[-1][0]), NT)


def above(s, turned, w, inside, outside, live, index, flipped):
    _, cols, cells, members = turned.shape
    columns = w.shape[2]
    return pl.pallas_call(
        above_kernel,
        out_shape=(
            jax.ShapeDtypeStruct((cols, columns, cells), jnp.bfloat16),
            jax.ShapeDtypeStruct((cols, cells, 3 * cells), jnp.bfloat16),
            jax.ShapeDtypeStruct((columns, cells), jnp.float32),
            jax.ShapeDtypeStruct((columns, cells), jnp.bfloat16),
        ),
        in_specs=[VMEM] * 8,
        out_specs=(VMEM,) * 4,
        compiler_params=pltpu.CompilerParams(vmem_limit_bytes=GRANT),
        cost_estimate=pl.CostEstimate(
            flops=2 * 3 * cols * cells * cells * (members + columns),
            bytes_accessed=2 << 20,
            transcendentals=0,
        ),
        name="above",
    )(s, turned, w, inside, outside, live, index, flipped)


def column_part(outward, near, turned, w, live, index, tapers, flipped, side):
    rows, cols, cells, members = turned.shape
    deep = members + w.shape[2]
    last = cols - 1
    on_left = even_column() if outward else jnp.logical_not(even_column())
    b = jnp.where(on_left, 0, last)
    for a in range(rows):
        on, which = live[a], index[a]
        around = [q for q in (a - 1, a, a + 1) if 0 <= q < rows]
        gram = dot(turned[a, b], cat([near[q, :members] for q in around], 1), NN)
        blocks = []
        for n, q in enumerate(around):
            k = 3 * (q - a + 1)
            at = jnp.where(on_left, which[0, k], which[last, k + 2])
            if q < a:
                rho = flipped[at]
            elif q > a:
                rho = tapers[at]
            else:
                rho = jnp.where(on_left, flipped[at], tapers[at])
            lively = jnp.where(on_left, on[0, k], on[last, k + 2])
            blocks.append(tapered(gram[:, n * cells : (n + 1) * cells], rho, lively))
        side[a] = dot(cat([near[q, members:deep] for q in around], 1), cat(blocks, 1), NT)


def column_kernel(outward, alone, near, turned, w, live, index, tapers, flipped, side):
    place = lax.axis_index("col")
    here = jnp.logical_and(place == lax.axis_size("col") - 1, jnp.logical_not(even_column()))
    here = here if alone else jnp.logical_not(here)

    @pl.when(here)
    def _():
        column_part(outward, near, turned, w, live, index, tapers, flipped, side)

    @pl.when(jnp.logical_not(here))
    def _():
        side[...] = jnp.zeros_like(side)


def column(near, turned, w, live, index, tapers, flipped, outward, alone):
    rows, _, cells, members = turned.shape
    width = w.shape[2]
    return pl.pallas_call(
        functools.partial(column_kernel, outward, alone),
        out_shape=jax.ShapeDtypeStruct((rows, width, cells), jnp.float32),
        in_specs=[VMEM] * 7,
        out_specs=VMEM,
        compiler_params=pltpu.CompilerParams(vmem_limit_bytes=GRANT),
        cost_estimate=pl.CostEstimate(
            flops=6 * rows * cells * cells * (members + width), bytes_accessed=2 << 20, transcendentals=0
        ),
        name="column",
    )(near, turned, w, live, index, tapers, flipped)


def outer_kernel(inc, near_side, more_side, far_side, held, tail, rest, u, live, index, tapers, out, top, low):
    rows, cols, members, cells = u.shape
    width = inc.shape[2]
    last = cols - 1
    even = even_column()
    on, which = live[0], index[0]
    start = (cols - 1) * width
    gram = dot(rest[start : start + members], jnp.where(even, u[0, 0], u[0, last]), TN)
    at = jnp.where(even, which[0, 0], which[last, 2])
    block = tapered(gram, tapers[at], jnp.where(even, on[0, 0], on[last, 2]))
    far = dot(rest[start + members :], block, NN)
    blank = jnp.zeros_like(far)

    def side(q, a):
        near, other = near_side[a] + more_side[a], far_side[a]
        return jnp.where(even, other, near) if q == 0 else jnp.where(even, near, other)

    parts = [rest[c * width : (c + 1) * width] for c in range(cols - 1)]
    tail = tail[...]
    weights = [jnp.where(even, parts[0], tail)]
    weights += [jnp.where(even, parts[c], parts[c - 1]) for c in range(1, last)]
    weights.append(jnp.where(even, tail, parts[last - 1]))
    for q in range(cols):
        near = [c for c in (q - 1, q, q + 1) if 0 <= c < cols]
        block = held[q, :, (1 + near[0] - q) * cells : (2 + near[-1] - q) * cells]
        value = inc[0, q] + dot(cat([weights[c] for c in near], 1), block, NT)
        if q in (0, last):
            value += side(q, 0)
            value += jnp.where(even, far, blank) if q == 0 else jnp.where(even, blank, far)
            top[q // last] = value
        out[0, q] = value
    for a in range(1, rows):
        for q in range(cols):
            value = inc[a, q] + side(q, a) if q in (0, last) else inc[a, q]
            out[a, q] = value
            if a == rows - 1:
                low[q] = value


def outer(inc, near_side, more_side, far_side, held, tail, rest, u, live, index, tapers):
    rows, cols, width, cells = inc.shape
    return pl.pallas_call(
        outer_kernel,
        out_shape=(
            jax.ShapeDtypeStruct(inc.shape, inc.dtype),
            jax.ShapeDtypeStruct((2, width, cells), inc.dtype),
            jax.ShapeDtypeStruct(inc.shape[1:], inc.dtype),
        ),
        in_specs=[VMEM] * 11,
        out_specs=(VMEM,) * 3,
        compiler_params=pltpu.CompilerParams(vmem_limit_bytes=GRANT),
        cost_estimate=pl.CostEstimate(flops=6 * cols * cells * cells * width, bytes_accessed=4 << 20, transcendentals=0),
        name="outer",
    )(inc, near_side, more_side, far_side, held, tail, rest, u, live, index, tapers)


def finish_kernel(inc, top, low, back, from_inside, out, end, total, sem):
    del inc
    rows, cols = out.shape[:2]
    half = cols // 2
    side = even_column().astype(jnp.int32)
    copies = []
    for n, part in enumerate((slice(0, half), slice(half, cols))):
        total[part] = low[part] + back[part].astype(jnp.float32)
        copies.append(pltpu.make_async_copy(total.at[part], out.at[rows - 1, part], sem.at[n]))
        copies[-1].start()
    end[...] = top[side] + from_inside[...]
    copies.append(pltpu.make_async_copy(end, out.at[0, side * (cols - 1)], sem.at[2]))
    copies[-1].start()
    for copy in copies:
        copy.wait()


def finish(inc, top, low, back, from_inside):
    return pl.pallas_call(
        finish_kernel,
        out_shape=jax.ShapeDtypeStruct(inc.shape, inc.dtype),
        in_specs=[ANY] + [VMEM] * 4,
        out_specs=ANY,
        scratch_shapes=[
            pltpu.VMEM(top.shape[1:], top.dtype),
            pltpu.VMEM(low.shape, low.dtype),
            pltpu.SemaphoreType.DMA((3,)),
        ],
        input_output_aliases={0: 0},
        compiler_params=pltpu.CompilerParams(vmem_limit_bytes=GRANT),
        cost_estimate=pl.CostEstimate(flops=low.size, bytes_accessed=10 * low.size, transcendentals=0),
        name="finish",
    )(inc, top, low, back, from_inside)


def forward(axis):
    return [(i, i + 1) for i in range(lax.axis_size(axis) - 1)]


def swaps(axis, start):
    pairs = [(i, i + 1) for i in range(start, lax.axis_size(axis) - 1, 2)]
    return pairs + [(b, a) for a, b in pairs]


def backward(axis):
    return [(i + 1, i) for i in range(lax.axis_size(axis) - 1)]


def pack_row_kernel(u, w, out, sem):
    rows, cols, members, cells = u.shape
    beside = (cols - 1) * even_column().astype(jnp.int32)
    deep = cols * members
    copies = [
        pltpu.make_async_copy(u.at[rows - 1].reshape(deep, cells), out.at[:deep], sem.at[0]),
        pltpu.make_async_copy(w.at[rows - 1, beside], out.at[deep:], sem.at[1]),
    ]
    for copy in copies:
        copy.start()
    for copy in copies:
        copy.wait()


def pack_row(u, w):
    _, cols, members, cells = u.shape
    shape = (cols * members + w.shape[2], cells)
    return pl.pallas_call(
        pack_row_kernel,
        out_shape=pltpu.VMEM(shape, u.dtype),
        in_specs=[HBM, HBM],
        out_specs=VMEM,
        scratch_shapes=[pltpu.SemaphoreType.DMA((2,))],
        cost_estimate=pl.CostEstimate(flops=0, bytes_accessed=4 * shape[0] * cells, transcendentals=0),
        name="pack_row",
    )(u, w)


def pack_rest_kernel(w, outside, out):
    rows, cols, width, _ = w.shape
    skip = 1 - even_column().astype(jnp.int32)
    for q in range(cols - 1):
        out[q * width : (q + 1) * width] = w[rows - 1, q + skip]
    start = (cols - 1) * width
    out[start:] = outside[rows - 1, : out.shape[0] - start]


def pack_rest(w, outside, members):
    _, cols, width, cells = w.shape
    return pl.pallas_call(
        pack_rest_kernel,
        out_shape=jax.ShapeDtypeStruct(((cols - 1) * width + members + width, cells), w.dtype),
        in_specs=[VMEM, VMEM],
        out_specs=VMEM,
        compiler_params=pltpu.CompilerParams(vmem_limit_bytes=GRANT),
        cost_estimate=pl.CostEstimate(flops=0, bytes_accessed=8 * cols * width * cells, transcendentals=0),
        name="pack_rest",
    )(w, outside)


def pack_columns_kernel(u, w, live, index, packed, inner_side, outer_side, sem):
    del packed
    rows, cols, members, cells = u.shape
    deep = members + w.shape[2]
    turn = (cols - 1) * even_column().astype(jnp.int32)
    copies = []
    for n, (out, b) in enumerate(((inner_side, turn), (outer_side, cols - 1 - turn))):
        copies.append(pltpu.make_async_copy(u.at[:, b], out.at[:, :members], sem.at[n, 0]))
        copies.append(pltpu.make_async_copy(w.at[:, b], out.at[:, members:deep], sem.at[n, 1]))
    for copy in copies:
        copy.start()
    for a in range(rows):
        lines = jnp.concatenate([live[a], index[a]], 0).astype(jnp.float32)
        blank = jnp.zeros((2 * cols, cells - live.shape[2]), jnp.float32)
        note = jnp.concatenate([lines, blank], 1).astype(jnp.bfloat16)
        inner_side[a, deep:] = note
        outer_side[a, deep:] = note
    for copy in copies:
        copy.wait()


def pack_columns(u, w, live, index, packed):
    rows, cols, members, cells = u.shape
    shape = (rows, members + w.shape[2] + 2 * cols, cells)
    return pl.pallas_call(
        pack_columns_kernel,
        out_shape=(jax.ShapeDtypeStruct(shape, u.dtype),) * 2,
        in_specs=[ANY, ANY, VMEM, VMEM, VMEM],
        out_specs=(VMEM, VMEM),
        scratch_shapes=[pltpu.SemaphoreType.DMA((2, 2))],
        compiler_params=pltpu.CompilerParams(vmem_limit_bytes=GRANT),
        cost_estimate=pl.CostEstimate(flops=0, bytes_accessed=8 * rows * shape[1] * cells, transcendentals=0),
        name="pack_columns",
    )(u, w, live, index, packed)


def body(u, w, live, index, tapers):
    packed = pack_row(u, w)
    s = lax.ppermute(packed, "row", forward("row"))
    inner_side, outer_side = pack_columns(u, w, live, index, packed)
    outside = lax.ppermute(outer_side, "col", swaps("col", 1))
    inside = lax.ppermute(inner_side, "col", swaps("col", 0))
    inc, turned, flipped = inner(u, w, live, index, tapers)
    inc, outside, inside = lax.optimization_barrier((inc, outside, inside))
    near_side = column(inside, turned, w, live, index, tapers, flipped, False, True)
    near_side, outside = lax.optimization_barrier((near_side, outside))
    rest = lax.ppermute(pack_rest(w, outside, u.shape[2]), "row", forward("row"))
    back, held, to_inside, tail = above(s, turned, w, inside, outside, live, index, flipped)
    back = lax.ppermute(back, "row", backward("row"))
    from_inside = lax.ppermute(to_inside, "col", swaps("col", 0))
    more_side = column(inside, turned, w, live, index, tapers, flipped, False, False)
    far_side = column(outside, turned, w, live, index, tapers, flipped, True, False)
    inc, top, low = outer(inc, near_side, more_side, far_side, held, tail, rest, u, live, index, tapers)
    return finish(inc, top, low, back, from_inside)


def solution(mesh):
    return jax.shard_map(
        body,
        mesh=mesh,
        in_specs=(
            P("row", "col", None, None),
            P("row", "col", None, None),
            P("row", "col", None),
            P("row", "col", None),
            P(),
        ),
        out_specs=P("row", "col", None, None),
        check_vma=False,
    )
```

```python
import jax
import jax.numpy as jnp
from jax import lax
from jax.experimental import pallas as pl
from jax.experimental.pallas import tpu as pltpu
from jax.sharding import PartitionSpec as P

MEMBERS = 256
GRANT = 16 << 20
SCALE = 1.0 / (MEMBERS - 1)
TN = (((0,), (0,)), ((), ()))
NT = (((1,), (1,)), ((), ()))
NN = (((1,), (0,)), ((), ()))
VMEM = pl.BlockSpec(memory_space=pltpu.VMEM)
ANY = pl.BlockSpec(memory_space=pl.ANY)
HBM = pl.BlockSpec(memory_space=pltpu.HBM)


def dot(a, b, dims):
    return lax.dot_general(a, b, dims, preferred_element_type=jnp.float32)


def cat(parts, axis):
    return parts[0] if len(parts) == 1 else jnp.concatenate(parts, axis=axis)


def tapered(gram, rho, live):
    factor = live.astype(jnp.float32) * SCALE
    return (rho.astype(jnp.float32) * gram * factor).astype(jnp.bfloat16)


def even_column():
    return lax.rem(lax.axis_index("col"), 2) == 0


def sides(inside, outside):
    even = even_column()
    return (
        lambda *at: jnp.where(even, outside[at], inside[at]),
        lambda *at: jnp.where(even, inside[at], outside[at]),
    )


def inner_kernel(u, w, live, index, tapers, out, turned, flipped, sym, held):
    rows, cols, _, cells = u.shape
    for n in range(tapers.shape[0]):
        t = tapers[n].astype(jnp.float32)
        sym[n] = 0.5 * (t + t.T)
        flipped[n] = t.T.astype(jnp.bfloat16)

    def ahead(a, b, last):
        near = [(4, a, b)]
        if b + 1 < cols:
            near.append((5, a, b + 1))
        if not last:
            for k in (6, 7, 8):
                if 0 <= b + k - 7 < cols:
                    near.append((k, a + 1, b + k - 7))
        return near

    def row(a, last):
        on, which = live[a], index[a]
        for b in range(cols):
            near = ahead(a, b, last)
            side_on = u[a, b].T
            turned[a, b] = side_on
            gram = dot(side_on, cat([u[p, q] for _, p, q in near], 1), NN)
            for n, (k, _, _) in enumerate(near):
                at = which[b, k]
                rho = sym[at] if k == 4 else tapers[at]
                held[b, :, (k - 4) * cells : (k - 3) * cells] = tapered(
                    gram[:, n * cells : (n + 1) * cells], rho, on[b, k]
                )
        for b in range(cols):
            near = ahead(a, b, last)
            total = dot(
                cat([w[p, q] for _, p, q in near], 1),
                cat([held[b, :, (k - 4) * cells : (k - 3) * cells] for k, _, _ in near], 1),
                NT,
            )
            if b > 0:
                total += dot(w[a, b - 1], held[b - 1, :, cells : 2 * cells], NN)
            out[a, b] += total
            if not last:
                back = [(k, b - (k - 7)) for k in (6, 7, 8) if 0 <= b - (k - 7) < cols]
                out[a + 1, b] = dot(
                    cat([w[a, q] for _, q in back], 1),
                    cat([held[q, :, (k - 4) * cells : (k - 3) * cells] for k, q in back], 0),
                    NN,
                )

    out[0] = jnp.zeros_like(out[0])

    @pl.loop(0, rows - 1)
    def _(a):
        row(a, False)

    row(rows - 1, True)


def inner(u, w, live, index, tapers):
    rows, cols, members, cells = u.shape
    columns = w.shape[2]
    pairs = 5 * rows * cols
    return pl.pallas_call(
        inner_kernel,
        out_shape=(
            jax.ShapeDtypeStruct((rows, cols, columns, cells), jnp.float32),
            jax.ShapeDtypeStruct((rows, cols, cells, members), jnp.bfloat16),
            jax.ShapeDtypeStruct(tapers.shape, jnp.bfloat16),
        ),
        in_specs=[VMEM] * 5,
        out_specs=(VMEM,) * 3,
        scratch_shapes=[
            pltpu.VMEM(tapers.shape, jnp.float32),
            pltpu.VMEM((cols, cells, 5 * cells), jnp.bfloat16),
        ],
        compiler_params=pltpu.CompilerParams(vmem_limit_bytes=GRANT),
        cost_estimate=pl.CostEstimate(
            flops=2 * pairs * cells * cells * (members + 2 * columns),
            bytes_accessed=4 << 20,
            transcendentals=0,
        ),
        name="inner",
    )(u, w, live, index, tapers)


def above_kernel(s, turned, w, inside, outside, live, index, flipped, back, held, to_inside, tail):
    _, cols, cells, members = turned.shape
    deep = members + w.shape[2]
    last = cols - 1
    left, right = sides(inside, outside)
    on, which = live[0], index[0]

    def upper(c):
        return s[c * members : (c + 1) * members]

    beyond = {}
    for q, near, k, line in ((-1, left, 2, last), (cols, right, 0, 0)):
        note = near(0, slice(deep, None)).astype(jnp.int32)
        gram = dot(near(0, slice(0, members)), upper(min(max(q, 0), last)), TN)
        block = tapered(gram, flipped[note[cols + line, k]], note[line, k])
        beyond[q] = block, near(0, slice(members, deep))
    for q in range(cols):
        near = [c for c in (q - 1, q, q + 1) if 0 <= c < cols]
        gram = dot(turned[0, q], cat([upper(c) for c in near], 1), NN)
        for n, c in enumerate(near):
            k = 1 + c - q
            held[q, :, k * cells : (k + 1) * cells] = tapered(
                gram[:, n * cells : (n + 1) * cells], flipped[which[q, k]], on[q, k]
            )
    for c in range(cols):
        blocks, weights = [], []
        for q in (c - 1, c, c + 1):
            if q in beyond:
                block, weight = beyond[q]
            else:
                k = 1 + c - q
                block, weight = held[q, :, k * cells : (k + 1) * cells], w[0, q]
            blocks.append(block)
            weights.append(weight)
        back[c] = dot(cat(weights, 1), cat(blocks, 0), NN).astype(jnp.bfloat16)
    tail[...] = s[cols * members :]
    to_inside[...] = dot(s[cols * members :], jnp.where(even_column(), beyond[cols][0], beyond[-1][0]), NT)


def above(s, turned, w, inside, outside, live, index, flipped):
    _, cols, cells, members = turned.shape
    columns = w.shape[2]
    return pl.pallas_call(
        above_kernel,
        out_shape=(
            jax.ShapeDtypeStruct((cols, columns, cells), jnp.bfloat16),
            jax.ShapeDtypeStruct((cols, cells, 3 * cells), jnp.bfloat16),
            jax.ShapeDtypeStruct((columns, cells), jnp.float32),
            jax.ShapeDtypeStruct((columns, cells), jnp.bfloat16),
        ),
        in_specs=[VMEM] * 8,
        out_specs=(VMEM,) * 4,
        compiler_params=pltpu.CompilerParams(vmem_limit_bytes=GRANT),
        cost_estimate=pl.CostEstimate(
            flops=2 * 3 * cols * cells * cells * (members + columns),
            bytes_accessed=2 << 20,
            transcendentals=0,
        ),
        name="above",
    )(s, turned, w, inside, outside, live, index, flipped)


def columns_kernel(u, w, inside, outside, live, index, tapers, side):
    rows, cols, members, cells = u.shape
    deep = members + w.shape[2]
    last = cols - 1
    left, right = sides(inside, outside)
    on = [live[a] for a in range(rows)]
    which = [index[a] for a in range(rows)]
    total = {}

    def add(a, q, value):
        total[a, q] = total[a, q] + value if (a, q) in total else value

    for a in range(rows):
        near = [(5, a)] + ([(8, a + 1)] if a + 1 < rows else [])
        gram = dot(left(a, slice(0, members)), cat([u[p, 0] for _, p in near], 1), TN)
        blocks = cat(
            [
                tapered(gram[:, n * cells : (n + 1) * cells], tapers[which[p][0, 8 - k]], on[p][0, 8 - k])
                for n, (k, p) in enumerate(near)
            ],
            1,
        )
        both = dot(left(a, slice(members, deep)), blocks, NN)
        for n, (_, p) in enumerate(near):
            add(p, 0, both[:, n * cells : (n + 1) * cells])
        gram = dot(u[a, last], cat([right(p, slice(0, members)) for _, p in near], 1), TN)
        blocks = cat(
            [
                tapered(gram[:, n * cells : (n + 1) * cells], tapers[which[a][last, k]], on[a][last, k])
                for n, (k, _) in enumerate(near)
            ],
            1,
        )
        add(a, last, dot(cat([right(p, slice(members, deep)) for _, p in near], 1), blocks, NT))
        if a + 1 < rows:
            gram = dot(u[a, 0], left(a + 1, slice(0, members)), TN)
            block = tapered(gram, tapers[which[a][0, 6]], on[a][0, 6])
            add(a, 0, dot(left(a + 1, slice(members, deep)), block, NT))
            gram = dot(right(a, slice(0, members)), u[a + 1, last], TN)
            block = tapered(gram, tapers[which[a + 1][last, 2]], on[a + 1][last, 2])
            add(a + 1, last, dot(right(a, slice(members, deep)), block, NN))

    for a in range(rows):
        side[0, a] = total[a, 0]
        side[1, a] = total[a, last]


def columns(u, w, inside, outside, live, index, tapers):
    rows, _, members, cells = u.shape
    width = w.shape[2]
    return pl.pallas_call(
        columns_kernel,
        out_shape=jax.ShapeDtypeStruct((2, rows, width, cells), jnp.float32),
        in_specs=[VMEM] * 7,
        out_specs=VMEM,
        compiler_params=pltpu.CompilerParams(vmem_limit_bytes=GRANT),
        cost_estimate=pl.CostEstimate(
            flops=12 * rows * cells * cells * (members + width), bytes_accessed=2 << 20, transcendentals=0
        ),
        name="columns",
    )(u, w, inside, outside, live, index, tapers)


def outer_kernel(inc, side, held, tail, rest, u, live, index, tapers, out, top, low):
    rows, cols, members, cells = u.shape
    width = inc.shape[2]
    last = cols - 1
    even = even_column()
    on, which = live[0], index[0]
    start = (cols - 1) * width
    gram = dot(rest[start : start + members], jnp.where(even, u[0, 0], u[0, last]), TN)
    at = jnp.where(even, which[0, 0], which[last, 2])
    block = tapered(gram, tapers[at], jnp.where(even, on[0, 0], on[last, 2]))
    far = dot(rest[start + members :], block, NN)
    blank = jnp.zeros_like(far)
    parts = [rest[c * width : (c + 1) * width] for c in range(cols - 1)]
    tail = tail[...]
    weights = [jnp.where(even, parts[0], tail)]
    weights += [jnp.where(even, parts[c], parts[c - 1]) for c in range(1, last)]
    weights.append(jnp.where(even, tail, parts[last - 1]))
    for q in range(cols):
        near = [c for c in (q - 1, q, q + 1) if 0 <= c < cols]
        block = held[q, :, (1 + near[0] - q) * cells : (2 + near[-1] - q) * cells]
        value = inc[0, q] + dot(cat([weights[c] for c in near], 1), block, NT)
        if q in (0, last):
            value += side[q // last, 0]
            value += jnp.where(even, far, blank) if q == 0 else jnp.where(even, blank, far)
            top[q // last] = value
        out[0, q] = value
    for a in range(1, rows):
        for q in range(cols):
            value = inc[a, q] + side[q // last, a] if q in (0, last) else inc[a, q]
            out[a, q] = value
            if a == rows - 1:
                low[q] = value


def outer(inc, side, held, tail, rest, u, live, index, tapers):
    rows, cols, width, cells = inc.shape
    return pl.pallas_call(
        outer_kernel,
        out_shape=(
            jax.ShapeDtypeStruct(inc.shape, inc.dtype),
            jax.ShapeDtypeStruct((2, width, cells), inc.dtype),
            jax.ShapeDtypeStruct(inc.shape[1:], inc.dtype),
        ),
        in_specs=[VMEM] * 9,
        out_specs=(VMEM,) * 3,
        compiler_params=pltpu.CompilerParams(vmem_limit_bytes=GRANT),
        cost_estimate=pl.CostEstimate(flops=6 * cols * cells * cells * width, bytes_accessed=4 << 20, transcendentals=0),
        name="outer",
    )(inc, side, held, tail, rest, u, live, index, tapers)


def finish_kernel(inc, top, low, back, from_inside, out, end, total, sem):
    del inc
    rows, cols = out.shape[:2]
    half = cols // 2
    side = even_column().astype(jnp.int32)
    copies = []
    for n, part in enumerate((slice(0, half), slice(half, cols))):
        total[part] = low[part] + back[part].astype(jnp.float32)
        copies.append(pltpu.make_async_copy(total.at[part], out.at[rows - 1, part], sem.at[n]))
        copies[-1].start()
    end[...] = top[side] + from_inside[...]
    copies.append(pltpu.make_async_copy(end, out.at[0, side * (cols - 1)], sem.at[2]))
    copies[-1].start()
    for copy in copies:
        copy.wait()


def finish(inc, top, low, back, from_inside):
    return pl.pallas_call(
        finish_kernel,
        out_shape=jax.ShapeDtypeStruct(inc.shape, inc.dtype),
        in_specs=[ANY] + [VMEM] * 4,
        out_specs=ANY,
        scratch_shapes=[
            pltpu.VMEM(top.shape[1:], top.dtype),
            pltpu.VMEM(low.shape, low.dtype),
            pltpu.SemaphoreType.DMA((3,)),
        ],
        input_output_aliases={0: 0},
        compiler_params=pltpu.CompilerParams(vmem_limit_bytes=GRANT),
        cost_estimate=pl.CostEstimate(flops=low.size, bytes_accessed=10 * low.size, transcendentals=0),
        name="finish",
    )(inc, top, low, back, from_inside)


def forward(axis):
    return [(i, i + 1) for i in range(lax.axis_size(axis) - 1)]


def swaps(axis, start):
    pairs = [(i, i + 1) for i in range(start, lax.axis_size(axis) - 1, 2)]
    return pairs + [(b, a) for a, b in pairs]


def backward(axis):
    return [(i + 1, i) for i in range(lax.axis_size(axis) - 1)]


def pack_row_kernel(u, w, out, sem):
    rows, cols, members, cells = u.shape
    beside = (cols - 1) * even_column().astype(jnp.int32)
    deep = cols * members
    half = cols // 2 * members
    copies = [
        pltpu.make_async_copy(u.at[rows - 1, : cols // 2].reshape(half, cells), out.at[:half], sem.at[0]),
        pltpu.make_async_copy(u.at[rows - 1, cols // 2 :].reshape(deep - half, cells), out.at[half:deep], sem.at[2]),
        pltpu.make_async_copy(w.at[rows - 1, beside], out.at[deep:], sem.at[1]),
    ]
    for copy in copies:
        copy.start()
    for copy in copies:
        copy.wait()


def pack_row(u, w):
    _, cols, members, cells = u.shape
    shape = (cols * members + w.shape[2], cells)
    return pl.pallas_call(
        pack_row_kernel,
        out_shape=pltpu.VMEM(shape, u.dtype),
        in_specs=[HBM, HBM],
        out_specs=VMEM,
        scratch_shapes=[pltpu.SemaphoreType.DMA((3,))],
        cost_estimate=pl.CostEstimate(flops=0, bytes_accessed=4 * shape[0] * cells, transcendentals=0),
        name="pack_row",
    )(u, w)


def pack_rest_kernel(w, outside, out):
    rows, cols, width, _ = w.shape
    skip = 1 - even_column().astype(jnp.int32)
    for q in range(cols - 1):
        out[q * width : (q + 1) * width] = w[rows - 1, q + skip]
    start = (cols - 1) * width
    out[start:] = outside[rows - 1, : out.shape[0] - start]


def pack_rest(w, outside, members):
    _, cols, width, cells = w.shape
    return pl.pallas_call(
        pack_rest_kernel,
        out_shape=jax.ShapeDtypeStruct(((cols - 1) * width + members + width, cells), w.dtype),
        in_specs=[VMEM, VMEM],
        out_specs=VMEM,
        compiler_params=pltpu.CompilerParams(vmem_limit_bytes=GRANT),
        cost_estimate=pl.CostEstimate(flops=0, bytes_accessed=8 * cols * width * cells, transcendentals=0),
        name="pack_rest",
    )(w, outside)


def pack_columns_kernel(u, w, live, index, packed, inner_side, outer_side, sem):
    del packed
    rows, cols, members, cells = u.shape
    deep = members + w.shape[2]
    turn = (cols - 1) * even_column().astype(jnp.int32)
    copies = []
    for n, (out, b) in enumerate(((inner_side, turn), (outer_side, cols - 1 - turn))):
        copies.append(pltpu.make_async_copy(u.at[:, b], out.at[:, :members], sem.at[n, 0]))
        copies.append(pltpu.make_async_copy(w.at[:, b], out.at[:, members:deep], sem.at[n, 1]))
    for copy in copies:
        copy.start()
    for a in range(rows):
        lines = jnp.concatenate([live[a], index[a]], 0).astype(jnp.float32)
        blank = jnp.zeros((2 * cols, cells - live.shape[2]), jnp.float32)
        note = jnp.concatenate([lines, blank], 1).astype(jnp.bfloat16)
        inner_side[a, deep:] = note
        outer_side[a, deep:] = note
    for copy in copies:
        copy.wait()


def pack_columns(u, w, live, index, packed):
    rows, cols, members, cells = u.shape
    shape = (rows, members + w.shape[2] + 2 * cols, cells)
    return pl.pallas_call(
        pack_columns_kernel,
        out_shape=(jax.ShapeDtypeStruct(shape, u.dtype),) * 2,
        in_specs=[ANY, ANY, VMEM, VMEM, VMEM],
        out_specs=(VMEM, VMEM),
        scratch_shapes=[pltpu.SemaphoreType.DMA((2, 2))],
        compiler_params=pltpu.CompilerParams(vmem_limit_bytes=GRANT),
        cost_estimate=pl.CostEstimate(flops=0, bytes_accessed=8 * rows * shape[1] * cells, transcendentals=0),
        name="pack_columns",
    )(u, w, live, index, packed)


def body(u, w, live, index, tapers):
    packed = pack_row(u, w)
    s = lax.ppermute(packed, "row", forward("row"))
    inner_side, outer_side = pack_columns(u, w, live, index, packed)
    outside = lax.ppermute(outer_side, "col", swaps("col", 1))
    inside = lax.ppermute(inner_side, "col", swaps("col", 0))
    inc, turned, flipped = inner(u, w, live, index, tapers)
    inc, outside, inside = lax.optimization_barrier((inc, outside, inside))
    rest = lax.ppermute(pack_rest(w, outside, u.shape[2]), "row", forward("row"))
    back, held, to_inside, tail = above(s, turned, w, inside, outside, live, index, flipped)
    back = lax.ppermute(back, "row", backward("row"))
    from_inside = lax.ppermute(to_inside, "col", swaps("col", 0))
    side = columns(u, w, inside, outside, live, index, tapers)
    inc, top, low = outer(inc, side, held, tail, rest, u, live, index, tapers)
    return finish(inc, top, low, back, from_inside)


def solution(mesh):
    return jax.shard_map(
        body,
        mesh=mesh,
        in_specs=(
            P("row", "col", None, None),
            P("row", "col", None, None),
            P("row", "col", None),
            P("row", "col", None),
            P(),
        ),
        out_specs=P("row", "col", None, None),
        check_vma=False,
    )
```
